32 devices in a mesh: dp: 16 (over z, y, core), seq: 2 (over x).
Axes of the slice: x: 2, y: 2, z: 4, core: 2. Of those that a mesh axis runs over, the one named last changes fastest.
Arguments:
- tokens: bfloat16 [16384, 768], P(('dp', 'seq')), may hold values from -6 to 6
- w_qkv: bfloat16 [768, 2304], replicated, may hold values from -0.21875 to 0.21875
- w_out: bfloat16 [768, 768], replicated, may hold values from -0.875 to 0.875
- w_up: bfloat16 [768, 3072], replicated, may hold values from -0.21875 to 0.21875
- w_down: bfloat16 [3072, 768], replicated, may hold values from -0.109375 to 0.109375
- gains: float32 [2, 768], replicated, may hold values from 0.25 to 1.75
- biases: float32 [6, 768], replicated, may hold values from -2 to 2
- up_bias: float32 [3072], replicated, may hold values from -2 to 2
- image_cut: int32 [16], P('dp'), may hold values from 256 to 768, as said below
- group_live: int32 [16], P('dp'), may hold values from 768 to 1024, as said below
- cotangent: bfloat16 [16384, 768], P(('dp', 'seq')), may hold values from -6 to 6
Outputs:
- block_out: bfloat16 [16384, 768], P(('dp', 'seq'))
- grad_tokens: bfloat16 [16384, 768], P(('dp', 'seq'))
- grad_qkv: float32 [768, 2304], P(('dp', 'seq'))
- grad_wout: float32 [768, 768], P(('dp', 'seq'))
- grad_wup: float32 [768, 3072], P(('dp', 'seq'))
- grad_wdown: float32 [3072, 768], P(('dp', 'seq'))
- grad_gains: float32 [2, 768], P(None, ('dp', 'seq'))
- grad_biases: float32 [6, 768], P(None, ('dp', 'seq'))
- grad_upbias: float32 [3072], P(('dp', 'seq'))
The draws below stay inside these ranges and needn't reach their ends.
Inputs may be any that keep to these rules, and one draw needn't show every extreme that they name: `group_live`: live rows of a group; the first group is full. The second image of a group spans rows image_cut to group_live - 1; each of a group's two images has 256 rows or more.
All inputs are finite; a program needn't handle non-finite values.
Results may differ from the reference program's by a relative error of at most 0.012.
Values may be sent and summed in bfloat16 or wider, within the bound.
No kernel may reach another device: no remote copies, remote signals or barrier semaphores. Data moves between devices by JAX's collectives and lax.ppermute only.
A program may use at most 192 MiB of HBM per device.

```python
import jax
import jax.numpy as jnp
from jax import lax

HEADS = 12
HEAD_DIM = 64
D = 768
FF = 3072
GROUP = 1024
IMAGE_MIN = 256
TOKENS = 16384
N_DP = 16


def live_counts(key):
    dropped = jax.random.randint(jax.random.fold_in(key, 11), (N_DP,), 0, GROUP // 4 + 1)
    places = jnp.arange(N_DP)
    dropped = jnp.where(places == N_DP - 1, GROUP // 4, dropped)
    dropped = jnp.where(places == 0, 0, dropped)
    return GROUP - dropped


def draw_group_live(key, part):
    return live_counts(key).astype(jnp.int32)


def draw_image_cut(key, part):
    live = live_counts(key)
    upper = live - IMAGE_MIN + 1
    cut_row = jax.random.randint(jax.random.fold_in(key, 23), (N_DP,), IMAGE_MIN, upper)
    places = jnp.arange(N_DP)
    cut_row = jnp.where(places == 0, GROUP - IMAGE_MIN, cut_row)
    cut_row = jnp.where(places == 1, IMAGE_MIN, cut_row)
    return cut_row.astype(jnp.int32)


def levels(own_key, dims, split, low, largest):
    level = 1.0
    for dim, blocks in split:
        steps = jax.random.uniform(jax.random.fold_in(jax.random.fold_in(own_key, 6), dim), (blocks,), jnp.float32, low / len(split), largest / len(split))
        level = level * jnp.repeat(jnp.exp(steps), dims[dim] // blocks).reshape((-1,) + (1,) * (len(dims) - 1 - dim))
    return level


def centred(own_key, dims, scale, limit, pieces=(), kind=jnp.bfloat16):
    entries = scale * jax.random.normal(own_key, dims, jnp.float32)
    if pieces:
        entries = entries * levels(own_key, dims, pieces, -0.22, 0.18)
    return jnp.clip(entries, -limit, limit).astype(kind)


def setup_inputs(seed: int = 0) -> dict:
    arg_keys = jax.random.split(jax.random.key(seed), 12)
    return {
        "tokens": centred(arg_keys[0], (TOKENS, D), 1.0, 6.0, ((0, 32),)),
        "w_qkv": centred(arg_keys[1], (D, 3 * D), D ** -0.5, 0.21875),
        "w_out": centred(arg_keys[2], (D, D), (D // 16) ** -0.5, 0.875),
        "w_up": centred(arg_keys[3], (D, FF), D ** -0.5, 0.21875),
        "w_down": centred(arg_keys[4], (FF, D), FF ** -0.5, 0.109375),
        "gains": jnp.clip(1.0 + 0.15 * jax.random.normal(arg_keys[5], (2, D), jnp.float32), 0.25, 1.75),
        "biases": centred(arg_keys[6], (6, D), 0.3, 2.0, (), jnp.float32),
        "up_bias": centred(arg_keys[7], (FF,), 0.3, 2.0, (), jnp.float32),
        "image_cut": draw_image_cut(jax.random.fold_in(arg_keys[11], 71), 0),
        "group_live": draw_group_live(jax.random.fold_in(arg_keys[11], 71), 0),
        "cotangent": centred(arg_keys[10], (TOKENS, D), 1.0, 6.0, ((0, 32),)),
    }


EPSILON = 1e-06
HIGHEST = lax.Precision.HIGHEST

@jax.custom_vjp
def low(v):
    return lax.optimization_barrier(v.astype(jnp.bfloat16)).astype(jnp.float32)

@jax.custom_vjp
def low_back(v):
    return v

def low_keep(v):
    return (low(v), None)

def low_pass(kept, grad):
    return (grad,)

def back_keep(v):
    return (v, None)

def back_low(kept, grad):
    return (low(grad),)
low.defvjp(low_keep, low_pass)
low_back.defvjp(back_keep, back_low)

def norm_rows(values, gain, shift):
    center = values - lax.optimization_barrier(jnp.mean(values, axis=-1, keepdims=True))
    spread = lax.optimization_barrier(jnp.mean(center * center, axis=-1, keepdims=True))
    return center * lax.rsqrt(spread + EPSILON) * gain + shift

def head_attention(query_head, key_head, value_head, mask):
    raw = low_back(jnp.dot(query_head, key_head.T, precision=HIGHEST))
    probs = jax.nn.softmax(raw * 0.125 + mask, axis=-1)
    return jnp.dot(low(probs), value_head, precision=HIGHEST)

def split_heads(values):
    return values.reshape(values.shape[0], HEADS, HEAD_DIM).transpose(1, 0, 2)

def group_forward(block, cut_row, live_rows, w_qkv, w_out, w_up, w_down, gains, biases, up_bias):
    positions = jnp.arange(GROUP, dtype=jnp.int32)
    second = positions >= cut_row
    alive = positions < live_rows
    allowed = (second[:, None] == second[None, :]) & alive[None, :]
    mask = jnp.where(allowed, 0.0, -1000000000.0).astype(jnp.float32)
    normed_one = low(norm_rows(block, gains[0], biases[0]))
    projected = jnp.dot(normed_one, w_qkv, precision=HIGHEST)
    queries = low_back(low(projected[:, :D] + biases[2]))
    keys_all = low_back(low(projected[:, D:2 * D]))
    values_all = low_back(low(projected[:, 2 * D:] + biases[3]))
    attend = jax.checkpoint(lambda operands: head_attention(operands[0], operands[1], operands[2], mask))
    heads_out = lax.map(attend, (split_heads(queries), split_heads(keys_all), split_heads(values_all)))
    attended = heads_out.transpose(1, 0, 2).reshape(GROUP, D)
    attended = low_back(low(attended))
    branch = low_back(jnp.dot(attended, w_out, precision=HIGHEST) + biases[4])
    residual = block + branch
    normed_two = low(norm_rows(residual, gains[1], biases[1]))
    hidden_pre = low_back(jnp.dot(normed_two, w_up, precision=HIGHEST) + up_bias)
    activated = low(jax.nn.gelu(hidden_pre, approximate=False))
    mlp_out = low_back(jnp.dot(activated, w_down, precision=HIGHEST) + biases[5])
    return jnp.where(alive[:, None], residual + mlp_out, 0.0)

def make_forward(image_cut, group_live):

    def forward(tokens, w_qkv, w_out, w_up, w_down, gains, biases, up_bias):
        one = jax.checkpoint(group_forward)

        def step(carry, operands):
            block, cut_row, live_rows = operands
            return (carry, one(block, cut_row, live_rows, w_qkv, w_out, w_up, w_down, gains, biases, up_bias))
        blocks = tokens.reshape(N_DP, GROUP, D)
        _, outputs = lax.scan(step, jnp.float32(0.0), (blocks, image_cut, group_live))
        return outputs.reshape(N_DP * GROUP, D)
    return forward

def reference(tokens, w_qkv, w_out, w_up, w_down, gains, biases, up_bias, image_cut, group_live, cotangent):
    primals = (tokens.astype(jnp.float32), w_qkv.astype(jnp.float32), w_out.astype(jnp.float32), w_up.astype(jnp.float32), w_down.astype(jnp.float32), gains.astype(jnp.float32), biases.astype(jnp.float32), up_bias.astype(jnp.float32))
    output, back = jax.vjp(make_forward(image_cut, group_live), *primals)
    grads = back(cotangent.astype(jnp.float32))
    return (output.astype(jnp.bfloat16), grads[0].astype(jnp.bfloat16), grads[1], grads[2], grads[3], grads[4], grads[5], grads[6], grads[7])
```

```python
from functools import partial

import jax
import jax.numpy as jnp
from jax import lax
from jax.experimental import pallas as pl
from jax.experimental.pallas import tpu as pltpu
from jax.sharding import PartitionSpec as P

HEADS = 12
HEAD_DIM = 64
PAIR = 2 * HEAD_DIM
EPSILON = 1e-06
BOTH = ("dp", "seq")
FAR = -1000000000.0
F32 = jnp.float32
BF16 = jnp.bfloat16

ME, HALF, CUT, LIVE = 0, 1, 2, 3

NN = (((1,), (0,)), ((), ()))
NT = (((1,), (1,)), ((), ()))
TN = (((0,), (0,)), ((), ()))


def mm(a, b, dims=NN):
    return lax.dot_general(a, b, dims, preferred_element_type=F32)


def params(**more):
    return pltpu.CompilerParams(vmem_limit_bytes=56 * 1024 * 1024, **more)


def norm_parts(values):
    center = values - jnp.mean(values, axis=-1, keepdims=True)
    spread = jnp.mean(center * center, axis=-1, keepdims=True)
    rstd = lax.rsqrt(spread + EPSILON)
    return center * rstd, rstd


def norm_back(grad, unit, rstd, gain):
    scaled = grad * gain
    first = jnp.mean(scaled, axis=-1, keepdims=True)
    second = jnp.mean(scaled * unit, axis=-1, keepdims=True)
    return rstd * (scaled - first - unit * second)


def hop(value, mask, count):
    return lax.ppermute(value, BOTH, [(i, i ^ mask) for i in range(count)])


def add_up(a, b):
    return a.astype(F32) + b.astype(F32)


def reduce_streams(streams, count):
    state = [(keep, send) for keep, send, _ in streams]
    depth = len(streams[0][2])
    for step in range(depth):
        got = [hop(send, masks[step], count) for (_, send), (_, _, masks) in zip(state, streams)]
        following = []
        for (keep, _), arrived in zip(state, got):
            if step + 1 < depth:
                send = add_up(keep[1], arrived[1]).astype(BF16)
                keep = add_up(keep[0], arrived[0]).astype(BF16)
                following.append((keep, send))
            else:
                following.append((add_up(keep, arrived), None))
        state = following
    return [keep for keep, _ in state]


def places(masks):
    out = [((), 0)]
    for mask in masks:
        out = [(at + (bit,), value ^ (mask * bit)) for at, value in out for bit in (0, 1)]
    return out


def qkv_kernel(meta, mine, other, wq, wk, wv, gains, biases, n1_ref, q_ref, k_ref, v_ref):
    step = pl.program_id(0)

    def run(ref):
        unit, _ = norm_parts(ref[...].astype(F32))
        normed = (unit * gains[0:1, :] + biases[0:1, :]).astype(BF16)
        n1_ref[...] = normed
        half = q_ref.shape[1]
        first = pl.multiple_of(meta[HALF] * half, half)
        q_ref[...] = (mm(normed, wq[...]) + biases_at(biases, 2, first, half)).astype(BF16)
        k_ref[...] = mm(normed, wk[...]).astype(BF16)
        v_ref[...] = (mm(normed, wv[...]) + biases_at(biases, 3, first, half)).astype(BF16)

    @pl.when(step == 0)
    def _():
        run(mine)

    @pl.when(step == 1)
    def _():
        run(other)


def biases_at(biases, row, first, size):
    return biases[row : row + 1, pl.ds(first, size)]


def qkv_call(meta, mine, other, w_qkv, gains, biases):
    rows, width = mine.shape
    half = width // 2
    full = lambda shape: pl.BlockSpec(shape, lambda i, m: (0, 0))
    weight = lambda part: pl.BlockSpec((width, half), lambda i, m: (0, 2 * part + m[HALF]))
    out = lambda cols: pl.BlockSpec((rows, cols), lambda i, m: (i ^ m[HALF], 0))
    shape = lambda cols: jax.ShapeDtypeStruct((2 * rows, cols), BF16)
    return pl.pallas_call(
        qkv_kernel,
        grid_spec=pltpu.PrefetchScalarGridSpec(
            num_scalar_prefetch=1,
            grid=(2,),
            in_specs=[
                full((rows, width)), full((rows, width)), weight(0), weight(1), weight(2),
                full(gains.shape), full(biases.shape),
            ],
            out_specs=[out(width), out(half), out(half), out(half)],
        ),
        out_shape=[shape(width), shape(half), shape(half), shape(half)],
        compiler_params=params(),
        name="qkv",
    )(meta, mine, other, w_qkv, w_qkv, w_qkv, gains, biases)


TILE = 256


def lanes(rows):
    return lax.broadcasted_iota(jnp.int32, (rows, PAIR), 1)


def own_lanes(rows, head):
    return (lanes(rows) // HEAD_DIM) == head


def key_side(key_pair, head, meta):
    rows = key_pair.shape[0]
    at = lanes(rows) - (1 - head) * HEAD_DIM
    pos = lax.broadcasted_iota(jnp.int32, (rows, PAIR), 0)
    alive = pos < meta[LIVE]
    second = pos >= meta[CUT]
    in_first = alive & jnp.logical_not(second)
    in_second = alive & second
    extra = jnp.where(
        ((at == 0) & jnp.logical_not(in_first)) | ((at == 1) & jnp.logical_not(in_second)), FAR, 0.0
    )
    return jnp.where(own_lanes(rows, head), key_pair.astype(F32), extra).astype(BF16)


def query_side(query_pair, head, first_row, meta):
    rows = query_pair.shape[0]
    at = lanes(rows) - (1 - head) * HEAD_DIM
    second = first_row + lax.broadcasted_iota(jnp.int32, (rows, PAIR), 0) >= meta[CUT]
    extra = jnp.where(
        ((at == 0) & jnp.logical_not(second)) | ((at == 1) & second), 1.0, 0.0
    )
    return jnp.where(own_lanes(rows, head), query_pair.astype(F32) * 0.125, extra).astype(BF16)


def key_range(first_row, group, meta):
    cut = meta[CUT]
    live = meta[LIVE]
    only_first = first_row + TILE <= cut
    only_second = first_row >= cut
    low = jnp.where(only_second, cut, 0)
    high = jnp.where(only_first, cut, live)
    low = (low // 128) * 128
    steps = (high - low + (TILE - 1)) // TILE
    start = jnp.minimum(low, group - steps * TILE)
    return pl.multiple_of(start, 128), steps


def by_width(steps, group, body):
    for count in range(1, group // TILE + 1):

        @pl.when(steps == count)
        def _(count=count):
            body(count * TILE)


def attend_kernel(meta, which, q_ref, k_ref, v_ref, o_ref, lse_ref, kx_ref, vt_ref):
    rows = q_ref.shape[0]
    group = k_ref.shape[0]
    base = which[0] * rows
    for head in (0, 1):
        kx_ref[head] = key_side(k_ref[...], head, meta)
    vt_ref[...] = v_ref[...].T

    def tile(index, carry):
        at = pl.multiple_of(index * TILE, TILE)
        first_row = base + at
        start, steps = key_range(first_row, group, meta)
        query = q_ref[pl.ds(at, TILE), :]

        def body(width):
            parts = []
            for head in (0, 1):
                qx = query_side(query, head, first_row, meta)
                scores = mm(kx_ref[head, pl.ds(start, width), :], qx, NT)
                top = jnp.max(scores, axis=0, keepdims=True)
                weight = jnp.exp(scores - top).astype(BF16)
                value = vt_ref[head * HEAD_DIM : (head + 1) * HEAD_DIM, pl.ds(start, width)]
                left = jnp.concatenate([value, jnp.ones((16, width), BF16)], axis=0)
                both = mm(left, weight)
                total = both[HEAD_DIM : HEAD_DIM + 1, :]
                parts.append(both[:HEAD_DIM, :] / total)
                lse_ref[0, head : head + 1, pl.ds(at, TILE)] = top + jnp.log(total)
            o_ref[pl.ds(at, TILE), :] = jnp.concatenate(parts, axis=0).T.astype(BF16)

        by_width(steps, group, body)
        return carry

    lax.fori_loop(0, rows // TILE, tile, 0)


def attend_call(meta, which, q, k, v):
    group, half = q.shape
    rows = group // 2
    pairs = half // PAIR
    return pl.pallas_call(
        attend_kernel,
        grid_spec=pltpu.PrefetchScalarGridSpec(
            num_scalar_prefetch=2,
            grid=(pairs,),
            in_specs=[
                pl.BlockSpec((rows, PAIR), lambda p, m, w: (w[0], p)),
                pl.BlockSpec((group, PAIR), lambda p, m, w: (0, p)),
                pl.BlockSpec((group, PAIR), lambda p, m, w: (0, p)),
            ],
            out_specs=[
                pl.BlockSpec((rows, PAIR), lambda p, m, w: (0, p)),
                pl.BlockSpec((1, 2, rows), lambda p, m, w: (p, 0, 0)),
            ],
            scratch_shapes=[pltpu.VMEM((2, group, PAIR), BF16), pltpu.VMEM((PAIR, group), BF16)],
        ),
        out_shape=[
            jax.ShapeDtypeStruct((rows, half), BF16),
            jax.ShapeDtypeStruct((pairs, 2, rows), F32),
        ],
        compiler_params=params(),
        name="attend",
    )(meta, which, q, k, v)


def attend_back_kernel(
    meta, q_ref, k_ref, v_ref, do_mine, do_other, o_mine, o_other, lse_mine, lse_other,
    dq_ref, dk_ref, dv_ref, kx_ref, kt_ref, dk_acc, dv_acc,
):
    group = k_ref.shape[0]
    rows = do_mine.shape[0]
    for head in (0, 1):
        kx_ref[head] = key_side(k_ref[...], head, meta)
    kt_ref[...] = k_ref[...].T
    dk_acc[...] = jnp.zeros_like(dk_acc)
    dv_acc[...] = jnp.zeros_like(dv_acc)
    for place, do_ref, o_ref, lse_ref in (
        (0, do_mine, o_mine, lse_mine), (1, do_other, o_other, lse_other),
    ):
        base = (meta[HALF] ^ place) * rows

        def tile(index, carry, do_ref=do_ref, o_ref=o_ref, lse_ref=lse_ref, base=base):
            at = pl.multiple_of(index * TILE, TILE)
            first_row = pl.multiple_of(base + at, TILE)
            start, steps = key_range(first_row, group, meta)
            query = q_ref[pl.ds(first_row, TILE), :]
            grad = do_ref[pl.ds(at, TILE), :]
            dots = (grad.astype(F32) * o_ref[pl.ds(at, TILE), :].astype(F32)).T

            def body(width):
                probs, raws, masked_grads, masked_queries, dqs = [], [], [], [], []
                for head in (0, 1):
                    mine = own_lanes(TILE, head)
                    qx = query_side(query, head, first_row, meta)
                    dox = jnp.where(mine, grad, jnp.zeros_like(grad))
                    scores = mm(kx_ref[head, pl.ds(start, width), :], qx, NT)
                    prob = jnp.exp(scores - lse_ref[0, head : head + 1, pl.ds(at, TILE)])
                    gprob = mm(v_ref[pl.ds(start, width), :], dox, NT)
                    delta = jnp.sum(dots[head * HEAD_DIM : (head + 1) * HEAD_DIM, :], axis=0, keepdims=True)
                    raw = (prob * (gprob - delta)).astype(BF16)
                    keys_t = kt_ref[head * HEAD_DIM : (head + 1) * HEAD_DIM, pl.ds(start, width)]
                    dqs.append(mm(keys_t, raw))
                    probs.append(prob.astype(BF16))
                    raws.append(raw)
                    masked_grads.append(dox)
                    masked_queries.append(jnp.where(mine, query * jnp.asarray(0.125, BF16), jnp.zeros_like(query)))
                dv_acc[pl.ds(start, width), :] += mm(
                    jnp.concatenate(probs, axis=1), jnp.concatenate(masked_grads, axis=0)
                )
                dk_acc[pl.ds(start, width), :] += mm(
                    jnp.concatenate(raws, axis=1), jnp.concatenate(masked_queries, axis=0)
                )
                dq = jnp.concatenate(dqs, axis=0).T * 0.125
                dq_ref[pl.ds(first_row, TILE), :] = dq.astype(BF16)

            by_width(steps, group, body)
            return carry

        lax.fori_loop(0, rows // TILE, tile, 0)
    dk_ref[...] = dk_acc[...].astype(BF16)
    dv_ref[...] = dv_acc[...].astype(BF16)


def attend_back_call(meta, q, k, v, do_mine, do_other, o_mine, o_other, lse_mine, lse_other, first, count):
    group, half = q.shape
    rows = group // 2
    whole = pl.BlockSpec((group, PAIR), lambda p, m: (0, p + first))
    part = pl.BlockSpec((rows, PAIR), lambda p, m: (0, p + first))
    lse = pl.BlockSpec((1, 2, rows), lambda p, m: (p + first, 0, 0))
    out = pl.BlockSpec((group, PAIR), lambda p, m: (0, p))
    return pl.pallas_call(
        attend_back_kernel,
        grid_spec=pltpu.PrefetchScalarGridSpec(
            num_scalar_prefetch=1,
            grid=(count,),
            in_specs=[whole, whole, whole, part, part, part, part, lse, lse],
            out_specs=[out, out, out],
            scratch_shapes=[
                pltpu.VMEM((2, group, PAIR), BF16),
                pltpu.VMEM((PAIR, group), BF16),
                pltpu.VMEM((group, PAIR), F32),
                pltpu.VMEM((group, PAIR), F32),
            ],
        ),
        out_shape=[jax.ShapeDtypeStruct((group, count * PAIR), BF16)] * 3,
        compiler_params=params(),
        name="attend_back",
    )(meta, q, k, v, do_mine, do_other, o_mine, o_other, lse_mine, lse_other)


CORE, SIDE_X, SIDE_Y, Z_NEAR, Z_FAR = 2, 1, 4, 8, 24
ORDER_ZXY = (CORE, Z_NEAR, Z_FAR, SIDE_X, SIDE_Y)
ORDER_XYZ = (CORE, SIDE_X, SIDE_Y, Z_NEAR, Z_FAR)
ORDER_YXZ = (CORE, SIDE_Y, SIDE_X, Z_NEAR, Z_FAR)
ORDERS = (ORDER_ZXY, ORDER_XYZ, ORDER_YXZ)
COUNT = 32
UP_STEPS = ((0, 2), (2, 5), (5, 8))
DOWN_ROWS = ((0, 24), (24, 64), (64, 96))
OUT_COLS = ((0, 128), (128, 512), (512, 768))

ERF_TOP = (0.00022905065861350646, 0.0034082910107109506, 0.050955695062380861, 0.18520832239976145, 1.128379143519084)
ERF_LOW = (
    -1.1791602954361697e-7, 0.000023547966471313185, 0.0010179625278914885, 0.014070470171167667,
    0.11098505178285362, 0.49746925110067538, 1.0,
)


def erf(x):
    x = jnp.clip(x, -3.832506856900711, 3.832506856900711)
    square = x * x
    top = jnp.full_like(x, ERF_TOP[0])
    for c in ERF_TOP[1:]:
        top = top * square + c
    low = jnp.full_like(x, ERF_LOW[0])
    for c in ERF_LOW[1:]:
        low = low * square + c
    return x * top / low


def put_parts(source, me, masks, keep, send, rows, here=lambda at: at):
    for bit, ref in ((0, keep), (1, send)):
        for at, value in places(masks[1:]):
            target = me ^ (value ^ (masks[0] * bit))
            first = pl.multiple_of(target * rows, 8)
            ref[here(at)] = source[pl.ds(first, rows), :].astype(BF16)


def mid_kernel(
    meta, tok, cot, a_own, a_got, w_out, w_up, w_down, gains, biases, up_bias,
    block_ref, gres_ref, gb_ref, ga_own, ga_send, small_ref, gub_ref,
    up0k, up0s, up1k, up1s, up2k, up2s, dn0k, dn0s, dn1k, dn1s, dn2k, dn2s,
    res_ref, n2_ref, n2t_ref, gl_ref, out_acc, dn_acc, up_blk, down_blk,
):
    step = pl.program_id(0)
    rows, width = tok.shape
    half = a_own.shape[1]
    me = meta[ME]
    own = pl.multiple_of(meta[HALF] * half, half)
    far = pl.multiple_of((1 - meta[HALF]) * half, half)
    live = meta[HALF] * rows + lax.broadcasted_iota(jnp.int32, (rows, 1), 0) < meta[LIVE]

    @pl.when(step == 0)
    def _():
        residual = (
            tok[...].astype(F32)
            + mm(a_own[...], w_out[pl.ds(own, half), :])
            + mm(a_got[...], w_out[pl.ds(far, half), :])
            + biases[4:5, :]
        )
        res_ref[...] = residual
        unit, _ = norm_parts(residual)
        n2 = (unit * gains[1:2, :] + biases[1:2, :]).astype(BF16)
        n2_ref[...] = n2
        n2t_ref[...] = n2.T
        gl_ref[...] = jnp.where(live, cot[...], jnp.zeros_like(cot))
        out_acc[...] = jnp.zeros_like(out_acc)
        dn_acc[...] = jnp.zeros_like(dn_acc)

    hidden = mm(n2_ref[...], w_up[...]) + up_bias[...]
    gact = mm(gl_ref[...], w_down[...], NT)
    cdf = 0.5 * (1.0 + erf(hidden * 0.7071067811865476))
    pdf = jnp.exp(-0.5 * hidden * hidden) * 0.3989422804014327
    act = (hidden * cdf).astype(BF16)
    grad_hidden = gact * (cdf + hidden * pdf)
    gub_ref[...] = jnp.sum(grad_hidden, axis=0, keepdims=True)
    grad_hidden = grad_hidden.astype(BF16)
    out_acc[...] += mm(act, w_down[...])
    dn_acc[...] += mm(grad_hidden, w_up[...], NT)
    down_blk[...] = mm(act, gl_ref[...], TN)
    up_blk[...] = mm(n2t_ref[...], grad_hidden)

    part = down_blk.shape[0] // 4
    for (low, high), masks, keep, send in zip(DOWN_ROWS, ORDERS, (dn0k, dn1k, dn2k), (dn0s, dn1s, dn2s)):
        dim = masks.index(SIDE_X) - 1
        for bit, ref in ((0, keep), (1, send)):
            for x_bit in (0, 1):
                target = (me & 3) ^ (bit * CORE + x_bit * SIDE_X)
                at = tuple(x_bit if i == dim else 0 for i in range(4))
                first = pl.multiple_of(target * part + low, 8)
                ref[at] = down_blk[pl.ds(first, high - low), :].astype(BF16)

    for (low, high), masks, keep, send in zip(UP_STEPS, ORDERS, (up0k, up1k, up2k), (up0s, up1s, up2s)):

        @pl.when((step >= low) & (step < high))
        def _(masks=masks, keep=keep, send=send):
            put_parts(up_blk, me, masks, keep, send, width // COUNT)

    @pl.when(step == pl.num_programs(0) - 1)
    def _():
        residual = res_ref[...]
        block_ref[...] = jnp.where(live, residual + out_acc[...] + biases[5:6, :], 0.0).astype(BF16)
        unit, rstd = norm_parts(residual)
        grad = dn_acc[...]
        gl = gl_ref[...].astype(F32)
        gres = gl + norm_back(grad, unit, rstd, gains[1:2, :])
        gb = gres.astype(BF16)
        gres_ref[...] = gres
        gb_ref[...] = gb
        ga_send[...] = mm(gb, w_out[pl.ds(far, half), :], NT).astype(BF16)
        ga_own[...] = mm(gb, w_out[pl.ds(own, half), :], NT).astype(BF16)
        small_ref[0:1, :] = jnp.sum(grad * unit, axis=0, keepdims=True)
        small_ref[1:2, :] = jnp.sum(grad, axis=0, keepdims=True)
        small_ref[2:3, :] = jnp.sum(gb.astype(F32), axis=0, keepdims=True)
        small_ref[3:4, :] = jnp.sum(gl, axis=0, keepdims=True)
        small_ref[4:8, :] = jnp.zeros((4, width), F32)


def mid_call(meta, tok, cot, a_own, a_got, w_out, w_up, w_down, gains, biases, up_bias):
    rows, width = tok.shape
    ff = w_up.shape[1]
    steps = COUNT // 4
    chunk = ff // steps
    part = width // COUNT

    def full(shape):
        return pl.BlockSpec(shape, lambda i, m: (0,) * len(shape))

    def up_spec(low, high):
        return pl.BlockSpec(
            (2, 2, 2, 2, part, chunk),
            lambda i, m: (0, 0, 0, 0, 0, jnp.clip(i - low, 0, high - low - 1)),
        )

    def down_spec(masks, size):
        def at(i, m):
            column = i ^ (m[ME] // 4)
            z = column // 2
            bits = {SIDE_Y: column % 2, Z_FAR: z // 2, Z_NEAR: (z % 2) ^ (z // 2), SIDE_X: 0}
            return tuple(bits[mask] for mask in masks[1:]) + (0, 0)

        return pl.BlockSpec(tuple(2 if mask == SIDE_X else 1 for mask in masks[1:]) + (size, width), at)

    out_specs = [
        full((rows, width)), full((rows, width)), full((rows, width)),
        full((rows, width // 2)), full((rows, width // 2)), full((8, width)),
        pl.BlockSpec((1, chunk), lambda i, m: (0, i)),
    ]
    out_shape = [
        jax.ShapeDtypeStruct((rows, width), BF16), jax.ShapeDtypeStruct((rows, width), F32),
        jax.ShapeDtypeStruct((rows, width), BF16), jax.ShapeDtypeStruct((rows, width // 2), BF16),
        jax.ShapeDtypeStruct((rows, width // 2), BF16), jax.ShapeDtypeStruct((8, width), F32),
        jax.ShapeDtypeStruct((1, ff), F32),
    ]
    for low, high in UP_STEPS:
        out_specs += [up_spec(low, high)] * 2
        out_shape += [jax.ShapeDtypeStruct((2, 2, 2, 2, part, (high - low) * chunk), BF16)] * 2
    for (low, high), masks in zip(DOWN_ROWS, ORDERS):
        out_specs += [down_spec(masks, high - low)] * 2
        out_shape += [jax.ShapeDtypeStruct((2, 2, 2, 2, high - low, width), BF16)] * 2
    out = pl.pallas_call(
        mid_kernel,
        grid_spec=pltpu.PrefetchScalarGridSpec(
            num_scalar_prefetch=1,
            grid=(steps,),
            in_specs=[
                full((rows, width)), full((rows, width)), full((rows, width // 2)), full((rows, width // 2)),
                full(w_out.shape),
                pl.BlockSpec((width, chunk), lambda i, m: (0, i)),
                pl.BlockSpec((chunk, width), lambda i, m: (i, 0)),
                full(gains.shape), full(biases.shape),
                pl.BlockSpec((1, chunk), lambda i, m: (0, i)),
            ],
            out_specs=out_specs,
            scratch_shapes=[
                pltpu.VMEM((rows, width), F32), pltpu.VMEM((rows, width), BF16), pltpu.VMEM((width, rows), BF16),
                pltpu.VMEM((rows, width), BF16), pltpu.VMEM((rows, width), F32), pltpu.VMEM((rows, width), F32),
                pltpu.VMEM((width, chunk), F32), pltpu.VMEM((chunk, width), F32),
            ],
        ),
        out_shape=out_shape,
        compiler_params=params(),
        name="mid",
    )(meta, tok, cot, a_own, a_got, w_out, w_up, w_down, gains, biases, up_bias.reshape(1, ff))
    up = [(out[7 + 2 * i], out[8 + 2 * i], ORDERS[i]) for i in range(3)]
    down = [(out[13 + 2 * i], out[14 + 2 * i], ORDERS[i]) for i in range(3)]
    return out[:7], up, down


def wout_kernel(meta, a_own, a_got, gb, k0, s0, k1, s1, k2, s2, whole):
    half = a_own.shape[1]
    own = pl.multiple_of(meta[HALF] * half, half)
    far = pl.multiple_of((1 - meta[HALF]) * half, half)
    whole[pl.ds(own, half), :] = mm(a_own[...], gb[...], TN)
    whole[pl.ds(far, half), :] = mm(a_got[...], gb[...], TN)
    part = whole.shape[0] // COUNT
    for (low, high), masks, keep, send in zip(OUT_COLS, ORDERS, (k0, k1, k2), (s0, s1, s2)):
        put_parts(whole.at[:, low:high], meta[ME], masks, keep, send, part)


def wout_call(meta, a_own, a_got, gb):
    rows, width = gb.shape
    out_shape = []
    for low, high in OUT_COLS:
        out_shape += [jax.ShapeDtypeStruct((2, 2, 2, 2, width // COUNT, high - low), BF16)] * 2
    out = pl.pallas_call(
        wout_kernel,
        grid_spec=pltpu.PrefetchScalarGridSpec(
            num_scalar_prefetch=1,
            grid=(1,),
            in_specs=[pl.BlockSpec(a.shape, lambda i, m: (0, 0)) for a in (a_own, a_got, gb)],
            out_specs=[pl.BlockSpec(s.shape, lambda i, m: (0,) * 6) for s in out_shape],
            scratch_shapes=[pltpu.VMEM((width, width), F32)],
        ),
        out_shape=out_shape,
        compiler_params=params(),
        name="wout",
    )(meta, a_own, a_got, gb)
    return [(out[2 * i], out[2 * i + 1], ORDERS[i]) for i in range(3)]


QKV_ORDERS = (
    (SIDE_X, SIDE_Y, Z_NEAR, Z_FAR, CORE), (SIDE_Y, SIDE_X, Z_NEAR, Z_FAR, CORE), (Z_NEAR, Z_FAR, SIDE_Y, SIDE_X, CORE),
)
SMALL = 128


def qkv_back_kernel(
    meta, n1, dq, dk, dv, wq, wk, wv, tok_mine, tok_other, early,
    dn_own, dn_send, qk, qs, kk, ks, vk, vs, n1t, dn_acc, block, late,
):
    me = meta[ME]
    rows, width = tok_mine.shape
    half = dq.shape[1]
    part = width // COUNT
    own = pl.multiple_of(meta[HALF] * half, half)
    n1t[...] = n1[...].T
    late[...] = jnp.zeros_like(late)
    late[4:5, pl.ds(own, half)] = jnp.sum(dq[...].astype(F32), axis=0, keepdims=True)
    late[5:6, pl.ds(own, half)] = jnp.sum(dv[...].astype(F32), axis=0, keepdims=True)
    dn_acc[...] = mm(dq[...], wq[...], NT) + mm(dk[...], wk[...], NT) + mm(dv[...], wv[...], NT)
    mine = pl.multiple_of(meta[HALF] * rows, rows)
    other = pl.multiple_of((1 - meta[HALF]) * rows, rows)
    dn_send[...] = dn_acc[pl.ds(other, rows), :].astype(BF16)
    dn_own[...] = dn_acc[pl.ds(mine, rows), :]
    gain = jnp.zeros((1, width), F32)
    for place, tok in ((mine, tok_mine), (other, tok_other)):
        unit, _ = norm_parts(tok[...].astype(F32))
        gain += jnp.sum(dn_acc[pl.ds(place, rows), :] * unit, axis=0, keepdims=True)
    late[0:1, :] = gain
    late[2:3, :] = jnp.sum(dn_acc[...], axis=0, keepdims=True)
    for grad, masks, keep, send in zip((dq, dk, dv), QKV_ORDERS, (qk, kk, vk), (qs, ks, vs)):
        block[:, :half] = mm(n1t[...], grad[...])
        cols = half
        if grad is dv:
            cols = half + SMALL
            block[:, half:] = late[...].T + early[...]
        put_parts(block.at[:, :cols], me, masks, keep, send, part)


def qkv_back_call(meta, n1, dq, dk, dv, w_qkv, tok_mine, tok_other, early):
    group, width = n1.shape
    half = dq.shape[1]
    part = width // COUNT

    def full(shape):
        return pl.BlockSpec(shape, lambda i, m: (0,) * len(shape))

    def weight(which):
        return pl.BlockSpec((width, half), lambda i, m: (0, 2 * which + m[HALF]))

    rows = group // 2
    out_shape = [jax.ShapeDtypeStruct((rows, width), F32), jax.ShapeDtypeStruct((rows, width), BF16)]
    for cols in (half, half, half + SMALL):
        out_shape += [jax.ShapeDtypeStruct((2, 2, 2, 2, part, cols), BF16)] * 2
    out = pl.pallas_call(
        qkv_back_kernel,
        grid_spec=pltpu.PrefetchScalarGridSpec(
            num_scalar_prefetch=1,
            grid=(1,),
            in_specs=[
                full(n1.shape), full(dq.shape), full(dk.shape), full(dv.shape), weight(0), weight(1), weight(2),
                full(tok_mine.shape), full(tok_other.shape), full(early.shape),
            ],
            out_specs=[full(s.shape) for s in out_shape],
            scratch_shapes=[
                pltpu.VMEM((width, group), BF16), pltpu.VMEM((group, width), F32),
                pltpu.VMEM((width, half + SMALL), F32), pltpu.VMEM((SMALL, width), F32),
            ],
        ),
        out_shape=out_shape,
        compiler_params=params(),
        name="qkv_back",
    )(meta, n1, dq, dk, dv, w_qkv, w_qkv, w_qkv, tok_mine, tok_other, early)
    streams = [(out[2 + 2 * i], out[3 + 2 * i], QKV_ORDERS[i][:-1]) for i in range(3)]
    return out[0], out[1], streams


def tail_kernel(tok, gres, dn_own, dn_got, gains, out):
    unit, rstd = norm_parts(tok[...].astype(F32))
    grad = dn_own[...] + dn_got[...].astype(F32)
    out[...] = (gres[...] + norm_back(grad, unit, rstd, gains[0:1, :])).astype(BF16)


def tail_call(tok, gres, dn_own, dn_got, gains):
    rows, width = tok.shape
    block = pl.BlockSpec((rows // 4, width), lambda i: (i, 0))
    return pl.pallas_call(
        tail_kernel,
        grid=(4,),
        in_specs=[block, block, block, block, pl.BlockSpec(gains.shape, lambda i: (0, 0))],
        out_specs=block,
        out_shape=jax.ShapeDtypeStruct((rows, width), BF16),
        compiler_params=params(),
        name="tail",
    )(tok, gres, dn_own, dn_got, gains)


def paired(
    tokens, w_qkv, w_out, w_up, w_down, gains, biases, up_bias, image_cut, group_live, cotangent
):
    width = tokens.shape[1]
    half = width // 2
    part = width // COUNT
    core = lax.axis_index("dp") % 2
    me = (lax.axis_index("dp") * 2 + lax.axis_index("seq")).astype(jnp.int32)
    swap = [(i, (i & ~3) | ((i & 1) << 1) | ((i >> 1) & 1)) for i in range(COUNT)]

    def trade(value):
        return lax.ppermute(value, BOTH, swap)

    def across(value):
        return hop(value, CORE, COUNT)

    bounds = trade(jnp.concatenate([image_cut, group_live]))
    tok = trade(tokens)
    tok_far = across(tok)
    cot = trade(cotangent)
    meta = jnp.concatenate([jnp.stack([me, core.astype(jnp.int32)]), bounds])
    here = core.astype(jnp.int32).reshape(1)

    n1, q, k, v = qkv_call(meta, tok, tok_far, w_qkv, gains, biases)
    o_far, lse_far = attend_call(meta, 1 - here, q, k, v)
    a_got = across(o_far)
    o_own, lse_own = attend_call(meta, here, q, k, v)
    (block, gres, gb, ga_own, ga_send, small, gub), up, down = mid_call(
        meta, tok, cot, o_own, a_got, w_out, w_up, w_down, gains, biases, up_bias
    )
    ga_far = across(ga_send)
    block_out = trade(block)
    out = wout_call(meta, o_own, a_got, gb)
    dq, dk, dv = attend_back_call(
        meta, q, k, v, ga_own, ga_far, o_own, o_far, lse_own, lse_far, 0, half // PAIR
    )
    zero = jnp.zeros((width,), F32)
    rows = jnp.stack([zero, small[0], zero, small[1], zero, zero, small[2], small[3]])
    units = gub.reshape(COUNT, 4, part).transpose(0, 2, 1).reshape(width, 4)
    early = jnp.concatenate([rows.T, units, jnp.zeros((width, SMALL - 12), F32)], axis=1)
    dn_own, dn_send, qkv = qkv_back_call(meta, n1, dq, dk, dv, w_qkv, tok, tok_far, early)
    dn_got = across(dn_send)
    grad_tokens = trade(tail_call(tok, gres, dn_own, dn_got, gains))

    downs = reduce_streams(down, COUNT)
    grad_wdown = jnp.concatenate(downs, axis=0)
    grad_wup = jnp.concatenate(reduce_streams(up, COUNT), axis=1)
    grad_wout = jnp.concatenate(reduce_streams(out, COUNT), axis=1)
    sums = jnp.concatenate(reduce_streams(qkv, COUNT), axis=2)
    kept, got = sums[0], across(sums[1])
    first = jnp.where(core == 0, kept, got)
    second = jnp.where(core == 0, got, kept)
    cols = []
    for i in range(3):
        cols += [first[:, i * half : (i + 1) * half], second[:, i * half : (i + 1) * half]]
    grad_qkv = jnp.concatenate(cols, axis=1)
    little = kept[:, 3 * half :] + got[:, 3 * half :]
    grad_gains = little[:, 0:2].T
    grad_biases = little[:, 2:8].T
    grad_upbias = little[:, 8:12].T.reshape(-1)
    return (
        block_out, grad_tokens, grad_qkv, grad_wout, grad_wup, grad_wdown, grad_gains, grad_biases, grad_upbias,
    )


def norm_rows(values, gain, shift):
    center = values - jnp.mean(values, axis=-1, keepdims=True)
    spread = jnp.mean(center * center, axis=-1, keepdims=True)
    return center * lax.rsqrt(spread + EPSILON) * gain + shift


def split_heads(values):
    return values.reshape(values.shape[0], HEADS, -1).transpose(1, 0, 2)


def join_heads(values):
    return values.transpose(1, 0, 2).reshape(values.shape[1], -1)


def head_probs(query_head, key_head, mask):
    raw = jnp.einsum("qd,kd->qk", query_head, key_head, preferred_element_type=jnp.float32)
    return jax.nn.softmax(raw * 0.125 + mask, axis=-1)


def shards(
    tokens, w_qkv, w_out, w_up, w_down, gains, biases, up_bias, image_cut, group_live, cotangent
):
    rows_here = tokens.shape[0]
    width = tokens.shape[1]
    group = rows_here * lax.axis_size("seq")
    first_row = lax.axis_index("seq") * rows_here
    cut_row = image_cut[0]
    live_rows = group_live[0]
    key_pos = jnp.arange(group, dtype=jnp.int32)
    query_pos = first_row + jnp.arange(rows_here, dtype=jnp.int32)
    query_live = (query_pos < live_rows)[:, None]
    allowed = ((query_pos >= cut_row)[:, None] == (key_pos >= cut_row)[None, :]) & (
        key_pos < live_rows
    )[None, :]
    mask = jnp.where(allowed, 0.0, -1000000000.0).astype(jnp.float32)
    inputs = tokens.astype(jnp.float32)
    normed_one, norm_back_one = jax.vjp(norm_rows, inputs, gains[0], biases[0])
    normed_one = normed_one.astype(jnp.bfloat16)
    projected = jnp.dot(normed_one, w_qkv, preferred_element_type=jnp.float32)
    queries = (projected[:, :width] + biases[2]).astype(jnp.bfloat16)
    key_rows = projected[:, width : 2 * width].astype(jnp.bfloat16)
    value_rows = (projected[:, 2 * width :] + biases[3]).astype(jnp.bfloat16)
    kv_local = jnp.concatenate([key_rows, value_rows], axis=1)
    kv_whole = lax.all_gather(kv_local, "seq", axis=0, tiled=True)
    query_heads = split_heads(queries)

    def attend(operands):
        query_head, key_head, value_head = operands
        probs = head_probs(query_head, key_head, mask)
        return jnp.dot(probs.astype(jnp.bfloat16), value_head, preferred_element_type=jnp.float32)

    heads_out = lax.map(
        attend, (query_heads, split_heads(kv_whole[:, :width]), split_heads(kv_whole[:, width:]))
    )
    attended = join_heads(heads_out).astype(jnp.bfloat16)
    residual = inputs + jnp.dot(attended, w_out, preferred_element_type=jnp.float32) + biases[4]
    normed_two, norm_back_two = jax.vjp(norm_rows, residual, gains[1], biases[1])
    normed_two = normed_two.astype(jnp.bfloat16)
    hidden_pre = jnp.dot(normed_two, w_up, preferred_element_type=jnp.float32) + up_bias
    activated, gelu_back = jax.vjp(partial(jax.nn.gelu, approximate=False), hidden_pre)
    activated = activated.astype(jnp.bfloat16)
    mlp_out = jnp.dot(activated, w_down, preferred_element_type=jnp.float32) + biases[5]
    block_out = jnp.where(query_live, residual + mlp_out, 0.0).astype(jnp.bfloat16)
    grad_live = jnp.where(query_live, cotangent, jnp.zeros_like(cotangent))
    grad_wdown = jnp.einsum("rf,rd->fd", activated, grad_live, preferred_element_type=jnp.float32)
    grad_activated = jnp.einsum("rd,fd->rf", grad_live, w_down, preferred_element_type=jnp.float32)
    grad_hidden = gelu_back(grad_activated)[0].astype(jnp.bfloat16)
    grad_wup = jnp.einsum("rd,rf->df", normed_two, grad_hidden, preferred_element_type=jnp.float32)
    grad_normed_two = jnp.einsum("rf,df->rd", grad_hidden, w_up, preferred_element_type=jnp.float32)
    grad_res_norm, gain_two, shift_two = norm_back_two(grad_normed_two)
    grad_residual = grad_live.astype(jnp.float32) + grad_res_norm
    grad_branch = grad_residual.astype(jnp.bfloat16)
    grad_wout = jnp.einsum("rd,re->de", attended, grad_branch, preferred_element_type=jnp.float32)
    grad_attended = jnp.einsum(
        "re,de->rd", grad_branch, w_out, preferred_element_type=jnp.float32
    ).astype(jnp.bfloat16)

    def attend_back(operands):
        query_head, key_head, value_head, grad_head = operands
        probs = head_probs(query_head, key_head, mask)
        grad_probs = jnp.einsum(
            "qd,kd->qk", grad_head, value_head, preferred_element_type=jnp.float32
        )
        grad_scores = probs * (grad_probs - jnp.sum(probs * grad_probs, axis=-1, keepdims=True))
        grad_raw = (grad_scores * 0.125).astype(jnp.bfloat16)
        grad_query = jnp.dot(grad_raw, key_head, preferred_element_type=jnp.float32)
        grad_key = jnp.einsum("qk,qd->kd", grad_raw, query_head, preferred_element_type=jnp.float32)
        grad_value = jnp.einsum(
            "qk,qd->kd", probs.astype(jnp.bfloat16), grad_head, preferred_element_type=jnp.float32
        )
        return (grad_query, grad_key, grad_value)

    grad_q_heads, grad_k_heads, grad_v_heads = lax.map(
        attend_back,
        (
            query_heads,
            split_heads(kv_whole[:, :width]),
            split_heads(kv_whole[:, width:]),
            split_heads(grad_attended),
        ),
    )
    grad_queries = join_heads(grad_q_heads).astype(jnp.bfloat16)
    grad_kv_terms = jnp.concatenate([join_heads(grad_k_heads), join_heads(grad_v_heads)], axis=1)
    grad_kv = lax.psum_scatter(
        grad_kv_terms.astype(jnp.bfloat16), "seq", scatter_dimension=0, tiled=True
    )
    grad_projected = jnp.concatenate([grad_queries, grad_kv], axis=1)
    grad_wqkv = jnp.einsum(
        "rd,re->de", normed_one, grad_projected, preferred_element_type=jnp.float32
    )
    grad_normed_one = jnp.einsum(
        "re,de->rd", grad_projected, w_qkv, preferred_element_type=jnp.float32
    )
    grad_in_norm, gain_one, shift_one = norm_back_one(grad_normed_one)
    grad_tokens = (grad_residual + grad_in_norm).astype(jnp.bfloat16)
    grad_gains = jnp.stack([gain_one, gain_two])
    grad_biases = jnp.stack(
        [
            shift_one,
            shift_two,
            jnp.sum(grad_queries.astype(jnp.float32), axis=0),
            jnp.sum(grad_kv[:, width:].astype(jnp.float32), axis=0),
            jnp.sum(grad_branch.astype(jnp.float32), axis=0),
            jnp.sum(grad_live.astype(jnp.float32), axis=0),
        ]
    )
    grad_upbias = jnp.sum(grad_hidden.astype(jnp.float32), axis=0)
    summed = (
        lax.psum_scatter(grad_wqkv, ("dp", "seq"), scatter_dimension=0, tiled=True),
        lax.psum_scatter(grad_wout, ("dp", "seq"), scatter_dimension=0, tiled=True),
        lax.psum_scatter(grad_wup, ("dp", "seq"), scatter_dimension=0, tiled=True),
        lax.psum_scatter(grad_wdown, ("dp", "seq"), scatter_dimension=0, tiled=True),
        lax.psum_scatter(grad_gains, ("dp", "seq"), scatter_dimension=1, tiled=True),
        lax.psum_scatter(grad_biases, ("dp", "seq"), scatter_dimension=1, tiled=True),
        lax.psum_scatter(grad_upbias, ("dp", "seq"), scatter_dimension=0, tiled=True),
    )
    return (
        block_out,
        grad_tokens,
        summed[0],
        summed[1],
        summed[2],
        summed[3],
        summed[4],
        summed[5],
        summed[6],
    )


def solution(mesh):
    in_specs = (
        P(("dp", "seq"), None),
        P(),
        P(),
        P(),
        P(),
        P(),
        P(),
        P(),
        P("dp"),
        P("dp"),
        P(("dp", "seq"), None),
    )
    out_specs = (
        P(("dp", "seq"), None),
        P(("dp", "seq"), None),
        P(("dp", "seq"), None),
        P(("dp", "seq"), None),
        P(("dp", "seq"), None),
        P(("dp", "seq"), None),
        P(None, ("dp", "seq")),
        P(None, ("dp", "seq")),
        P(("dp", "seq")),
    )
    fits = mesh.shape["seq"] == 2 and mesh.shape["dp"] * 2 == COUNT
    return jax.shard_map(paired if fits else shards, mesh=mesh, in_specs=in_specs, out_specs=out_specs, check_vma=False)
```

```python
from functools import partial

import jax
import jax.numpy as jnp
from jax import lax
from jax.experimental import pallas as pl
from jax.experimental.pallas import tpu as pltpu
from jax.sharding import PartitionSpec as P

HEADS = 12
HEAD_DIM = 64
PAIR = 2 * HEAD_DIM
EPSILON = 1e-06
BOTH = ("dp", "seq")
FAR = -1000000000.0
F32 = jnp.float32
BF16 = jnp.bfloat16

ME, HALF, CUT, LIVE = 0, 1, 2, 3

NN = (((1,), (0,)), ((), ()))
NT = (((1,), (1,)), ((), ()))
TN = (((0,), (0,)), ((), ()))


def mm(a, b, dims=NN):
    return lax.dot_general(a, b, dims, preferred_element_type=F32)


def params(**more):
    return pltpu.CompilerParams(vmem_limit_bytes=56 * 1024 * 1024, **more)


def norm_parts(values):
    center = values - jnp.mean(values, axis=-1, keepdims=True)
    spread = jnp.mean(center * center, axis=-1, keepdims=True)
    rstd = lax.rsqrt(spread + EPSILON)
    return center * rstd, rstd


def norm_back(grad, unit, rstd, gain):
    scaled = grad * gain
    first = jnp.mean(scaled, axis=-1, keepdims=True)
    second = jnp.mean(scaled * unit, axis=-1, keepdims=True)
    return rstd * (scaled - first - unit * second)


SIDE_X, CORE, SIDE_Y, Z_NEAR, Z_FAR = 1, 2, 4, 8, 24
ORDERS = (
    (SIDE_X, SIDE_Y, Z_NEAR, Z_FAR), (SIDE_Y, Z_NEAR, SIDE_X, Z_FAR), (Z_NEAR, SIDE_X, SIDE_Y, Z_FAR),
)
COUNT = 32
LANES = 384
PART = 24


def hop(value, mask):
    return lax.ppermute(value, BOTH, [(i, i ^ mask) for i in range(COUNT)])


def places(masks):
    out = [0]
    for mask in masks:
        out = [value ^ (mask * bit) for value in out for bit in (0, 1)]
    return out


def without(kernel, first, count):
    def run(*refs):
        return kernel(*refs[:first], *refs[first + count :])

    return run


def unread(count):
    return [pl.BlockSpec(memory_space=pl.ANY)] * count


def fold_kernel(*refs, sizes):
    total = sum(len(pieces) for pieces in sizes)
    keeps, got, outs = refs[:total], refs[total : 2 * total], refs[2 * total :]
    at = 0
    for stream, pieces in enumerate(sizes):
        low = 0
        for rows in pieces:
            for bit in (0, 1):
                both = keeps[at][bit, 0].astype(F32) + got[at][bit, 0].astype(F32)
                outs[2 * stream + bit][0, low : low + rows, :] = both.astype(BF16)
            low += rows
            at += 1


def fold_call(streams, after=()):
    sizes = [[kept.shape[1] for kept, _ in pieces] for pieces in streams]
    count = streams[0][0][0].shape[0] // 2
    view = lambda a: a.reshape(2, count, *a.shape[1:])
    kept = [view(k) for pieces in streams for k, _ in pieces]
    got = [view(g) for pieces in streams for _, g in pieces]
    spec = lambda a: pl.BlockSpec((2, 1, *a.shape[2:]), lambda i: (0, i, 0, 0))
    rows = [sum(pieces) for pieces in sizes for _ in (0, 1)]
    out = pl.pallas_call(
        without(partial(fold_kernel, sizes=sizes), 2 * len(kept), len(after)),
        grid=(count,),
        in_specs=[spec(a) for a in kept + got] + unread(len(after)),
        out_specs=[pl.BlockSpec((1, n, LANES), lambda i: (i, 0, 0)) for n in rows],
        out_shape=[jax.ShapeDtypeStruct((count, n, LANES), BF16) for n in rows],
        compiler_params=params(),
        name="fold",
    )(*kept, *got, *after)
    return [(out[2 * i], out[2 * i + 1]) for i in range(len(streams))]


def hops(step, sends):
    return [hop(send, masks[step]) for send, masks in zip(sends, ORDERS)]


def put_rows(source, me, masks, keep, send, low, col=0, at=None):
    cols = pl.ds(col, LANES)
    for bit, ref in ((0, keep), (1, send)):
        for place, value in enumerate(places(masks[1:])):
            chip = (me & ~CORE) ^ (value ^ (masks[0] * bit))
            first = pl.multiple_of(chip * PART, 8)
            second = pl.multiple_of((chip + CORE) * PART, 8)
            where = (lambda r: source[pl.ds(r, PART), cols]) if at is None else (lambda r: source[at, pl.ds(r, PART), cols])
            both = jnp.concatenate([where(first), where(second)], axis=0)
            ref[place, low : low + 2 * PART, :] = both.astype(BF16)


def qkv_kernel(meta, mine, other, wq, wk, wv, gains, biases, n1_ref, q_ref, k_ref, v_ref):
    step = pl.program_id(0)

    def run(ref):
        unit, _ = norm_parts(ref[...].astype(F32))
        normed = (unit * gains[0:1, :] + biases[0:1, :]).astype(BF16)
        n1_ref[...] = normed
        half = q_ref.shape[1]
        first = pl.multiple_of(meta[HALF] * half, half)
        q_ref[...] = (mm(normed, wq[...]) + biases_at(biases, 2, first, half)).astype(BF16)
        k_ref[...] = mm(normed, wk[...]).astype(BF16)
        v_ref[...] = (mm(normed, wv[...]) + biases_at(biases, 3, first, half)).astype(BF16)

    @pl.when(step == 0)
    def _():
        run(mine)

    @pl.when(step == 1)
    def _():
        run(other)


def biases_at(biases, row, first, size):
    return biases[row : row + 1, pl.ds(first, size)]


def qkv_call(meta, mine, other, w_qkv, gains, biases):
    rows, width = mine.shape
    half = width // 2
    full = lambda shape: pl.BlockSpec(shape, lambda i, m: (0, 0))
    weight = lambda part: pl.BlockSpec((width, half), lambda i, m: (0, 2 * part + m[HALF]))
    out = lambda cols: pl.BlockSpec((rows, cols), lambda i, m: (i ^ m[HALF], 0))
    shape = lambda cols: jax.ShapeDtypeStruct((2 * rows, cols), BF16)
    return pl.pallas_call(
        qkv_kernel,
        grid_spec=pltpu.PrefetchScalarGridSpec(
            num_scalar_prefetch=1,
            grid=(2,),
            in_specs=[
                full((rows, width)), full((rows, width)), weight(0), weight(1), weight(2),
                full(gains.shape), full(biases.shape),
            ],
            out_specs=[out(width), out(half), out(half), out(half)],
        ),
        out_shape=[shape(width), shape(half), shape(half), shape(half)],
        compiler_params=params(),
        name="qkv",
    )(meta, mine, other, w_qkv, w_qkv, w_qkv, gains, biases)


TILE = 256


def lanes(rows):
    return lax.broadcasted_iota(jnp.int32, (rows, PAIR), 1)


def own_lanes(rows, head):
    return (lanes(rows) // HEAD_DIM) == head


def key_side(key_pair, head, meta):
    rows = key_pair.shape[0]
    at = lanes(rows) - (1 - head) * HEAD_DIM
    pos = lax.broadcasted_iota(jnp.int32, (rows, PAIR), 0)
    alive = pos < meta[LIVE]
    second = pos >= meta[CUT]
    in_first = alive & jnp.logical_not(second)
    in_second = alive & second
    extra = jnp.where(
        ((at == 0) & jnp.logical_not(in_first)) | ((at == 1) & jnp.logical_not(in_second)), FAR, 0.0
    )
    return jnp.where(own_lanes(rows, head), key_pair.astype(F32), extra).astype(BF16)


def query_side(query_pair, head, first_row, meta):
    rows = query_pair.shape[0]
    at = lanes(rows) - (1 - head) * HEAD_DIM
    second = first_row + lax.broadcasted_iota(jnp.int32, (rows, PAIR), 0) >= meta[CUT]
    extra = jnp.where(
        ((at == 0) & jnp.logical_not(second)) | ((at == 1) & second), 1.0, 0.0
    )
    return jnp.where(own_lanes(rows, head), query_pair.astype(F32) * 0.125, extra).astype(BF16)


def key_range(first_row, group, meta):
    cut = meta[CUT]
    live = meta[LIVE]
    only_first = first_row + TILE <= cut
    only_second = first_row >= cut
    low = jnp.where(only_second, cut, 0)
    high = jnp.where(only_first, cut, live)
    low = (low // 128) * 128
    steps = (high - low + (TILE - 1)) // TILE
    start = jnp.minimum(low, group - steps * TILE)
    return pl.multiple_of(start, 128), steps


def by_width(steps, group, body):
    for count in range(1, group // TILE + 1):

        @pl.when(steps == count)
        def _(count=count):
            body(count * TILE)


def attend_kernel(meta, q_ref, k_ref, v_ref, o_ref, lse_ref, kx_ref, vt_ref):
    rows = q_ref.shape[0]
    group = k_ref.shape[0]
    for head in (0, 1):
        kx_ref[head] = key_side(k_ref[...], head, meta)
    vt_ref[...] = v_ref[...].T

    def tile(index, carry):
        at = pl.multiple_of(index * TILE, TILE)
        first_row = at
        start, steps = key_range(first_row, group, meta)
        query = q_ref[pl.ds(at, TILE), :]

        def body(width):
            parts = []
            for head in (0, 1):
                qx = query_side(query, head, first_row, meta)
                scores = mm(kx_ref[head, pl.ds(start, width), :], qx, NT)
                top = jnp.max(scores, axis=0, keepdims=True)
                weight = jnp.exp(scores - top).astype(BF16)
                value = vt_ref[head * HEAD_DIM : (head + 1) * HEAD_DIM, pl.ds(start, width)]
                left = jnp.concatenate([value, jnp.ones((16, width), BF16)], axis=0)
                both = mm(left, weight)
                total = both[HEAD_DIM : HEAD_DIM + 1, :]
                parts.append(both[:HEAD_DIM, :] / total)
                lse_ref[0, head : head + 1, pl.ds(at, TILE)] = top + jnp.log(total)
            o_ref[pl.ds(at, TILE), :] = jnp.concatenate(parts, axis=0).T.astype(BF16)

        by_width(steps, group, body)
        return carry

    lax.fori_loop(0, rows // TILE, tile, 0)


def attend_call(meta, q, k, v):
    group, half = q.shape
    pairs = half // PAIR
    whole = pl.BlockSpec((group, PAIR), lambda p, m: (0, p))
    return pl.pallas_call(
        attend_kernel,
        grid_spec=pltpu.PrefetchScalarGridSpec(
            num_scalar_prefetch=1,
            grid=(pairs,),
            in_specs=[whole, whole, whole],
            out_specs=[whole, pl.BlockSpec((1, 2, group), lambda p, m: (p, 0, 0))],
            scratch_shapes=[pltpu.VMEM((2, group, PAIR), BF16), pltpu.VMEM((PAIR, group), BF16)],
        ),
        out_shape=[
            jax.ShapeDtypeStruct((group, half), BF16),
            jax.ShapeDtypeStruct((pairs, 2, group), F32),
        ],
        compiler_params=params(),
        name="attend",
    )(meta, q, k, v)


def attend_back_kernel(
    meta, q_ref, k_ref, v_ref, do_ref, o_ref, lse_ref, dq_ref, dk_ref, dv_ref, kx_ref, kt_ref, dk_acc, dv_acc,
):
    group = k_ref.shape[0]
    for head in (0, 1):
        kx_ref[head] = key_side(k_ref[...], head, meta)
    kt_ref[...] = k_ref[...].T
    dk_acc[...] = jnp.zeros_like(dk_acc)
    dv_acc[...] = jnp.zeros_like(dv_acc)

    def tile(index, carry):
        at = pl.multiple_of(index * TILE, TILE)
        first_row = at
        start, steps = key_range(first_row, group, meta)
        query = q_ref[pl.ds(first_row, TILE), :]
        grad = do_ref[pl.ds(at, TILE), :]
        dots = (grad.astype(F32) * o_ref[pl.ds(at, TILE), :].astype(F32)).T

        def body(width):
            probs, raws, masked_grads, masked_queries, dqs = [], [], [], [], []
            for head in (0, 1):
                mine = own_lanes(TILE, head)
                qx = query_side(query, head, first_row, meta)
                dox = jnp.where(mine, grad, jnp.zeros_like(grad))
                scores = mm(kx_ref[head, pl.ds(start, width), :], qx, NT)
                prob = jnp.exp(scores - lse_ref[0, head : head + 1, pl.ds(at, TILE)])
                gprob = mm(v_ref[pl.ds(start, width), :], dox, NT)
                delta = jnp.sum(dots[head * HEAD_DIM : (head + 1) * HEAD_DIM, :], axis=0, keepdims=True)
                raw = (prob * (gprob - delta)).astype(BF16)
                keys_t = kt_ref[head * HEAD_DIM : (head + 1) * HEAD_DIM, pl.ds(start, width)]
                dqs.append(mm(keys_t, raw))
                probs.append(prob.astype(BF16))
                raws.append(raw)
                masked_grads.append(dox)
                masked_queries.append(jnp.where(mine, query * jnp.asarray(0.125, BF16), jnp.zeros_like(query)))
            dv_acc[pl.ds(start, width), :] += mm(
                jnp.concatenate(probs, axis=1), jnp.concatenate(masked_grads, axis=0)
            )
            dk_acc[pl.ds(start, width), :] += mm(
                jnp.concatenate(raws, axis=1), jnp.concatenate(masked_queries, axis=0)
            )
            dq = jnp.concatenate(dqs, axis=0).T * 0.125
            dq_ref[pl.ds(first_row, TILE), :] = dq.astype(BF16)

        by_width(steps, group, body)
        return carry

    lax.fori_loop(0, group // TILE, tile, 0)
    dk_ref[...] = dk_acc[...].astype(BF16)
    dv_ref[...] = dv_acc[...].astype(BF16)


def attend_back_call(meta, q, k, v, grad, o, lse, first, count, after=()):
    group, half = q.shape
    whole = pl.BlockSpec((group, PAIR), lambda p, m: (0, p + first))
    out = pl.BlockSpec((group, PAIR), lambda p, m: (0, p))
    return pl.pallas_call(
        without(attend_back_kernel, 7, len(after)),
        grid_spec=pltpu.PrefetchScalarGridSpec(
            num_scalar_prefetch=1,
            grid=(count,),
            in_specs=[whole] * 5 + [pl.BlockSpec((1, 2, group), lambda p, m: (p + first, 0, 0))] + unread(len(after)),
            out_specs=[out, out, out],
            scratch_shapes=[
                pltpu.VMEM((2, group, PAIR), BF16),
                pltpu.VMEM((PAIR, group), BF16),
                pltpu.VMEM((group, PAIR), F32),
                pltpu.VMEM((group, PAIR), F32),
            ],
        ),
        out_shape=[jax.ShapeDtypeStruct((group, count * PAIR), BF16)] * 3,
        compiler_params=params(),
        name="attend_back",
    )(meta, q, k, v, grad, o, lse, *after)


UNITS = 192
STEPS = 2
ROWS = 256

ERF_TOP = (0.00022905065861350646, 0.0034082910107109506, 0.050955695062380861, 0.18520832239976145, 1.128379143519084)
ERF_LOW = (
    -1.1791602954361697e-7, 0.000023547966471313185, 0.0010179625278914885, 0.014070470171167667,
    0.11098505178285362, 0.49746925110067538, 1.0,
)


def erf(x):
    x = jnp.clip(x, -3.832506856900711, 3.832506856900711)
    square = x * x
    top = jnp.full_like(x, ERF_TOP[0])
    for c in ERF_TOP[1:]:
        top = top * square + c
    low = jnp.full_like(x, ERF_LOW[0])
    for c in ERF_LOW[1:]:
        low = low * square + c
    return x * top / low


def mid_kernel(
    meta, tok_mine, tok_other, cot_mine, cot_other, a_own, a_got, w_out, w_up, w_down, gains, biases, up_bias,
    res_ref, block_ref, block_send, dn_ref, gub_ref, k0, s0, k1, s1, k2, s2,
    n2, n2t, gl, act, gh, wu, up_acc, down_acc, out_acc, dn_acc,
):
    step = pl.program_id(0)
    rows, width = tok_mine.shape
    half = a_own.shape[1]
    chunk = wu.shape[1]
    me = meta[ME]
    own = pl.multiple_of(meta[HALF] * half, half)
    far = pl.multiple_of((1 - meta[HALF]) * half, half)
    mine = pl.multiple_of(meta[HALF] * rows, rows)
    other = pl.multiple_of((1 - meta[HALF]) * rows, rows)

    @pl.when(step == 0)
    def _():
        for place, tok, cot in ((mine, tok_mine, cot_mine), (other, tok_other, cot_other)):
            for low in range(0, rows, ROWS):
                at = pl.ds(pl.multiple_of(place + low, ROWS), ROWS)
                residual = (
                    tok[low : low + ROWS, :].astype(F32)
                    + mm(a_own[at, :], w_out[pl.ds(own, half), :])
                    + mm(a_got[at, :], w_out[pl.ds(far, half), :])
                    + biases[4:5, :]
                )
                res_ref[at, :] = residual
                unit, _ = norm_parts(residual)
                n2[at, :] = (unit * gains[1:2, :] + biases[1:2, :]).astype(BF16)
                live = place + low + lax.broadcasted_iota(jnp.int32, (ROWS, 1), 0) < meta[LIVE]
                cots = cot[low : low + ROWS, :]
                gl[at, :] = jnp.where(live, cots, jnp.zeros_like(cots))
        n2t[...] = n2[...].T

    for core in (0, 1):

        @pl.when(meta[HALF] == core)
        def _(core=core):
            for block in range(chunk // UNITS):
                at = (2 * block + core) * UNITS
                wu[:, block * UNITS : (block + 1) * UNITS] = w_up[:, at : at + UNITS]

    wd = w_down[...].reshape(chunk, width)
    gub = jnp.zeros((1, chunk), F32)
    for low in range(0, 2 * rows, ROWS):
        at = slice(low, low + ROWS)
        hidden = mm(n2[at, :], wu[...]) + up_bias[...]
        gact = mm(gl[at, :], wd, NT)
        cdf = 0.5 * (1.0 + erf(hidden * 0.7071067811865476))
        pdf = jnp.exp(-0.5 * hidden * hidden) * 0.3989422804014327
        active = (hidden * cdf).astype(BF16)
        grad_hidden = gact * (cdf + hidden * pdf)
        gub += jnp.sum(grad_hidden, axis=0, keepdims=True)
        grad_hidden = grad_hidden.astype(BF16)
        act[at, :] = active
        gh[at, :] = grad_hidden
        out_acc[at, :] = jnp.where(step == 0, 0.0, out_acc[at, :]) + mm(active, wd)
        dn_acc[at, :] = jnp.where(step == 0, 0.0, dn_acc[at, :]) + mm(grad_hidden, wu[...], NT)
    gub_ref[...] = gub
    down_acc[pl.ds(pl.multiple_of(step * chunk, chunk), chunk), :] = mm(act[...], gl[...], TN).astype(BF16)
    up_acc[step] = mm(n2t[...], gh[...])

    @pl.when(step == STEPS - 1)
    def _():
        at = pl.ds(mine, rows)
        block_ref[...] = res_ref[at, :] + out_acc[at, :] + biases[5:6, :]
        block_send[...] = out_acc[pl.ds(other, rows), :].astype(BF16)
        dn_ref[...] = dn_acc[...].astype(BF16)
        for block, (keep, send, masks, low) in enumerate(
            ((k0, s0, ORDERS[0], 0), (k0, s0, ORDERS[0], 48), (k0, s0, ORDERS[0], 96), (k1, s1, ORDERS[1], 0))
        ):
            put_rows(up_acc, me, masks, keep, send, low, (block % 2) * LANES, block // 2)
        for col, (keep, send, masks, low) in enumerate(((k1, s1, ORDERS[1], 48), (k2, s2, ORDERS[2], 0))):
            for bit, ref in ((0, keep), (1, send)):
                for place, value in enumerate(places(masks[1:])):
                    chip = me ^ (value ^ (masks[0] * bit))
                    first = pl.multiple_of((chip // 4) * UNITS + (chip & 1) * (UNITS // 2), UNITS // 2)
                    ref[place, low : low + UNITS // 2, :] = down_acc[
                        pl.ds(first, UNITS // 2), col * LANES : (col + 1) * LANES
                    ]


def full(shape):
    return pl.BlockSpec(shape, lambda *a: (0,) * len(shape))


def once(shape):
    return pl.BlockSpec(shape, lambda *a: (0,) * len(shape), pipeline_mode=pl.Buffered(1))


def mid_call(meta, tok_mine, tok_other, cot_mine, cot_other, a_own, a_got, w_out, w_up, w_down, gains, biases, up_bias):
    rows, width = tok_mine.shape
    ff = w_up.shape[1]
    chunk = ff // 2 // STEPS
    blocks = chunk // UNITS
    group = 2 * rows
    stream = [144, 144, 144, 144, 96, 96]
    out_shape = [
        jax.ShapeDtypeStruct((group, width), F32), jax.ShapeDtypeStruct((rows, width), F32),
        jax.ShapeDtypeStruct((rows, width), BF16), jax.ShapeDtypeStruct((group, width), BF16),
        jax.ShapeDtypeStruct((1, ff // 2), F32),
    ] + [jax.ShapeDtypeStruct((8, n, LANES), BF16) for n in stream]
    out_specs = [once(s.shape) for s in out_shape]
    out_specs[4] = pl.BlockSpec((1, chunk), lambda i, m: (0, i))
    out = pl.pallas_call(
        mid_kernel,
        grid_spec=pltpu.PrefetchScalarGridSpec(
            num_scalar_prefetch=1,
            grid=(STEPS,),
            in_specs=[
                once((rows, width)), once((rows, width)), once((rows, width)), once((rows, width)),
                once(a_own.shape), once(a_got.shape), once(w_out.shape),
                pl.BlockSpec((width, 2 * chunk), lambda i, m: (0, i)),
                pl.BlockSpec((blocks, 1, UNITS, width), lambda i, m: (i, m[HALF], 0, 0)),
                full(gains.shape), full(biases.shape),
                pl.BlockSpec((1, chunk), lambda i, m: (0, i)),
            ],
            out_specs=out_specs,
            scratch_shapes=[
                pltpu.VMEM((group, width), BF16), pltpu.VMEM((width, group), BF16), pltpu.VMEM((group, width), BF16),
                pltpu.VMEM((group, chunk), BF16), pltpu.VMEM((group, chunk), BF16), pltpu.VMEM((width, chunk), BF16),
                pltpu.VMEM((STEPS, width, chunk), F32), pltpu.VMEM((ff // 2, width), BF16),
                pltpu.VMEM((group, width), F32), pltpu.VMEM((group, width), F32),
            ],
        ),
        out_shape=out_shape,
        compiler_params=params(),
        name="mid",
    )(
        meta, tok_mine, tok_other, cot_mine, cot_other, a_own, a_got, w_out, w_up,
        w_down.reshape(ff // UNITS // 2, 2, UNITS, width), gains, biases, up_bias,
    )
    return out[:5], out[5::2], out[6::2]


def branch_kernel(
    meta, res, cot_mine, cot_other, dn_own, dn_got, a_own, a_got, w_out, gains,
    gres_ref, ga_ref, small_ref, keep, send, gb, whole,
):
    rows, width = cot_mine.shape
    half = a_own.shape[1]
    own = pl.multiple_of(meta[HALF] * half, half)
    far = pl.multiple_of((1 - meta[HALF]) * half, half)
    mine = pl.multiple_of(meta[HALF] * rows, rows)
    other = pl.multiple_of((1 - meta[HALF]) * rows, rows)
    small = jnp.zeros((4, width), F32)
    for place, cot in ((mine, cot_mine), (other, cot_other)):
        for low in range(0, rows, ROWS):
            at = pl.ds(pl.multiple_of(place + low, ROWS), ROWS)
            unit, rstd = norm_parts(res[at, :])
            grad = dn_own[at, :].astype(F32) + dn_got[at, :].astype(F32)
            live = place + low + lax.broadcasted_iota(jnp.int32, (ROWS, 1), 0) < meta[LIVE]
            gl = jnp.where(live, cot[low : low + ROWS, :].astype(F32), 0.0)
            gres = gl + norm_back(grad, unit, rstd, gains[1:2, :])
            branch = gres.astype(BF16)
            gb[at, :] = branch
            if cot is cot_mine:
                gres_ref[low : low + ROWS, :] = gres
                small += jnp.concatenate(
                    [jnp.sum(a, axis=0, keepdims=True) for a in (grad * unit, grad, branch.astype(F32), gl)], axis=0
                )
    small_ref[0:4, :] = small
    small_ref[4:8, :] = jnp.zeros((4, width), F32)
    ga_ref[...] = mm(gb[...], w_out[pl.ds(own, half), :], NT).astype(BF16)
    part = gb[:, pl.ds(own, half)]
    whole[pl.ds(own, half), :] = mm(a_own[...], part, TN)
    whole[pl.ds(far, half), :] = mm(a_got[...], part, TN)
    put_rows(whole, meta[ME], ORDERS[2], keep, send, 0)


def branch_call(meta, res, cot_mine, cot_other, dn_own, dn_got, a_own, a_got, w_out, gains):
    rows, width = cot_mine.shape
    group, half = a_own.shape
    args = (res, cot_mine, cot_other, dn_own, dn_got, a_own, a_got, w_out, gains)
    out_shape = [
        jax.ShapeDtypeStruct((rows, width), F32), jax.ShapeDtypeStruct((group, half), BF16),
        jax.ShapeDtypeStruct((8, width), F32),
    ] + [jax.ShapeDtypeStruct((8, 2 * PART, LANES), BF16)] * 2
    return pl.pallas_call(
        branch_kernel,
        grid_spec=pltpu.PrefetchScalarGridSpec(
            num_scalar_prefetch=1,
            grid=(1,),
            in_specs=[full(a.shape) for a in args],
            out_specs=[full(a.shape) for a in out_shape],
            scratch_shapes=[pltpu.VMEM((group, width), BF16), pltpu.VMEM((width, half), F32)],
        ),
        out_shape=out_shape,
        compiler_params=params(),
        name="branch",
    )(meta, *args)


SMALL = 128


def qkv_back_kernel(
    meta, n1, d0, d1, d2, d3, d4, d5, d6, d7, d8, wq, wk, wv, tok_mine, tok_other, early,
    dn_own, dn_send, k0, s0, k1, s1, k2, s2, n1t, dn_acc, block, late,
):
    me = meta[ME]
    rows, width = tok_mine.shape
    half = wq.shape[1]
    own = pl.multiple_of(meta[HALF] * half, half)
    dq, dk, dv = [
        jnp.concatenate([a[...] for a in parts], axis=1) for parts in ((d0, d3, d6), (d1, d4, d7), (d2, d5, d8))
    ]
    n1t[...] = n1[...].T
    late[...] = jnp.zeros_like(late)
    late[4:5, pl.ds(own, half)] = jnp.sum(dq.astype(F32), axis=0, keepdims=True)
    late[5:6, pl.ds(own, half)] = jnp.sum(dv.astype(F32), axis=0, keepdims=True)
    dn_acc[...] = mm(dq, wq[...], NT) + mm(dk, wk[...], NT) + mm(dv, wv[...], NT)
    mine = pl.multiple_of(meta[HALF] * rows, rows)
    other = pl.multiple_of((1 - meta[HALF]) * rows, rows)
    dn_send[...] = dn_acc[pl.ds(other, rows), :].astype(BF16)
    dn_own[...] = dn_acc[pl.ds(mine, rows), :]
    gain = jnp.zeros((1, width), F32)
    for place, tok in ((mine, tok_mine), (other, tok_other)):
        unit, _ = norm_parts(tok[...].astype(F32))
        gain += jnp.sum(dn_acc[pl.ds(place, rows), :] * unit, axis=0, keepdims=True)
    late[0:1, :] = gain
    late[2:3, :] = jnp.sum(dn_acc[...], axis=0, keepdims=True)
    for grad, masks, keep, send in zip((dq, dk, dv), ORDERS, (k0, k1, k2), (s0, s1, s2)):
        block[...] = mm(n1t[...], grad)
        put_rows(block, me, masks, keep, send, 0)
    block[:, :SMALL] = late[...].T + early[...]
    for bit, ref in ((0, k2), (1, s2)):
        for place, value in enumerate(places(ORDERS[2][1:])):
            chip = (me & ~CORE) ^ (value ^ (ORDERS[2][0] * bit))
            both = jnp.concatenate(
                [block[pl.ds(pl.multiple_of((chip + c) * PART, 8), PART), :SMALL] for c in (0, CORE)], axis=0
            )
            ref[place, 2 * PART :, :] = jnp.concatenate([both[16 * i : 16 * i + 16] for i in range(3)], axis=1).astype(BF16)


def qkv_back_call(meta, n1, grads, w_qkv, tok_mine, tok_other, early, after=()):
    group, width = n1.shape
    rows = group // 2
    half = width // 2

    def weight(which):
        return pl.BlockSpec((width, half), lambda i, m: (0, 2 * which + m[HALF]))

    out_shape = [jax.ShapeDtypeStruct((rows, width), F32), jax.ShapeDtypeStruct((rows, width), BF16)]
    for n in (48, 48, 64):
        out_shape += [jax.ShapeDtypeStruct((8, n, LANES), BF16)] * 2
    out = pl.pallas_call(
        without(qkv_back_kernel, 17, len(after)),
        grid_spec=pltpu.PrefetchScalarGridSpec(
            num_scalar_prefetch=1,
            grid=(1,),
            in_specs=[full(n1.shape)] + [full(a.shape) for a in grads] + [weight(0), weight(1), weight(2)]
            + [full(tok_mine.shape), full(tok_other.shape), full(early.shape)] + unread(len(after)),
            out_specs=[full(s.shape) for s in out_shape],
            scratch_shapes=[
                pltpu.VMEM((width, group), BF16), pltpu.VMEM((group, width), F32),
                pltpu.VMEM((width, half), F32), pltpu.VMEM((SMALL, width), F32),
            ],
        ),
        out_shape=out_shape,
        compiler_params=params(),
        name="qkv_back",
    )(meta, n1, *grads, w_qkv, w_qkv, w_qkv, tok_mine, tok_other, early, *after)
    return out[0], out[1], out[2::2], out[3::2]


def tail_kernel(tok, gres, dn_own, dn_got, gains, out):
    unit, rstd = norm_parts(tok[...].astype(F32))
    grad = dn_own[...] + dn_got[...].astype(F32)
    out[...] = (gres[...] + norm_back(grad, unit, rstd, gains[0:1, :])).astype(BF16)


def tail_call(tok, gres, dn_own, dn_got, gains, after=()):
    rows, width = tok.shape
    block = pl.BlockSpec((rows // 2, width), lambda i: (i, 0))
    return pl.pallas_call(
        without(tail_kernel, 5, len(after)),
        grid=(2,),
        in_specs=[block, block, block, block, pl.BlockSpec(gains.shape, lambda i: (0, 0))] + unread(len(after)),
        out_specs=block,
        out_shape=jax.ShapeDtypeStruct((rows, width), BF16),
        compiler_params=params(),
        name="tail",
    )(tok, gres, dn_own, dn_got, gains, *after)


def split_rows(meta, source, mine, send, at):
    own = pl.multiple_of(meta[HALF] * PART, 8)
    far = pl.multiple_of((1 - meta[HALF]) * PART, 8)
    mine[at] = source[pl.ds(own, PART), :]
    send[at] = source[pl.ds(far, PART), :]


def last_a_kernel(meta, k0, g0, k1, g1, k2, g2, down, mine, send, total):
    def add(keep, got, low, high):
        return keep[0, low:high, :].astype(F32) + got[0, low:high, :].astype(F32)

    sections = [(k0, g0, 0), (k0, g0, 48), (k0, g0, 96), (k1, g1, 0), (k2, g2, 96)]
    for at, (keep, got, low) in enumerate(sections):
        total[...] = add(keep, got, low, low + 48)
        split_rows(meta, total, mine, send, at)
    down[:, :LANES] = add(k1, g1, 48, 144)
    down[:, LANES:] = add(k2, g2, 0, 96)


def last_b_kernel(meta, k0, g0, k1, g1, k2, g2, mine, send, total):
    for at, (keep, got) in enumerate(((k0, g0), (k1, g1), (k2, g2))):
        total[...] = keep[0, :48, :].astype(F32) + got[0, :48, :].astype(F32)
        split_rows(meta, total, mine, send, at)
    small = k2[0, 48:, :].astype(F32) + got[0, 48:, :].astype(F32)
    total[...] = jnp.zeros_like(total)
    for i in range(3):
        total[16 * i : 16 * i + 16, :SMALL] = small[:, i * SMALL : (i + 1) * SMALL]
    split_rows(meta, total, mine, send, 3)


def join_a_kernel(meta, mine, got, up, out):
    for core in (0, 1):

        @pl.when(meta[HALF] == core)
        def _(core=core):
            for side, ref in ((core, mine), (1 - core, got)):
                for block in range(8):
                    at = (2 * block + side) * UNITS
                    low = (block % 2) * UNITS
                    up[:, at : at + UNITS] = ref[block // 2, :, low : low + UNITS]
                out[:, side * LANES : (side + 1) * LANES] = ref[4]


def join_b_kernel(meta, mine, got, qkv, little):
    for core in (0, 1):

        @pl.when(meta[HALF] == core)
        def _(core=core):
            for side, ref in ((core, mine), (1 - core, got)):
                for i in range(3):
                    at = (2 * i + side) * LANES
                    qkv[:, at : at + LANES] = ref[i]

    little[...] = (mine[3] + got[3])[:, :SMALL].T[:16, :]


def whole_call(kernel, name, meta, args, shapes, scratch=()):
    return pl.pallas_call(
        kernel,
        grid_spec=pltpu.PrefetchScalarGridSpec(
            num_scalar_prefetch=1,
            grid=(1,),
            in_specs=[full(a.shape) for a in args],
            out_specs=[full(s) for s in shapes],
            scratch_shapes=[pltpu.VMEM(s, F32) for s in scratch],
        ),
        out_shape=[jax.ShapeDtypeStruct(s, F32) for s in shapes],
        compiler_params=params(),
        name=name,
    )(meta, *args)


def paired(
    tokens, w_qkv, w_out, w_up, w_down, gains, biases, up_bias, image_cut, group_live, cotangent
):
    width = tokens.shape[1]
    half = width // 2
    core = lax.axis_index("dp") % 2
    me = (lax.axis_index("dp") * 2 + lax.axis_index("seq")).astype(jnp.int32)
    swap = [(i, (i & ~3) | ((i & 1) << 1) | ((i >> 1) & 1)) for i in range(COUNT)]

    def trade(value):
        return lax.ppermute(value, BOTH, swap)

    def across(value):
        return hop(value, CORE)

    tok = trade(tokens)
    tok_far = across(tok)
    bounds = trade(jnp.concatenate([image_cut, group_live]))
    cot = trade(cotangent)
    cot_far = across(cot)
    meta = jnp.concatenate([jnp.stack([me, core.astype(jnp.int32)]), bounds])
    blocks = up_bias.reshape(-1, 2, UNITS)
    own_bias = jnp.where(core == 0, blocks[:, 0], blocks[:, 1]).reshape(1, -1)

    n1, q, k, v = qkv_call(meta, tok, tok_far, w_qkv, gains, biases)
    o, lse = attend_call(meta, q, k, v)
    o_got = across(o)
    (res, block, block_send, dn, gub), keeps, sends = mid_call(
        meta, tok, tok_far, cot, cot_far, o, o_got, w_out, w_up, w_down, gains, biases, own_bias
    )
    dn_got = across(dn)
    got = hops(0, sends)
    block_got = across(block_send)
    live = core * tok.shape[0] + jnp.arange(tok.shape[0], dtype=jnp.int32)[:, None] < bounds[1]
    block_out = trade(jnp.where(live, block + block_got.astype(F32), 0.0).astype(BF16))
    gres, ga, small, out_keep, out_send = branch_call(meta, res, cot, cot_far, dn, dn_got, o, o_got, w_out, gains)
    out_got = hop(out_send, ORDERS[2][0])

    zero = jnp.zeros((width,), F32)
    rows = jnp.stack([zero, small[0], zero, small[1], zero, zero, small[2], small[3]])
    units = gub.reshape(-1, 1, UNITS)
    units = jnp.where(jnp.arange(2)[None, :, None] == core, units, 0.0)
    units = units.reshape(COUNT, 4, PART).transpose(0, 2, 1).reshape(width, 4)
    early = jnp.concatenate([rows.T, units, jnp.zeros((width, SMALL - 12), F32)], axis=1)

    grads = list(attend_back_call(meta, q, k, v, ga, o, lse, 0, 1))
    state = fold_call(
        [[(keeps[0], got[0])], [(keeps[1], got[1])], [(keeps[2], got[2]), (out_keep, out_got)]], grads[:1]
    )
    for step in (1, 2):
        got = hops(step, [send for _, send in state])
        grads += attend_back_call(meta, q, k, v, ga, o, lse, step, 1, [state[0][1]])
        state = fold_call([[(keep, g)] for (keep, _), g in zip(state, got)], grads[-1:])
    got = hops(3, [send for _, send in state])
    dn_own, dn_send, b_keeps, b_sends = qkv_back_call(
        meta, n1, grads, w_qkv, tok, tok_far, early, [state[0][1]]
    )
    b_got = hops(0, b_sends)
    dn_got = across(dn_send)
    width_ff = w_up.shape[1]
    last = [a for (keep, _), g in zip(state, got) for a in (keep, g)]
    grad_wdown, mine, send = whole_call(
        last_a_kernel, "last_a", meta, last, [(width_ff // COUNT, width), (5, PART, LANES), (5, PART, LANES)], [(48, LANES)]
    )
    a_got = across(send)
    grad_tokens = trade(tail_call(tok, gres, dn_own, dn_got, gains))
    grad_wup, grad_wout = whole_call(
        join_a_kernel, "join_a", meta, [mine, a_got], [(PART, width_ff), (PART, width)]
    )
    state = fold_call([[(keep, g)] for keep, g in zip(b_keeps, b_got)])
    for step in (1, 2):
        got = hops(step, [send for _, send in state])
        state = fold_call([[(keep, g)] for (keep, _), g in zip(state, got)])
    got = hops(3, [send for _, send in state])
    last = [a for (keep, _), g in zip(state, got) for a in (keep, g)]
    mine, send = whole_call(
        last_b_kernel, "last_b", meta, last, [(4, PART, LANES), (4, PART, LANES)], [(48, LANES)]
    )
    grad_qkv, little = whole_call(
        join_b_kernel, "join_b", meta, [mine, across(send)], [(PART, 3 * width), (16, PART)]
    )
    return (
        block_out, grad_tokens, grad_qkv, grad_wout, grad_wup, grad_wdown,
        little[0:2], little[2:8], little[8:12].reshape(-1),
    )


def norm_rows(values, gain, shift):
    center = values - jnp.mean(values, axis=-1, keepdims=True)
    spread = jnp.mean(center * center, axis=-1, keepdims=True)
    return center * lax.rsqrt(spread + EPSILON) * gain + shift


def split_heads(values):
    return values.reshape(values.shape[0], HEADS, -1).transpose(1, 0, 2)


def join_heads(values):
    return values.transpose(1, 0, 2).reshape(values.shape[1], -1)


def head_probs(query_head, key_head, mask):
    raw = jnp.einsum("qd,kd->qk", query_head, key_head, preferred_element_type=jnp.float32)
    return jax.nn.softmax(raw * 0.125 + mask, axis=-1)


def shards(
    tokens, w_qkv, w_out, w_up, w_down, gains, biases, up_bias, image_cut, group_live, cotangent
):
    rows_here = tokens.shape[0]
    width = tokens.shape[1]
    group = rows_here * lax.axis_size("seq")
    first_row = lax.axis_index("seq") * rows_here
    cut_row = image_cut[0]
    live_rows = group_live[0]
    key_pos = jnp.arange(group, dtype=jnp.int32)
    query_pos = first_row + jnp.arange(rows_here, dtype=jnp.int32)
    query_live = (query_pos < live_rows)[:, None]
    allowed = ((query_pos >= cut_row)[:, None] == (key_pos >= cut_row)[None, :]) & (
        key_pos < live_rows
    )[None, :]
    mask = jnp.where(allowed, 0.0, -1000000000.0).astype(jnp.float32)
    inputs = tokens.astype(jnp.float32)
    normed_one, norm_back_one = jax.vjp(norm_rows, inputs, gains[0], biases[0])
    normed_one = normed_one.astype(jnp.bfloat16)
    projected = jnp.dot(normed_one, w_qkv, preferred_element_type=jnp.float32)
    queries = (projected[:, :width] + biases[2]).astype(jnp.bfloat16)
    key_rows = projected[:, width : 2 * width].astype(jnp.bfloat16)
    value_rows = (projected[:, 2 * width :] + biases[3]).astype(jnp.bfloat16)
    kv_local = jnp.concatenate([key_rows, value_rows], axis=1)
    kv_whole = lax.all_gather(kv_local, "seq", axis=0, tiled=True)
    query_heads = split_heads(queries)

    def attend(operands):
        query_head, key_head, value_head = operands
        probs = head_probs(query_head, key_head, mask)
        return jnp.dot(probs.astype(jnp.bfloat16), value_head, preferred_element_type=jnp.float32)

    heads_out = lax.map(
        attend, (query_heads, split_heads(kv_whole[:, :width]), split_heads(kv_whole[:, width:]))
    )
    attended = join_heads(heads_out).astype(jnp.bfloat16)
    residual = inputs + jnp.dot(attended, w_out, preferred_element_type=jnp.float32) + biases[4]
    normed_two, norm_back_two = jax.vjp(norm_rows, residual, gains[1], biases[1])
    normed_two = normed_two.astype(jnp.bfloat16)
    hidden_pre = jnp.dot(normed_two, w_up, preferred_element_type=jnp.float32) + up_bias
    activated, gelu_back = jax.vjp(partial(jax.nn.gelu, approximate=False), hidden_pre)
    activated = activated.astype(jnp.bfloat16)
    mlp_out = jnp.dot(activated, w_down, preferred_element_type=jnp.float32) + biases[5]
    block_out = jnp.where(query_live, residual + mlp_out, 0.0).astype(jnp.bfloat16)
    grad_live = jnp.where(query_live, cotangent, jnp.zeros_like(cotangent))
    grad_wdown = jnp.einsum("rf,rd->fd", activated, grad_live, preferred_element_type=jnp.float32)
    grad_activated = jnp.einsum("rd,fd->rf", grad_live, w_down, preferred_element_type=jnp.float32)
    grad_hidden = gelu_back(grad_activated)[0].astype(jnp.bfloat16)
    grad_wup = jnp.einsum("rd,rf->df", normed_two, grad_hidden, preferred_element_type=jnp.float32)
    grad_normed_two = jnp.einsum("rf,df->rd", grad_hidden, w_up, preferred_element_type=jnp.float32)
    grad_res_norm, gain_two, shift_two = norm_back_two(grad_normed_two)
    grad_residual = grad_live.astype(jnp.float32) + grad_res_norm
    grad_branch = grad_residual.astype(jnp.bfloat16)
    grad_wout = jnp.einsum("rd,re->de", attended, grad_branch, preferred_element_type=jnp.float32)
    grad_attended = jnp.einsum(
        "re,de->rd", grad_branch, w_out, preferred_element_type=jnp.float32
    ).astype(jnp.bfloat16)

    def attend_back(operands):
        query_head, key_head, value_head, grad_head = operands
        probs = head_probs(query_head, key_head, mask)
        grad_probs = jnp.einsum(
            "qd,kd->qk", grad_head, value_head, preferred_element_type=jnp.float32
        )
        grad_scores = probs * (grad_probs - jnp.sum(probs * grad_probs, axis=-1, keepdims=True))
        grad_raw = (grad_scores * 0.125).astype(jnp.bfloat16)
        grad_query = jnp.dot(grad_raw, key_head, preferred_element_type=jnp.float32)
        grad_key = jnp.einsum("qk,qd->kd", grad_raw, query_head, preferred_element_type=jnp.float32)
        grad_value = jnp.einsum(
            "qk,qd->kd", probs.astype(jnp.bfloat16), grad_head, preferred_element_type=jnp.float32
        )
        return (grad_query, grad_key, grad_value)

    grad_q_heads, grad_k_heads, grad_v_heads = lax.map(
        attend_back,
        (
            query_heads,
            split_heads(kv_whole[:, :width]),
            split_heads(kv_whole[:, width:]),
            split_heads(grad_attended),
        ),
    )
    grad_queries = join_heads(grad_q_heads).astype(jnp.bfloat16)
    grad_kv_terms = jnp.concatenate([join_heads(grad_k_heads), join_heads(grad_v_heads)], axis=1)
    grad_kv = lax.psum_scatter(
        grad_kv_terms.astype(jnp.bfloat16), "seq", scatter_dimension=0, tiled=True
    )
    grad_projected = jnp.concatenate([grad_queries, grad_kv], axis=1)
    grad_wqkv = jnp.einsum(
        "rd,re->de", normed_one, grad_projected, preferred_element_type=jnp.float32
    )
    grad_normed_one = jnp.einsum(
        "re,de->rd", grad_projected, w_qkv, preferred_element_type=jnp.float32
    )
    grad_in_norm, gain_one, shift_one = norm_back_one(grad_normed_one)
    grad_tokens = (grad_residual + grad_in_norm).astype(jnp.bfloat16)
    grad_gains = jnp.stack([gain_one, gain_two])
    grad_biases = jnp.stack(
        [
            shift_one,
            shift_two,
            jnp.sum(grad_queries.astype(jnp.float32), axis=0),
            jnp.sum(grad_kv[:, width:].astype(jnp.float32), axis=0),
            jnp.sum(grad_branch.astype(jnp.float32), axis=0),
            jnp.sum(grad_live.astype(jnp.float32), axis=0),
        ]
    )
    grad_upbias = jnp.sum(grad_hidden.astype(jnp.float32), axis=0)
    summed = (
        lax.psum_scatter(grad_wqkv, ("dp", "seq"), scatter_dimension=0, tiled=True),
        lax.psum_scatter(grad_wout, ("dp", "seq"), scatter_dimension=0, tiled=True),
        lax.psum_scatter(grad_wup, ("dp", "seq"), scatter_dimension=0, tiled=True),
        lax.psum_scatter(grad_wdown, ("dp", "seq"), scatter_dimension=0, tiled=True),
        lax.psum_scatter(grad_gains, ("dp", "seq"), scatter_dimension=1, tiled=True),
        lax.psum_scatter(grad_biases, ("dp", "seq"), scatter_dimension=1, tiled=True),
        lax.psum_scatter(grad_upbias, ("dp", "seq"), scatter_dimension=0, tiled=True),
    )
    return (
        block_out,
        grad_tokens,
        summed[0],
        summed[1],
        summed[2],
        summed[3],
        summed[4],
        summed[5],
        summed[6],
    )


def solution(mesh):
    in_specs = (
        P(("dp", "seq"), None),
        P(),
        P(),
        P(),
        P(),
        P(),
        P(),
        P(),
        P("dp"),
        P("dp"),
        P(("dp", "seq"), None),
    )
    out_specs = (
        P(("dp", "seq"), None),
        P(("dp", "seq"), None),
        P(("dp", "seq"), None),
        P(("dp", "seq"), None),
        P(("dp", "seq"), None),
        P(("dp", "seq"), None),
        P(None, ("dp", "seq")),
        P(None, ("dp", "seq")),
        P(("dp", "seq")),
    )
    fits = mesh.shape["seq"] == 2 and mesh.shape["dp"] * 2 == COUNT
    return jax.shard_map(paired if fits else shards, mesh=mesh, in_specs=in_specs, out_specs=out_specs, check_vma=False)
```

```python
from functools import partial

import jax
import jax.numpy as jnp
from jax import lax
from jax.experimental import pallas as pl
from jax.experimental.pallas import tpu as pltpu
from jax.sharding import PartitionSpec as P

HEADS = 12
HEAD_DIM = 64
PAIR = 2 * HEAD_DIM
EPSILON = 1e-06
BOTH = ("dp", "seq")
FAR = -1000000000.0
F32 = jnp.float32
BF16 = jnp.bfloat16

ME, HALF, CUT, LIVE = 0, 1, 2, 3

NN = (((1,), (0,)), ((), ()))
NT = (((1,), (1,)), ((), ()))
TN = (((0,), (0,)), ((), ()))


def mm(a, b, dims=NN):
    return lax.dot_general(a, b, dims, preferred_element_type=F32)


def params(**more):
    return pltpu.CompilerParams(vmem_limit_bytes=56 * 1024 * 1024, **more)


def norm_parts(values):
    center = values - jnp.mean(values, axis=-1, keepdims=True)
    spread = jnp.mean(center * center, axis=-1, keepdims=True)
    rstd = lax.rsqrt(spread + EPSILON)
    return center * rstd, rstd


def norm_back(grad, unit, rstd, gain):
    scaled = grad * gain
    first = jnp.mean(scaled, axis=-1, keepdims=True)
    second = jnp.mean(scaled * unit, axis=-1, keepdims=True)
    return rstd * (scaled - first - unit * second)


SIDE_X, CORE, SIDE_Y, Z_NEAR, Z_FAR = 1, 2, 4, 8, 24
ORDERS = (
    (SIDE_X, SIDE_Y, Z_NEAR, Z_FAR), (SIDE_Y, Z_NEAR, SIDE_X, Z_FAR), (Z_NEAR, SIDE_X, SIDE_Y, Z_FAR),
)
PAIR_ORDERS = (
    (SIDE_Y, Z_NEAR, SIDE_X, Z_FAR), (SIDE_Y, SIDE_X, Z_NEAR, Z_FAR), (SIDE_Y, SIDE_X, Z_NEAR, Z_FAR),
)
COUNT = 32
LANES = 384
PART = 24


def hop(value, mask):
    return lax.ppermute(value, BOTH, [(i, i ^ mask) for i in range(COUNT)])


def places(masks):
    out = [0]
    for mask in masks:
        out = [value ^ (mask * bit) for value in out for bit in (0, 1)]
    return out


def without(kernel, first, count):
    def run(*refs):
        return kernel(*refs[:first], *refs[first + count :])

    return run


def unread(count):
    return [pl.BlockSpec(memory_space=pl.ANY)] * count


def fold_kernel(*refs, jobs):
    total = sum(terms for pieces, _ in jobs for _, terms in pieces)
    meta, parts, outs = refs[0], refs[1 : total + 1], refs[total + 1 :]
    at = 0
    used = 0
    lasts = []
    for pieces, sections in jobs:
        low = 0
        for rows, terms in pieces:
            for bit in (0, 1):
                both = sum(ref[bit].astype(F32) for ref in parts[at : at + terms])
                if sections is None:
                    outs[used + bit][:, low : low + rows, :] = both.astype(BF16)
                elif bit == 0:
                    stay = both[0]
                else:
                    lasts += [(stay[a : a + n], both[0, a : a + n], split) for a, n, split in sections]
            low += rows
            at += terms
        used += 2 * (sections is None)
    if lasts:
        keep, to_core, to_chip, to_both = outs[used:]
        first = meta[HALF] == 0
        place = 0
        for stay, leave, split in sorted(lasts, key=lambda entry: not entry[2]):
            rows = stay.shape[0]
            if split:
                rows //= 2
                for value, own, far in ((stay, keep, to_core), (leave, to_chip, to_both)):
                    low, high = value[:rows], value[rows:]
                    own[place : place + rows, :] = jnp.where(first, low, high).astype(own.dtype)
                    far[place : place + rows, :] = jnp.where(first, high, low).astype(BF16)
            else:
                keep[place : place + rows, :] = stay
                to_chip[place : place + rows, :] = leave.astype(BF16)
            place += rows


def fold_call(meta, jobs, after=()):
    parts = [a for pieces, _ in jobs for piece in pieces for a in piece]
    steps = min(a.shape[0] // 2 for a in parts)
    view = lambda a: a.reshape(2, a.shape[0] // 2, *a.shape[1:])
    spec = lambda a: pl.BlockSpec((2, a.shape[0] // 2 // steps, *a.shape[1:]), lambda i, m: (0, i, 0, 0))
    sizes = [([(piece[0].shape[1], len(piece)) for piece in pieces], sections) for pieces, sections in jobs]
    out_shape, out_specs, ends = [], [], []
    for pieces, sections in jobs:
        if sections is None:
            count = pieces[0][0].shape[0] // 2
            rows = sum(piece[0].shape[1] for piece in pieces)
            out_shape += [jax.ShapeDtypeStruct((count, rows, LANES), BF16)] * 2
            out_specs += [pl.BlockSpec((count // steps, rows, LANES), lambda i, m: (i, 0, 0))] * 2
        else:
            ends += sections
    if ends:
        split = sum(n // 2 for _, n, s in ends if s)
        plain = split + sum(n for _, n, s in ends if not s)
        for rows, kind in ((plain, F32), (split, BF16), (plain, BF16), (split, BF16)):
            out_shape.append(jax.ShapeDtypeStruct((rows, LANES), kind))
            out_specs.append(pl.BlockSpec((rows, LANES), lambda i, m: (0, 0)))
    out = pl.pallas_call(
        without(partial(fold_kernel, jobs=sizes), 1 + len(parts), len(after)),
        grid_spec=pltpu.PrefetchScalarGridSpec(
            num_scalar_prefetch=1,
            grid=(steps,),
            in_specs=[spec(a) for a in parts] + unread(len(after)),
            out_specs=out_specs,
        ),
        out_shape=out_shape,
        compiler_params=params(),
        name="fold",
    )(meta, *[view(a) for a in parts], *after)
    moving = sum(sections is None for _, sections in jobs)
    result = [(out[2 * i], out[2 * i + 1]) for i in range(moving)]
    return result + ([tuple(out[2 * moving :])] if ends else [])


def hops(step, sends):
    return [hop(send, masks[step]) for send, masks in zip(sends, ORDERS)]


def last_hop(ends):
    keep, to_core, to_chip, to_both = ends
    return keep, hop(to_core, CORE), hop(to_chip, Z_FAR), hop(to_both, Z_FAR ^ CORE)


def put_rows(source, me, masks, keep, send, low, col=0, at=None):
    cols = pl.ds(col, LANES)
    for bit, ref in ((0, keep), (1, send)):
        for place, value in enumerate(places(masks[1:])):
            chip = (me & ~CORE) ^ (value ^ (masks[0] * bit))
            first = pl.multiple_of(chip * PART, 8)
            second = pl.multiple_of((chip + CORE) * PART, 8)
            where = (lambda r: source[pl.ds(r, PART), cols]) if at is None else (lambda r: source[at, pl.ds(r, PART), cols])
            both = jnp.concatenate([where(first), where(second)], axis=0)
            ref[place, low : low + 2 * PART, :] = both.astype(BF16)


def qkv_kernel(meta, mine, other, wq, wk, wv, gains, biases, unit_ref, q_ref, k_ref, v_ref):
    step = pl.program_id(0)

    def run(ref):
        unit, _ = norm_parts(ref[...].astype(F32))
        normed = (unit * gains[0:1, :] + biases[0:1, :]).astype(BF16)
        unit_ref[...] = unit.astype(BF16).T
        half = q_ref.shape[1]
        first = pl.multiple_of(meta[HALF] * half, half)
        q_ref[...] = (mm(normed, wq[...]) + biases_at(biases, 2, first, half)).astype(BF16)
        k_ref[...] = mm(normed, wk[...]).astype(BF16)
        v_ref[...] = (mm(normed, wv[...]) + biases_at(biases, 3, first, half)).astype(BF16)

    @pl.when(step == 0)
    def _():
        run(mine)

    @pl.when(step == 1)
    def _():
        run(other)


def biases_at(biases, row, first, size):
    return biases[row : row + 1, pl.ds(first, size)]


def qkv_call(meta, mine, other, w_qkv, gains, biases):
    rows, width = mine.shape
    half = width // 2
    full = lambda shape: pl.BlockSpec(shape, lambda i, m: (0, 0))
    weight = lambda part: pl.BlockSpec((width, half), lambda i, m: (0, 2 * part + m[HALF]))
    out = lambda cols: pl.BlockSpec((rows, cols), lambda i, m: (i ^ m[HALF], 0))
    shape = lambda cols: jax.ShapeDtypeStruct((2 * rows, cols), BF16)
    return pl.pallas_call(
        qkv_kernel,
        grid_spec=pltpu.PrefetchScalarGridSpec(
            num_scalar_prefetch=1,
            grid=(2,),
            in_specs=[
                full((rows, width)), full((rows, width)), weight(0), weight(1), weight(2),
                full(gains.shape), full(biases.shape),
            ],
            out_specs=[
                pl.BlockSpec((width, rows), lambda i, m: (0, i ^ m[HALF])), out(half), out(half), out(half)
            ],
        ),
        out_shape=[jax.ShapeDtypeStruct((width, 2 * rows), BF16), shape(half), shape(half), shape(half)],
        compiler_params=params(),
        name="qkv",
    )(meta, mine, other, w_qkv, w_qkv, w_qkv, gains, biases)


TILE = 256


def lanes(rows):
    return lax.broadcasted_iota(jnp.int32, (rows, PAIR), 1)


def own_lanes(rows, head):
    return (lanes(rows) // HEAD_DIM) == head


def key_side(key_pair, head, meta):
    rows = key_pair.shape[0]
    at = lanes(rows) - (1 - head) * HEAD_DIM
    pos = lax.broadcasted_iota(jnp.int32, (rows, PAIR), 0)
    alive = pos < meta[LIVE]
    second = pos >= meta[CUT]
    in_first = alive & jnp.logical_not(second)
    in_second = alive & second
    extra = jnp.where(
        ((at == 0) & jnp.logical_not(in_first)) | ((at == 1) & jnp.logical_not(in_second)), FAR, 0.0
    )
    return jnp.where(own_lanes(rows, head), key_pair.astype(F32), extra).astype(BF16)


def query_side(query_pair, head, first_row, meta):
    rows = query_pair.shape[0]
    at = lanes(rows) - (1 - head) * HEAD_DIM
    second = first_row + lax.broadcasted_iota(jnp.int32, (rows, PAIR), 0) >= meta[CUT]
    extra = jnp.where(
        ((at == 0) & jnp.logical_not(second)) | ((at == 1) & second), 1.0, 0.0
    )
    return jnp.where(own_lanes(rows, head), query_pair.astype(F32) * 0.125, extra).astype(BF16)


def key_range(first_row, group, meta):
    cut = meta[CUT]
    live = meta[LIVE]
    only_first = first_row + TILE <= cut
    only_second = first_row >= cut
    low = jnp.where(only_second, cut, 0)
    high = jnp.where(only_first, cut, live)
    low = (low // 128) * 128
    steps = (high - low + (TILE - 1)) // TILE
    start = jnp.minimum(low, group - steps * TILE)
    return pl.multiple_of(start, 128), steps


def by_width(steps, group, body):
    for count in range(1, group // TILE + 1):

        @pl.when(steps == count)
        def _(count=count):
            body(count * TILE)


def attend_kernel(meta, q_ref, k_ref, v_ref, o_ref, lse_ref, kx_ref, vt_ref):
    rows = q_ref.shape[0]
    group = k_ref.shape[0]
    for head in (0, 1):
        kx_ref[head] = key_side(k_ref[...], head, meta)
    vt_ref[...] = v_ref[...].T

    def tile(index, carry):
        at = pl.multiple_of(index * TILE, TILE)
        first_row = at
        start, steps = key_range(first_row, group, meta)
        query = q_ref[pl.ds(at, TILE), :]

        def body(width):
            parts = []
            for head in (0, 1):
                qx = query_side(query, head, first_row, meta)
                scores = mm(kx_ref[head, pl.ds(start, width), :], qx, NT)
                top = jnp.max(scores, axis=0, keepdims=True)
                weight = jnp.exp(scores - top).astype(BF16)
                value = vt_ref[head * HEAD_DIM : (head + 1) * HEAD_DIM, pl.ds(start, width)]
                left = jnp.concatenate([value, jnp.ones((16, width), BF16)], axis=0)
                both = mm(left, weight)
                total = both[HEAD_DIM : HEAD_DIM + 1, :]
                parts.append(both[:HEAD_DIM, :] / total)
                lse_ref[0, head : head + 1, pl.ds(at, TILE)] = top + jnp.log(total)
            o_ref[pl.ds(at, TILE), :] = jnp.concatenate(parts, axis=0).T.astype(BF16)

        by_width(steps, group, body)
        return carry

    lax.fori_loop(0, rows // TILE, tile, 0)


def attend_call(meta, q, k, v):
    group, half = q.shape
    pairs = half // PAIR
    whole = pl.BlockSpec((group, PAIR), lambda p, m: (0, p))
    return pl.pallas_call(
        attend_kernel,
        grid_spec=pltpu.PrefetchScalarGridSpec(
            num_scalar_prefetch=1,
            grid=(pairs,),
            in_specs=[whole, whole, whole],
            out_specs=[whole, pl.BlockSpec((1, 2, group), lambda p, m: (p, 0, 0))],
            scratch_shapes=[pltpu.VMEM((2, group, PAIR), BF16), pltpu.VMEM((PAIR, group), BF16)],
        ),
        out_shape=[
            jax.ShapeDtypeStruct((group, half), BF16),
            jax.ShapeDtypeStruct((pairs, 2, group), F32),
        ],
        compiler_params=params(),
        name="attend",
    )(meta, q, k, v)


def attend_back_kernel(
    meta, q_ref, k_ref, v_ref, do_ref, o_ref, lse_ref, unit, wq, wk, wv, gains, biases, *refs, pair,
):
    *sums, dq_ref, dk_ref, dv_ref, keep, send, sum_ref, kx_ref, kt_ref, dk_acc, dv_acc, block = refs
    group = k_ref.shape[0]
    for head in (0, 1):
        kx_ref[head] = key_side(k_ref[...], head, meta)
    kt_ref[...] = k_ref[...].T
    dk_acc[...] = jnp.zeros_like(dk_acc)
    dv_acc[...] = jnp.zeros_like(dv_acc)

    def tile(index, carry):
        at = pl.multiple_of(index * TILE, TILE)
        first_row = at
        start, steps = key_range(first_row, group, meta)
        query = q_ref[pl.ds(first_row, TILE), :]
        grad = do_ref[pl.ds(at, TILE), :]
        dots = (grad.astype(F32) * o_ref[pl.ds(at, TILE), :].astype(F32)).T

        def body(width):
            probs, raws, masked_grads, masked_queries, dqs = [], [], [], [], []
            for head in (0, 1):
                mine = own_lanes(TILE, head)
                qx = query_side(query, head, first_row, meta)
                dox = jnp.where(mine, grad, jnp.zeros_like(grad))
                scores = mm(kx_ref[head, pl.ds(start, width), :], qx, NT)
                prob = jnp.exp(scores - lse_ref[0, head : head + 1, pl.ds(at, TILE)])
                gprob = mm(v_ref[pl.ds(start, width), :], dox, NT)
                delta = jnp.sum(dots[head * HEAD_DIM : (head + 1) * HEAD_DIM, :], axis=0, keepdims=True)
                raw = (prob * (gprob - delta)).astype(BF16)
                keys_t = kt_ref[head * HEAD_DIM : (head + 1) * HEAD_DIM, pl.ds(start, width)]
                dqs.append(mm(keys_t, raw))
                probs.append(prob.astype(BF16))
                raws.append(raw)
                masked_grads.append(dox)
                masked_queries.append(jnp.where(mine, query * jnp.asarray(0.125, BF16), jnp.zeros_like(query)))
            dv_acc[pl.ds(start, width), :] += mm(
                jnp.concatenate(probs, axis=1), jnp.concatenate(masked_grads, axis=0)
            )
            dk_acc[pl.ds(start, width), :] += mm(
                jnp.concatenate(raws, axis=1), jnp.concatenate(masked_queries, axis=0)
            )
            dq = jnp.concatenate(dqs, axis=0).T * 0.125
            dq_ref[pl.ds(first_row, TILE), :] = dq.astype(BF16)

        by_width(steps, group, body)
        return carry

    lax.fori_loop(0, group // TILE, tile, 0)
    dk_ref[...] = dk_acc[...].astype(BF16)
    dv_ref[...] = dv_acc[...].astype(BF16)
    grads = jnp.concatenate([dq_ref[...], dk_ref[...], dv_ref[...]], axis=1)
    total = jnp.sum(grads.astype(F32), axis=0, keepdims=True)
    product = mm(unit[...], grads)
    column = lambda row: jnp.broadcast_to(row, (PAIR, row.shape[1])).T[:, :1]
    gain, shift = column(gains[0:1, :]), column(biases[0:1, :])
    block[...] = product * gain + total * shift
    weight = jnp.concatenate([wq[...], wk[...], wv[...]], axis=1).astype(F32)
    lane = lax.broadcasted_iota(jnp.int32, sum_ref.shape, 1)
    sum_ref[...] = (
        sum((ref[...] for ref in sums), jnp.zeros(sum_ref.shape, F32))
        + jnp.where(lane == 0, jnp.sum(weight * product, axis=1, keepdims=True), 0.0)
        + jnp.where(lane == 2, jnp.sum(weight * total, axis=1, keepdims=True), 0.0)
    )
    here = pl.ds(pl.multiple_of(meta[HALF] * LANES + pair * PAIR, PAIR), PAIR)
    lane = lax.broadcasted_iota(jnp.int32, (PAIR, PAIR), 1)
    for column, part in ((4, total[:, :PAIR]), (5, total[:, 2 * PAIR :])):
        sum_ref[here, :] += jnp.where(lane == column, jnp.broadcast_to(part, (PAIR, PAIR)).T, 0.0)
    put_rows(block, meta[ME], PAIR_ORDERS[pair], keep, send, 0)
    if pair == 2:
        put_sums(sum_ref, meta[ME], PAIR_ORDERS[pair], keep, send, 2 * PART)


SMALL = 128


def put_sums(source, me, masks, keep, send, low):
    for bit, ref in ((0, keep), (1, send)):
        for place, value in enumerate(places(masks[1:])):
            chip = (me & ~CORE) ^ (value ^ (masks[0] * bit))
            both = [
                jnp.concatenate([source[pl.ds(pl.multiple_of((chip + c) * PART + 8 * i, 8), 8), :] for i in range(3)], axis=1)
                for c in (0, CORE)
            ]
            ref[place, low : low + 16, :] = jnp.concatenate(both, axis=0).astype(BF16)


def attend_back_call(meta, q, k, v, grad, o, lse, unit, w_qkv, gains, biases, sums, pair, after=()):
    group, half = q.shape
    width = unit.shape[0]
    pairs = half // PAIR
    whole = pl.BlockSpec((group, PAIR), lambda i, m: (0, pair))

    def weight(which):
        return pl.BlockSpec((width, PAIR), lambda i, m: (0, 2 * pairs * which + pairs * m[HALF] + pair))

    rows = 2 * PART + 16 * (pair == 2)
    out_shape = [jax.ShapeDtypeStruct((group, PAIR), BF16)] * 3
    out_shape += [jax.ShapeDtypeStruct((8, rows, LANES), BF16)] * 2 + [jax.ShapeDtypeStruct((width, SMALL), F32)]
    return pl.pallas_call(
        without(partial(attend_back_kernel, pair=pair), 13 + len(sums), len(after)),
        grid_spec=pltpu.PrefetchScalarGridSpec(
            num_scalar_prefetch=1,
            grid=(1,),
            in_specs=[whole] * 5
            + [pl.BlockSpec((1, 2, group), lambda i, m: (pair, 0, 0)), full(unit.shape), weight(0), weight(1), weight(2)]
            + [full(a.shape) for a in (gains, biases, *sums)] + unread(len(after)),
            out_specs=[full(a.shape) for a in out_shape],
            scratch_shapes=[
                pltpu.VMEM((2, group, PAIR), BF16),
                pltpu.VMEM((PAIR, group), BF16),
                pltpu.VMEM((group, PAIR), F32),
                pltpu.VMEM((group, PAIR), F32),
                pltpu.VMEM((width, LANES), F32),
            ],
        ),
        out_shape=out_shape,
        compiler_params=params(),
        name="attend_back",
    )(meta, q, k, v, grad, o, lse, unit, w_qkv, w_qkv, w_qkv, gains, biases, *sums, *after)


UNITS = 192
STEPS = 2
ROWS = 256

ERF_TOP = (0.00022905065861350646, 0.0034082910107109506, 0.050955695062380861, 0.18520832239976145, 1.128379143519084)
ERF_LOW = (
    -1.1791602954361697e-7, 0.000023547966471313185, 0.0010179625278914885, 0.014070470171167667,
    0.11098505178285362, 0.49746925110067538, 1.0,
)


def erf(x):
    x = jnp.clip(x, -3.832506856900711, 3.832506856900711)
    square = x * x
    top = jnp.full_like(x, ERF_TOP[0])
    for c in ERF_TOP[1:]:
        top = top * square + c
    low = jnp.full_like(x, ERF_LOW[0])
    for c in ERF_LOW[1:]:
        low = low * square + c
    return x * top / low


def mid_kernel(
    meta, tok_mine, tok_other, cot_mine, cot_other, a_own, a_got, w_out, w_up, w_down, gains, biases, up_bias,
    res_ref, block_ref, block_send, dn_ref, gub_ref, k0, s0, k1, s1, k2, s2,
    n2, n2t, gl, act, gh, wu, up_acc, down_acc, out_acc, dn_acc,
):
    step = pl.program_id(0)
    rows, width = tok_mine.shape
    half = a_own.shape[1]
    chunk = wu.shape[1]
    me = meta[ME]
    own = pl.multiple_of(meta[HALF] * half, half)
    far = pl.multiple_of((1 - meta[HALF]) * half, half)
    mine = pl.multiple_of(meta[HALF] * rows, rows)
    other = pl.multiple_of((1 - meta[HALF]) * rows, rows)

    @pl.when(step == 0)
    def _():
        for place, tok, cot in ((mine, tok_mine, cot_mine), (other, tok_other, cot_other)):
            for low in range(0, rows, ROWS):
                at = pl.ds(pl.multiple_of(place + low, ROWS), ROWS)
                residual = (
                    tok[low : low + ROWS, :].astype(F32)
                    + mm(a_own[at, :], w_out[pl.ds(own, half), :])
                    + mm(a_got[at, :], w_out[pl.ds(far, half), :])
                    + biases[4:5, :]
                )
                res_ref[at, :] = residual
                unit, _ = norm_parts(residual)
                n2[at, :] = (unit * gains[1:2, :] + biases[1:2, :]).astype(BF16)
                live = place + low + lax.broadcasted_iota(jnp.int32, (ROWS, 1), 0) < meta[LIVE]
                cots = cot[low : low + ROWS, :]
                gl[at, :] = jnp.where(live, cots, jnp.zeros_like(cots))
        n2t[...] = n2[...].T

    for core in (0, 1):

        @pl.when(meta[HALF] == core)
        def _(core=core):
            for block in range(chunk // UNITS):
                at = (2 * block + core) * UNITS
                wu[:, block * UNITS : (block + 1) * UNITS] = w_up[:, at : at + UNITS]

    wd = w_down[...].reshape(chunk, width)
    gub = jnp.zeros((1, chunk), F32)
    for low in range(0, 2 * rows, ROWS):
        at = slice(low, low + ROWS)
        hidden = mm(n2[at, :], wu[...]) + up_bias[...]
        gact = mm(gl[at, :], wd, NT)
        cdf = 0.5 * (1.0 + erf(hidden * 0.7071067811865476))
        pdf = jnp.exp(-0.5 * hidden * hidden) * 0.3989422804014327
        active = (hidden * cdf).astype(BF16)
        grad_hidden = gact * (cdf + hidden * pdf)
        gub += jnp.sum(grad_hidden, axis=0, keepdims=True)
        grad_hidden = grad_hidden.astype(BF16)
        act[at, :] = active
        gh[at, :] = grad_hidden
        out_acc[at, :] = jnp.where(step == 0, 0.0, out_acc[at, :]) + mm(active, wd)
        dn_acc[at, :] = jnp.where(step == 0, 0.0, dn_acc[at, :]) + mm(grad_hidden, wu[...], NT)
    gub_ref[...] = gub
    down_acc[pl.ds(pl.multiple_of(step * chunk, chunk), chunk), :] = mm(act[...], gl[...], TN).astype(BF16)
    up_acc[step] = mm(n2t[...], gh[...])

    @pl.when(step == STEPS - 1)
    def _():
        pos = lax.broadcasted_iota(jnp.int32, (rows, 1), 0)
        at = pl.ds(mine, rows)
        block_ref[...] = jnp.where(
            mine + pos < meta[LIVE], res_ref[at, :] + out_acc[at, :] + biases[5:6, :], 0.0
        )
        block_send[...] = jnp.where(other + pos < meta[LIVE], out_acc[pl.ds(other, rows), :], 0.0).astype(BF16)
        dn_ref[...] = dn_acc[...].astype(BF16)
        for block, (keep, send, masks, low) in enumerate(
            ((k0, s0, ORDERS[0], 0), (k0, s0, ORDERS[0], 48), (k0, s0, ORDERS[0], 96), (k1, s1, ORDERS[1], 0))
        ):
            put_rows(up_acc, me, masks, keep, send, low, (block % 2) * LANES, block // 2)
        for col, (keep, send, masks, low) in enumerate(((k1, s1, ORDERS[1], 48), (k2, s2, ORDERS[2], 0))):
            for bit, ref in ((0, keep), (1, send)):
                for place, value in enumerate(places(masks[1:])):
                    chip = me ^ (value ^ (masks[0] * bit))
                    first = pl.multiple_of((chip // 4) * UNITS + (chip & 1) * (UNITS // 2), UNITS // 2)
                    ref[place, low : low + UNITS // 2, :] = down_acc[
                        pl.ds(first, UNITS // 2), col * LANES : (col + 1) * LANES
                    ]


def full(shape):
    return pl.BlockSpec(shape, lambda *a: (0,) * len(shape))


def once(shape):
    return pl.BlockSpec(shape, lambda *a: (0,) * len(shape), pipeline_mode=pl.Buffered(1))


def mid_call(meta, tok_mine, tok_other, cot_mine, cot_other, a_own, a_got, w_out, w_up, w_down, gains, biases, up_bias):
    rows, width = tok_mine.shape
    ff = w_up.shape[1]
    chunk = ff // 2 // STEPS
    blocks = chunk // UNITS
    group = 2 * rows
    stream = [144, 144, 144, 144, 96, 96]
    out_shape = [
        jax.ShapeDtypeStruct((group, width), F32), jax.ShapeDtypeStruct((rows, width), F32),
        jax.ShapeDtypeStruct((rows, width), BF16), jax.ShapeDtypeStruct((group, width), BF16),
        jax.ShapeDtypeStruct((1, ff // 2), F32),
    ] + [jax.ShapeDtypeStruct((8, n, LANES), BF16) for n in stream]
    out_specs = [once(s.shape) for s in out_shape]
    out_specs[4] = pl.BlockSpec((1, chunk), lambda i, m: (0, i))
    out = pl.pallas_call(
        mid_kernel,
        grid_spec=pltpu.PrefetchScalarGridSpec(
            num_scalar_prefetch=1,
            grid=(STEPS,),
            in_specs=[
                once((rows, width)), once((rows, width)), once((rows, width)), once((rows, width)),
                once(a_own.shape), once(a_got.shape), once(w_out.shape),
                pl.BlockSpec((width, 2 * chunk), lambda i, m: (0, i)),
                pl.BlockSpec((blocks, 1, UNITS, width), lambda i, m: (i, m[HALF], 0, 0)),
                full(gains.shape), full(biases.shape),
                pl.BlockSpec((1, chunk), lambda i, m: (0, i)),
            ],
            out_specs=out_specs,
            scratch_shapes=[
                pltpu.VMEM((group, width), BF16), pltpu.VMEM((width, group), BF16), pltpu.VMEM((group, width), BF16),
                pltpu.VMEM((group, chunk), BF16), pltpu.VMEM((group, chunk), BF16), pltpu.VMEM((width, chunk), BF16),
                pltpu.VMEM((STEPS, width, chunk), F32), pltpu.VMEM((ff // 2, width), BF16),
                pltpu.VMEM((group, width), F32), pltpu.VMEM((group, width), F32),
            ],
        ),
        out_shape=out_shape,
        compiler_params=params(),
        name="mid",
    )(
        meta, tok_mine, tok_other, cot_mine, cot_other, a_own, a_got, w_out, w_up,
        w_down.reshape(ff // UNITS // 2, 2, UNITS, width), gains, biases, up_bias,
    )
    return out[:5], out[5::2], out[6::2]


def branch_kernel(
    meta, res, cot_mine, cot_other, dn_own, dn_got, a_own, a_got, w_out, gains,
    gres_ref, ga_ref, small_ref, keep, send, gb, whole,
):
    rows, width = cot_mine.shape
    half = a_own.shape[1]
    own = pl.multiple_of(meta[HALF] * half, half)
    far = pl.multiple_of((1 - meta[HALF]) * half, half)
    mine = pl.multiple_of(meta[HALF] * rows, rows)
    other = pl.multiple_of((1 - meta[HALF]) * rows, rows)
    small = jnp.zeros((4, width), F32)
    for place, cot in ((mine, cot_mine), (other, cot_other)):
        for low in range(0, rows, ROWS):
            at = pl.ds(pl.multiple_of(place + low, ROWS), ROWS)
            unit, rstd = norm_parts(res[at, :])
            grad = dn_own[at, :].astype(F32) + dn_got[at, :].astype(F32)
            live = place + low + lax.broadcasted_iota(jnp.int32, (ROWS, 1), 0) < meta[LIVE]
            gl = jnp.where(live, cot[low : low + ROWS, :].astype(F32), 0.0)
            gres = gl + norm_back(grad, unit, rstd, gains[1:2, :])
            branch = gres.astype(BF16)
            gb[at, :] = branch
            if cot is cot_mine:
                gres_ref[low : low + ROWS, :] = gres
                small += jnp.concatenate(
                    [jnp.sum(a, axis=0, keepdims=True) for a in (grad * unit, grad, branch.astype(F32), gl)], axis=0
                )
    small_ref[0:4, :] = small
    small_ref[4:8, :] = jnp.zeros((4, width), F32)
    ga_ref[...] = mm(gb[...], w_out[pl.ds(own, half), :], NT).astype(BF16)
    part = gb[:, pl.ds(own, half)]
    whole[pl.ds(own, half), :] = mm(a_own[...], part, TN)
    whole[pl.ds(far, half), :] = mm(a_got[...], part, TN)
    put_rows(whole, meta[ME], ORDERS[2], keep, send, 0)


def branch_call(meta, res, cot_mine, cot_other, dn_own, dn_got, a_own, a_got, w_out, gains):
    rows, width = cot_mine.shape
    group, half = a_own.shape
    args = (res, cot_mine, cot_other, dn_own, dn_got, a_own, a_got, w_out, gains)
    out_shape = [
        jax.ShapeDtypeStruct((rows, width), F32), jax.ShapeDtypeStruct((group, half), BF16),
        jax.ShapeDtypeStruct((8, width), F32),
    ] + [jax.ShapeDtypeStruct((8, 2 * PART, LANES), BF16)] * 2
    return pl.pallas_call(
        branch_kernel,
        grid_spec=pltpu.PrefetchScalarGridSpec(
            num_scalar_prefetch=1,
            grid=(1,),
            in_specs=[full(a.shape) for a in args],
            out_specs=[full(a.shape) for a in out_shape],
            scratch_shapes=[pltpu.VMEM((group, width), BF16), pltpu.VMEM((width, half), F32)],
        ),
        out_shape=out_shape,
        compiler_params=params(),
        name="branch",
    )(meta, *args)


def qkv_back_kernel(meta, d0, d1, d2, d3, d4, d5, d6, d7, d8, wq, wk, wv, dn_own, dn_send):
    rows = dn_own.shape[0]
    for ref, half in ((dn_send, 1 - meta[HALF]), (dn_own, meta[HALF])):
        at = pl.ds(pl.multiple_of(half * rows, rows), rows)
        total = 0.0
        for parts, weight in (((d0, d3, d6), wq), ((d1, d4, d7), wk), ((d2, d5, d8), wv)):
            total += mm(jnp.concatenate([a[at, :] for a in parts], axis=1), weight[...], NT)
        ref[...] = total.astype(ref.dtype)


def qkv_back_call(meta, grads, w_qkv, after=()):
    group = grads[0].shape[0]
    width = w_qkv.shape[0]
    half = width // 2

    def weight(which):
        return pl.BlockSpec((width, half), lambda i, m: (0, 2 * which + m[HALF]))

    out_shape = [jax.ShapeDtypeStruct((group // 2, width), kind) for kind in (F32, BF16)]
    return pl.pallas_call(
        without(qkv_back_kernel, 13, len(after)),
        grid_spec=pltpu.PrefetchScalarGridSpec(
            num_scalar_prefetch=1,
            grid=(1,),
            in_specs=[full(a.shape) for a in grads] + [weight(0), weight(1), weight(2)] + unread(len(after)),
            out_specs=[full(a.shape) for a in out_shape],
        ),
        out_shape=out_shape,
        compiler_params=params(),
        name="qkv_back",
    )(meta, *grads, w_qkv, w_qkv, w_qkv, *after)


def tail_kernel(tok, gres, dn_own, dn_got, gains, out):
    unit, rstd = norm_parts(tok[...].astype(F32))
    grad = dn_own[...] + dn_got[...].astype(F32)
    out[...] = (gres[...] + norm_back(grad, unit, rstd, gains[0:1, :])).astype(BF16)


def tail_call(tok, gres, dn_own, dn_got, gains, after=()):
    rows, width = tok.shape
    block = pl.BlockSpec((rows // 2, width), lambda i: (i, 0))
    return pl.pallas_call(
        without(tail_kernel, 5, len(after)),
        grid=(2,),
        in_specs=[block, block, block, block, pl.BlockSpec(gains.shape, lambda i: (0, 0))] + unread(len(after)),
        out_specs=block,
        out_shape=jax.ShapeDtypeStruct((rows, width), BF16),
        compiler_params=params(),
        name="tail",
    )(tok, gres, dn_own, dn_got, gains, *after)


A_SECTIONS = (
    [(0, 48, True), (48, 48, True), (96, 48, True)], [(0, 48, True), (48, 96, False)], [(0, 96, False), (96, 48, True)],
)


def join_a_kernel(meta, keep, from_core, from_chip, from_both, up, out, down, own, far):
    split = from_core.shape[0]
    own[...] = keep[...] + from_chip[...].astype(F32)
    far[...] = from_core[...].astype(F32) + from_both[...].astype(F32)
    down[:, :LANES] = own[split : split + 4 * PART, :]
    down[:, LANES:] = own[split + 4 * PART :, :]
    for core in (0, 1):

        @pl.when(meta[HALF] == core)
        def _(core=core):
            for side, ref in ((core, own), (1 - core, far)):
                for block in range(8):
                    at = (2 * block + side) * UNITS
                    low = (block % 2) * UNITS
                    row = (block // 2) * PART
                    up[:, at : at + UNITS] = ref[row : row + PART, low : low + UNITS]
                out[:, side * LANES : (side + 1) * LANES] = ref[4 * PART : 5 * PART, :]


def join_b_kernel(meta, k0, r0, c0, b0, k1, r1, c1, b1, qkv, gain, bias, up_bias):
    own = [k[...] + c[...].astype(F32) for k, c in ((k0, c0), (k1, c1))]
    far = [r[...].astype(F32) + b[...].astype(F32) for r, b in ((r0, b0), (r1, b1))]
    pick = lambda side: [side[0][:PART], side[0][PART:], side[1][:PART]]
    for core in (0, 1):

        @pl.when(meta[HALF] == core)
        def _(core=core):
            for side, value in ((core, own), (1 - core, far)):
                for pair, part in enumerate(pick(value)):
                    for i in range(3):
                        at = (2 * i + side) * LANES + pair * PAIR
                        qkv[:, at : at + PAIR] = part[:, i * PAIR : (i + 1) * PAIR]

    small = own[1][PART:] + far[1][PART:]
    turned = jnp.concatenate([small[:, i * SMALL : (i + 1) * SMALL] for i in range(3)], axis=0).T
    gain[...] = turned[0:2]
    bias[...] = turned[2:8]
    up_bias[...] = jnp.concatenate([turned[8 + i : 9 + i] for i in range(4)], axis=1)


def whole_call(kernel, name, meta, args, shapes, scratch=(), after=()):
    return pl.pallas_call(
        without(kernel, 1 + len(args), len(after)),
        grid_spec=pltpu.PrefetchScalarGridSpec(
            num_scalar_prefetch=1,
            grid=(1,),
            in_specs=[full(a.shape) for a in args] + unread(len(after)),
            out_specs=[full(s) for s in shapes],
            scratch_shapes=[pltpu.VMEM(s, F32) for s in scratch],
        ),
        out_shape=[jax.ShapeDtypeStruct(s, F32) for s in shapes],
        compiler_params=params(),
        name=name,
    )(meta, *args, *after)


def paired(
    tokens, w_qkv, w_out, w_up, w_down, gains, biases, up_bias, image_cut, group_live, cotangent
):
    width = tokens.shape[1]
    half = width // 2
    width_ff = w_up.shape[1]
    core = lax.axis_index("dp") % 2
    me = (lax.axis_index("dp") * 2 + lax.axis_index("seq")).astype(jnp.int32)
    swap = [(i, (i & ~3) | ((i & 1) << 1) | ((i >> 1) & 1)) for i in range(COUNT)]

    def trade(value):
        return lax.ppermute(value, BOTH, swap)

    def across(value):
        return hop(value, CORE)

    tok = trade(tokens)
    own_bounds = jnp.concatenate([image_cut, group_live])
    bounds = jnp.where(core == lax.axis_index("seq"), own_bounds, across(own_bounds))
    tok_far = across(tok)
    meta = jnp.concatenate([jnp.stack([me, core.astype(jnp.int32)]), bounds])
    cot_here, tok_far, meta = lax.optimization_barrier((cotangent, tok_far, meta))
    cot = trade(cot_here)
    blocks = up_bias.reshape(-1, 2, UNITS)
    own_bias = jnp.where(core == 0, blocks[:, 0], blocks[:, 1]).reshape(1, -1)

    unit, q, k, v = qkv_call(meta, tok, tok_far, w_qkv, gains, biases)
    o, lse = attend_call(meta, q, k, v)
    o_got = across(o)
    cot_far = across(lax.optimization_barrier((cot, o))[0])
    (res, block, block_send, dn, gub), keeps, sends = mid_call(
        meta, tok, tok_far, cot, cot_far, o, o_got, w_out, w_up, w_down, gains, biases, own_bias
    )
    dn_got = across(dn)
    a_got = hops(0, sends)
    block_got = across(block_send)
    block_out = trade((block + block_got.astype(F32)).astype(BF16))
    gres, ga, small, out_keep, out_send = branch_call(meta, res, cot, cot_far, dn, dn_got, o, o_got, w_out, gains)
    out_got = hop(out_send, ORDERS[2][0])

    zero = jnp.zeros((width,), F32)
    rows = jnp.stack([zero, small[0], zero, small[1], zero, zero, small[2], small[3]])
    units = gub.reshape(-1, 1, UNITS)
    units = jnp.where(jnp.arange(2)[None, :, None] == core, units, 0.0)
    units = units.reshape(COUNT, 4, PART).transpose(0, 2, 1).reshape(width, 4)
    early = jnp.concatenate([rows.T, units, jnp.zeros((width, SMALL - 12), F32)], axis=1)

    def pair_hop(pair, step, send):
        return hop(send, PAIR_ORDERS[pair][step])

    def tied(value, to):
        return lax.optimization_barrier((value, to))[0]

    *grads, b0, b0_send, sums = attend_back_call(meta, q, k, v, ga, o, lse, unit, w_qkv, gains, biases, [], 0)
    a0, a1, a2 = fold_call(
        meta,
        [
            ([(keeps[0], a_got[0])], None), ([(keeps[1], a_got[1])], None),
            ([(keeps[2], a_got[2]), (out_keep, out_got)], None),
        ],
        [b0_send],
    )
    a_got = hops(1, [a0[1], a1[1], a2[1]])
    b0_got = pair_hop(0, 0, tied(b0_send, a0[1]))
    *more, b1, b1_send, sums = attend_back_call(meta, q, k, v, ga, o, lse, unit, w_qkv, gains, biases, [sums], 1, [a0[1]])
    grads = grads + more
    a0, a1, a2, p0 = fold_call(
        meta,
        [([(a[0], g)], None) for a, g in zip((a0, a1, a2), a_got)] + [([(b0, b0_got)], None)],
        [b1_send],
    )
    a_got = hops(2, [a0[1], a1[1], a2[1]])
    p0_got = pair_hop(0, 1, p0[1])
    b1_got = pair_hop(1, 0, tied(b1_send, p0[1]))
    *more, b2, b2_send, _ = attend_back_call(meta, q, k, v, ga, o, lse, unit, w_qkv, gains, biases, [sums, early], 2, [a0[1]])
    grads = grads + more
    p0, p1, a_end = fold_call(
        meta,
        [([(p0[0], p0_got)], None), ([(b1, b1_got)], None)]
        + [([(a[0], g)], sections) for a, g, sections in zip((a0, a1, a2), a_got, A_SECTIONS)],
        [b2_send, block_out],
    )
    p0_got, p1_got = pair_hop(0, 2, p0[1]), pair_hop(1, 1, p1[1])
    b2_got = pair_hop(2, 0, tied(b2_send, p1[1]))
    a_end = last_hop(a_end)
    dn_own, dn_send = qkv_back_call(meta, grads, w_qkv, [p1[1]])
    p1, p2 = fold_call(meta, [([(p1[0], p1_got)], None), ([(b2, b2_got)], None)], [dn_own, *a_end[1:]])
    p1_got, p2_got = pair_hop(1, 2, p1[1]), pair_hop(2, 1, p2[1])
    dn_got = across(tied(dn_send, p2[1]))
    mine = tail_call(tok, gres, dn_own, dn_got, gains, [p2[1]])
    half_cut = [(0, 48, True)]
    p2, b_end = fold_call(
        meta,
        [([(p2[0], p2_got)], None), ([(p0[0], p0_got)], half_cut), ([(p1[0], p1_got)], half_cut)],
        [mine],
    )
    p2_got = pair_hop(2, 2, p2[1])
    grad_tokens = trade(tied(mine, p2[1]))
    b_end = last_hop(b_end)
    grad_wup, grad_wout, grad_wdown = whole_call(
        join_a_kernel, "join_a", meta, a_end, [(PART, width_ff), (PART, width), (4 * PART, width)],
        [a_end[0].shape, a_end[1].shape], [p2[1]],
    )
    (c_end,) = fold_call(meta, [([(p2[0], p2_got)], [(0, 48, True), (48, 16, True)])], [grad_wdown])
    c_end = last_hop(c_end)
    grad_qkv, grad_gains, grad_biases, grad_upbias = whole_call(
        join_b_kernel, "join_b", meta, [*b_end, *c_end], [(PART, 3 * width), (2, PART), (6, PART), (1, 4 * PART)]
    )
    return (
        block_out, grad_tokens, grad_qkv, grad_wout, grad_wup, grad_wdown, grad_gains, grad_biases,
        grad_upbias.reshape(-1),
    )


def norm_rows(values, gain, shift):
    center = values - jnp.mean(values, axis=-1, keepdims=True)
    spread = jnp.mean(center * center, axis=-1, keepdims=True)
    return center * lax.rsqrt(spread + EPSILON) * gain + shift


def split_heads(values):
    return values.reshape(values.shape[0], HEADS, -1).transpose(1, 0, 2)


def join_heads(values):
    return values.transpose(1, 0, 2).reshape(values.shape[1], -1)


def head_probs(query_head, key_head, mask):
    raw = jnp.einsum("qd,kd->qk", query_head, key_head, preferred_element_type=jnp.float32)
    return jax.nn.softmax(raw * 0.125 + mask, axis=-1)


def shards(
    tokens, w_qkv, w_out, w_up, w_down, gains, biases, up_bias, image_cut, group_live, cotangent
):
    rows_here = tokens.shape[0]
    width = tokens.shape[1]
    group = rows_here * lax.axis_size("seq")
    first_row = lax.axis_index("seq") * rows_here
    cut_row = image_cut[0]
    live_rows = group_live[0]
    key_pos = jnp.arange(group, dtype=jnp.int32)
    query_pos = first_row + jnp.arange(rows_here, dtype=jnp.int32)
    query_live = (query_pos < live_rows)[:, None]
    allowed = ((query_pos >= cut_row)[:, None] == (key_pos >= cut_row)[None, :]) & (
        key_pos < live_rows
    )[None, :]
    mask = jnp.where(allowed, 0.0, -1000000000.0).astype(jnp.float32)
    inputs = tokens.astype(jnp.float32)
    normed_one, norm_back_one = jax.vjp(norm_rows, inputs, gains[0], biases[0])
    normed_one = normed_one.astype(jnp.bfloat16)
    projected = jnp.dot(normed_one, w_qkv, preferred_element_type=jnp.float32)
    queries = (projected[:, :width] + biases[2]).astype(jnp.bfloat16)
    key_rows = projected[:, width : 2 * width].astype(jnp.bfloat16)
    value_rows = (projected[:, 2 * width :] + biases[3]).astype(jnp.bfloat16)
    kv_local = jnp.concatenate([key_rows, value_rows], axis=1)
    kv_whole = lax.all_gather(kv_local, "seq", axis=0, tiled=True)
    query_heads = split_heads(queries)

    def attend(operands):
        query_head, key_head, value_head = operands
        probs = head_probs(query_head, key_head, mask)
        return jnp.dot(probs.astype(jnp.bfloat16), value_head, preferred_element_type=jnp.float32)

    heads_out = lax.map(
        attend, (query_heads, split_heads(kv_whole[:, :width]), split_heads(kv_whole[:, width:]))
    )
    attended = join_heads(heads_out).astype(jnp.bfloat16)
    residual = inputs + jnp.dot(attended, w_out, preferred_element_type=jnp.float32) + biases[4]
    normed_two, norm_back_two = jax.vjp(norm_rows, residual, gains[1], biases[1])
    normed_two = normed_two.astype(jnp.bfloat16)
    hidden_pre = jnp.dot(normed_two, w_up, preferred_element_type=jnp.float32) + up_bias
    activated, gelu_back = jax.vjp(partial(jax.nn.gelu, approximate=False), hidden_pre)
    activated = activated.astype(jnp.bfloat16)
    mlp_out = jnp.dot(activated, w_down, preferred_element_type=jnp.float32) + biases[5]
    block_out = jnp.where(query_live, residual + mlp_out, 0.0).astype(jnp.bfloat16)
    grad_live = jnp.where(query_live, cotangent, jnp.zeros_like(cotangent))
    grad_wdown = jnp.einsum("rf,rd->fd", activated, grad_live, preferred_element_type=jnp.float32)
    grad_activated = jnp.einsum("rd,fd->rf", grad_live, w_down, preferred_element_type=jnp.float32)
    grad_hidden = gelu_back(grad_activated)[0].astype(jnp.bfloat16)
    grad_wup = jnp.einsum("rd,rf->df", normed_two, grad_hidden, preferred_element_type=jnp.float32)
    grad_normed_two = jnp.einsum("rf,df->rd", grad_hidden, w_up, preferred_element_type=jnp.float32)
    grad_res_norm, gain_two, shift_two = norm_back_two(grad_normed_two)
    grad_residual = grad_live.astype(jnp.float32) + grad_res_norm
    grad_branch = grad_residual.astype(jnp.bfloat16)
    grad_wout = jnp.einsum("rd,re->de", attended, grad_branch, preferred_element_type=jnp.float32)
    grad_attended = jnp.einsum(
        "re,de->rd", grad_branch, w_out, preferred_element_type=jnp.float32
    ).astype(jnp.bfloat16)

    def attend_back(operands):
        query_head, key_head, value_head, grad_head = operands
        probs = head_probs(query_head, key_head, mask)
        grad_probs = jnp.einsum(
            "qd,kd->qk", grad_head, value_head, preferred_element_type=jnp.float32
        )
        grad_scores = probs * (grad_probs - jnp.sum(probs * grad_probs, axis=-1, keepdims=True))
        grad_raw = (grad_scores * 0.125).astype(jnp.bfloat16)
        grad_query = jnp.dot(grad_raw, key_head, preferred_element_type=jnp.float32)
        grad_key = jnp.einsum("qk,qd->kd", grad_raw, query_head, preferred_element_type=jnp.float32)
        grad_value = jnp.einsum(
            "qk,qd->kd", probs.astype(jnp.bfloat16), grad_head, preferred_element_type=jnp.float32
        )
        return (grad_query, grad_key, grad_value)

    grad_q_heads, grad_k_heads, grad_v_heads = lax.map(
        attend_back,
        (
            query_heads,
            split_heads(kv_whole[:, :width]),
            split_heads(kv_whole[:, width:]),
            split_heads(grad_attended),
        ),
    )
    grad_queries = join_heads(grad_q_heads).astype(jnp.bfloat16)
    grad_kv_terms = jnp.concatenate([join_heads(grad_k_heads), join_heads(grad_v_heads)], axis=1)
    grad_kv = lax.psum_scatter(
        grad_kv_terms.astype(jnp.bfloat16), "seq", scatter_dimension=0, tiled=True
    )
    grad_projected = jnp.concatenate([grad_queries, grad_kv], axis=1)
    grad_wqkv = jnp.einsum(
        "rd,re->de", normed_one, grad_projected, preferred_element_type=jnp.float32
    )
    grad_normed_one = jnp.einsum(
        "re,de->rd", grad_projected, w_qkv, preferred_element_type=jnp.float32
    )
    grad_in_norm, gain_one, shift_one = norm_back_one(grad_normed_one)
    grad_tokens = (grad_residual + grad_in_norm).astype(jnp.bfloat16)
    grad_gains = jnp.stack([gain_one, gain_two])
    grad_biases = jnp.stack(
        [
            shift_one,
            shift_two,
            jnp.sum(grad_queries.astype(jnp.float32), axis=0),
            jnp.sum(grad_kv[:, width:].astype(jnp.float32), axis=0),
            jnp.sum(grad_branch.astype(jnp.float32), axis=0),
            jnp.sum(grad_live.astype(jnp.float32), axis=0),
        ]
    )
    grad_upbias = jnp.sum(grad_hidden.astype(jnp.float32), axis=0)
    summed = (
        lax.psum_scatter(grad_wqkv, ("dp", "seq"), scatter_dimension=0, tiled=True),
        lax.psum_scatter(grad_wout, ("dp", "seq"), scatter_dimension=0, tiled=True),
        lax.psum_scatter(grad_wup, ("dp", "seq"), scatter_dimension=0, tiled=True),
        lax.psum_scatter(grad_wdown, ("dp", "seq"), scatter_dimension=0, tiled=True),
        lax.psum_scatter(grad_gains, ("dp", "seq"), scatter_dimension=1, tiled=True),
        lax.psum_scatter(grad_biases, ("dp", "seq"), scatter_dimension=1, tiled=True),
        lax.psum_scatter(grad_upbias, ("dp", "seq"), scatter_dimension=0, tiled=True),
    )
    return (
        block_out,
        grad_tokens,
        summed[0],
        summed[1],
        summed[2],
        summed[3],
        summed[4],
        summed[5],
        summed[6],
    )


def solution(mesh):
    in_specs = (
        P(("dp", "seq"), None),
        P(),
        P(),
        P(),
        P(),
        P(),
        P(),
        P(),
        P("dp"),
        P("dp"),
        P(("dp", "seq"), None),
    )
    out_specs = (
        P(("dp", "seq"), None),
        P(("dp", "seq"), None),
        P(("dp", "seq"), None),
        P(("dp", "seq"), None),
        P(("dp", "seq"), None),
        P(("dp", "seq"), None),
        P(None, ("dp", "seq")),
        P(None, ("dp", "seq")),
        P(("dp", "seq")),
    )
    fits = mesh.shape["seq"] == 2 and mesh.shape["dp"] * 2 == COUNT
    return jax.shard_map(paired if fits else shards, mesh=mesh, in_specs=in_specs, out_specs=out_specs, check_vma=False)
```

```python
from functools import partial

import jax
import jax.numpy as jnp
from jax import lax
from jax.experimental import pallas as pl
from jax.experimental.pallas import tpu as pltpu
from jax.sharding import PartitionSpec as P

HEADS = 12
HEAD_DIM = 64
PAIR = 2 * HEAD_DIM
EPSILON = 1e-06
BOTH = ("dp", "seq")
FAR = -1000000000.0
F32 = jnp.float32
BF16 = jnp.bfloat16

ME, HALF, CUT, LIVE = 0, 1, 2, 3

NN = (((1,), (0,)), ((), ()))
NT = (((1,), (1,)), ((), ()))
TN = (((0,), (0,)), ((), ()))


def mm(a, b, dims=NN):
    return lax.dot_general(a, b, dims, preferred_element_type=F32)


def params(**more):
    return pltpu.CompilerParams(vmem_limit_bytes=61 * 1024 * 1024, **more)


def norm_parts(values):
    center = values - jnp.mean(values, axis=-1, keepdims=True)
    spread = jnp.mean(center * center, axis=-1, keepdims=True)
    rstd = lax.rsqrt(spread + EPSILON)
    return center * rstd, rstd


def norm_back(grad, unit, rstd, gain):
    scaled = grad * gain
    first = jnp.mean(scaled, axis=-1, keepdims=True)
    second = jnp.mean(scaled * unit, axis=-1, keepdims=True)
    return rstd * (scaled - first - unit * second)


SIDE_X, CORE, SIDE_Y, Z_NEAR, Z_FAR = 1, 2, 4, 8, 24
ORDERS = (
    (SIDE_X, SIDE_Y, Z_NEAR, Z_FAR), (SIDE_Y, Z_NEAR, SIDE_X, Z_FAR), (Z_NEAR, SIDE_X, SIDE_Y, Z_FAR),
)
PAIR_ORDERS = (
    (SIDE_Y, Z_NEAR, SIDE_X, Z_FAR), (SIDE_Y, SIDE_X, Z_NEAR, Z_FAR), (SIDE_Y, SIDE_X, Z_NEAR, Z_FAR),
)
COUNT = 32
LANES = 384
PART = 24


def hop(value, mask):
    return lax.ppermute(value, BOTH, [(i, i ^ mask) for i in range(COUNT)])


def places(masks):
    out = [0]
    for mask in masks:
        out = [value ^ (mask * bit) for value in out for bit in (0, 1)]
    return out


def without(kernel, first, count):
    def run(*refs):
        return kernel(*refs[:first], *refs[first + count :])

    return run


def unread(count):
    return [pl.BlockSpec(memory_space=pl.ANY)] * count


def fold_kernel(*refs, jobs):
    total = sum(terms for pieces, _ in jobs for _, terms in pieces)
    meta, parts, outs = refs[0], refs[1 : total + 1], refs[total + 1 :]
    at = 0
    used = 0
    lasts = []
    for pieces, sections in jobs:
        low = 0
        for rows, terms in pieces:
            for bit in (0, 1):
                both = sum(ref[bit].astype(F32) for ref in parts[at : at + terms])
                if sections is None:
                    outs[used + bit][:, low : low + rows, :] = both.astype(BF16)
                elif bit == 0:
                    stay = both[0]
                else:
                    lasts += [(stay[a : a + n], both[0, a : a + n], split) for a, n, split in sections]
            low += rows
            at += terms
        used += 2 * (sections is None)
    if lasts:
        keep, to_core, to_chip, to_both = outs[used:]
        first = meta[HALF] == 0
        place = 0
        for stay, leave, split in sorted(lasts, key=lambda entry: not entry[2]):
            rows = stay.shape[0]
            if split:
                rows //= 2
                for value, own, far in ((stay, keep, to_core), (leave, to_chip, to_both)):
                    low, high = value[:rows], value[rows:]
                    own[place : place + rows, :] = jnp.where(first, low, high).astype(own.dtype)
                    far[place : place + rows, :] = jnp.where(first, high, low).astype(BF16)
            else:
                keep[place : place + rows, :] = stay
                to_chip[place : place + rows, :] = leave.astype(BF16)
            place += rows


def fold_call(meta, jobs, after=()):
    parts = [a for pieces, _ in jobs for piece in pieces for a in piece]
    steps = min(a.shape[0] // 2 for a in parts)
    view = lambda a: a.reshape(2, a.shape[0] // 2, *a.shape[1:])
    spec = lambda a: pl.BlockSpec((2, a.shape[0] // 2 // steps, *a.shape[1:]), lambda i, m: (0, i, 0, 0))
    sizes = [([(piece[0].shape[1], len(piece)) for piece in pieces], sections) for pieces, sections in jobs]
    out_shape, out_specs, ends = [], [], []
    for pieces, sections in jobs:
        if sections is None:
            count = pieces[0][0].shape[0] // 2
            rows = sum(piece[0].shape[1] for piece in pieces)
            out_shape += [jax.ShapeDtypeStruct((count, rows, LANES), BF16)] * 2
            out_specs += [pl.BlockSpec((count // steps, rows, LANES), lambda i, m: (i, 0, 0))] * 2
        else:
            ends += sections
    if ends:
        split = sum(n // 2 for _, n, s in ends if s)
        plain = split + sum(n for _, n, s in ends if not s)
        for rows, kind in ((plain, F32), (split, BF16), (plain, BF16), (split, BF16)):
            out_shape.append(jax.ShapeDtypeStruct((rows, LANES), kind))
            out_specs.append(pl.BlockSpec((rows, LANES), lambda i, m: (0, 0)))
    out = pl.pallas_call(
        without(partial(fold_kernel, jobs=sizes), 1 + len(parts), len(after)),
        grid_spec=pltpu.PrefetchScalarGridSpec(
            num_scalar_prefetch=1,
            grid=(steps,),
            in_specs=[spec(a) for a in parts] + unread(len(after)),
            out_specs=out_specs,
        ),
        out_shape=out_shape,
        compiler_params=params(),
        name="fold",
    )(meta, *[view(a) for a in parts], *after)
    moving = sum(sections is None for _, sections in jobs)
    result = [(out[2 * i], out[2 * i + 1]) for i in range(moving)]
    return result + ([tuple(out[2 * moving :])] if ends else [])


def hops(step, sends):
    return [hop(send, masks[step]) for send, masks in zip(sends, ORDERS)]


def last_hop(ends):
    keep, to_core, to_chip, to_both = ends
    return keep, hop(to_core, CORE), hop(to_chip, Z_FAR), hop(to_both, Z_FAR ^ CORE)


def put_rows(source, me, masks, keep, send, low, col=0, at=None):
    put_parts(source, me, masks[1:], (0, masks[0]), (keep, send), low, col, at)


def put_parts(source, me, masks, offsets, refs, low, col=0, at=None):
    cols = pl.ds(col, LANES)
    for offset, ref in zip(offsets, refs):
        for place, value in enumerate(places(masks)):
            chip = (me & ~CORE) ^ (value ^ offset)
            first = pl.multiple_of(chip * PART, 8)
            second = pl.multiple_of((chip + CORE) * PART, 8)
            where = (lambda r: source[pl.ds(r, PART), cols]) if at is None else (lambda r: source[at, pl.ds(r, PART), cols])
            both = jnp.concatenate([where(first), where(second)], axis=0)
            ref[place, low : low + 2 * PART, :] = both.astype(BF16)


def qkv_kernel(meta, mine, other, wq, wk, wv, gains, biases, unit_ref, q_ref, k_ref, v_ref, side_ref):
    step = pl.program_id(0)
    rows = side_ref.shape[1]
    key_lanes, query_lanes = mask_lanes((step ^ meta[HALF]) * rows, rows, meta)
    side_ref[0] = key_lanes
    side_ref[1] = query_lanes

    def run(ref):
        unit, _ = norm_parts(ref[...].astype(F32))
        normed = (unit * gains[0:1, :] + biases[0:1, :]).astype(BF16)
        unit_ref[...] = unit.astype(BF16).T
        half = q_ref.shape[1]
        first = pl.multiple_of(meta[HALF] * half, half)
        q_ref[...] = (mm(normed, wq[...]) + biases_at(biases, 2, first, half)).astype(BF16)
        k_ref[...] = mm(normed, wk[...]).astype(BF16)
        v_ref[...] = (mm(normed, wv[...]) + biases_at(biases, 3, first, half)).astype(BF16)

    @pl.when(step == 0)
    def _():
        run(mine)

    @pl.when(step == 1)
    def _():
        run(other)


def biases_at(biases, row, first, size):
    return biases[row : row + 1, pl.ds(first, size)]


def qkv_call(meta, mine, other, w_qkv, gains, biases):
    rows, width = mine.shape
    half = width // 2
    full = lambda shape: pl.BlockSpec(shape, lambda i, m: (0, 0))
    weight = lambda part: pl.BlockSpec((width, half), lambda i, m: (0, 2 * part + m[HALF]))
    out = lambda cols: pl.BlockSpec((rows, cols), lambda i, m: (i ^ m[HALF], 0))
    shape = lambda cols: jax.ShapeDtypeStruct((2 * rows, cols), BF16)
    return pl.pallas_call(
        qkv_kernel,
        grid_spec=pltpu.PrefetchScalarGridSpec(
            num_scalar_prefetch=1,
            grid=(2,),
            in_specs=[
                full((rows, width)), full((rows, width)), weight(0), weight(1), weight(2),
                full(gains.shape), full(biases.shape),
            ],
            out_specs=[
                pl.BlockSpec((width, rows), lambda i, m: (0, i ^ m[HALF])), out(half), out(half), out(half),
                pl.BlockSpec((2, rows, PAIR), lambda i, m: (0, i ^ m[HALF], 0)),
            ],
        ),
        out_shape=[
            jax.ShapeDtypeStruct((width, 2 * rows), BF16), shape(half), shape(half), shape(half),
            jax.ShapeDtypeStruct((2, 2 * rows, PAIR), BF16),
        ],
        compiler_params=params(),
        name="qkv",
    )(meta, mine, other, w_qkv, w_qkv, w_qkv, gains, biases)


TILE = 256


def mask_lanes(first_row, rows, meta):
    at = lax.broadcasted_iota(jnp.int32, (rows, PAIR), 1) % HEAD_DIM
    pos = first_row + lax.broadcasted_iota(jnp.int32, (rows, PAIR), 0)
    alive = pos < meta[LIVE]
    second = pos >= meta[CUT]
    first = jnp.logical_not(second)
    hidden = ((at == 0) & jnp.logical_not(alive & first)) | ((at == 1) & jnp.logical_not(alive & second))
    named = ((at == 0) & first) | ((at == 1) & second)
    keys = jnp.where(hidden, FAR, 0.0)
    queries = jnp.where(named, 1.0, 0.0)
    return keys.astype(BF16), queries.astype(BF16)


def head_lanes(head, value=1.0):
    lane = lax.broadcasted_iota(jnp.int32, (1, PAIR), 1)
    return jnp.where((lane // HEAD_DIM) == head, value, 0.0).astype(BF16)


def one_head(pair, side, head, scale=1.0):
    return pair * head_lanes(head, scale) + side * head_lanes(1 - head)


def key_range(first_row, group, meta):
    cut = meta[CUT]
    low = jnp.where(first_row >= cut, cut, 0)
    high = jnp.where(first_row + TILE <= cut, cut, meta[LIVE])
    low = (low // 128) * 128
    steps = (high - low + (TILE - 1)) // TILE
    return pl.multiple_of(jnp.minimum(low, group - steps * TILE), 128), steps


def by_width(steps, group, body):
    for count in range(1, group // TILE + 1):

        @pl.when(steps == count)
        def _(count=count):
            body(count * TILE)


def attend_kernel(meta, q_ref, k_ref, v_ref, side_ref, o_ref, lse_ref, kx_ref, vt_ref):
    group = k_ref.shape[0]
    for head in (0, 1):
        kx_ref[head] = one_head(k_ref[...], side_ref[0], head)
    vt_ref[...] = v_ref[...].T

    def tile(index, carry):
        at = pl.multiple_of(index * TILE, TILE)
        start, steps = key_range(at, group, meta)

        def body(width):
            query, side = q_ref[pl.ds(at, TILE), :], side_ref[1, pl.ds(at, TILE), :]
            parts = []
            for head in (0, 1):
                qx = one_head(query, side, head, 0.125)
                scores = mm(kx_ref[head, pl.ds(start, width), :], qx, NT)
                top = jnp.max(scores, axis=0, keepdims=True)
                weight = jnp.exp(scores - top).astype(BF16)
                value = vt_ref[head * HEAD_DIM : (head + 1) * HEAD_DIM, pl.ds(start, width)]
                left = jnp.concatenate([value, jnp.ones((16, width), BF16)], axis=0)
                both = mm(left, weight)
                total = both[HEAD_DIM : HEAD_DIM + 1, :]
                parts.append(both[:HEAD_DIM, :] / total)
                lse_ref[0, head : head + 1, pl.ds(at, TILE)] = top + jnp.log(total)
            o_ref[pl.ds(at, TILE), :] = jnp.concatenate(parts, axis=0).T.astype(BF16)

        by_width(steps, group, body)
        return carry

    lax.fori_loop(0, group // TILE, tile, 0)


def attend_call(meta, q, k, v, side):
    group, half = q.shape
    pairs = half // PAIR
    whole = pl.BlockSpec((group, PAIR), lambda p, m: (0, p))
    return pl.pallas_call(
        attend_kernel,
        grid_spec=pltpu.PrefetchScalarGridSpec(
            num_scalar_prefetch=1,
            grid=(pairs,),
            in_specs=[whole, whole, whole, full(side.shape)],
            out_specs=[whole, pl.BlockSpec((1, 2, group), lambda p, m: (p, 0, 0))],
            scratch_shapes=[pltpu.VMEM((2, group, PAIR), BF16), pltpu.VMEM((PAIR, group), BF16)],
        ),
        out_shape=[
            jax.ShapeDtypeStruct((group, half), BF16),
            jax.ShapeDtypeStruct((pairs, 2, group), F32),
        ],
        compiler_params=params(),
        name="attend",
    )(meta, q, k, v, side)


def attend_back_kernel(
    meta, q_ref, k_ref, v_ref, do_ref, o_ref, lse_ref, side_ref, unit, wq, wk, wv, gains, biases, *refs, pair,
):
    masks, offsets = pair_parts(pair)
    *refs, kx_ref, kt_ref, dk_acc, dv_acc, block = refs
    ends = len(refs) - 4 - len(offsets)
    sums, (dq_ref, dk_ref, dv_ref, sum_ref, *targets) = refs[:ends], refs[ends:]
    group = k_ref.shape[0]
    for head in (0, 1):
        kx_ref[head] = one_head(k_ref[...], side_ref[0], head)
    kt_ref[...] = k_ref[...].T
    dk_acc[...] = jnp.zeros_like(dk_acc)
    dv_acc[...] = jnp.zeros_like(dv_acc)

    def tile(index, carry):
        at = pl.multiple_of(index * TILE, TILE)
        start, steps = key_range(at, group, meta)

        def body(width):
            query, side = q_ref[pl.ds(at, TILE), :], side_ref[1, pl.ds(at, TILE), :]
            grad = do_ref[pl.ds(at, TILE), :]
            dots = (grad.astype(F32) * o_ref[pl.ds(at, TILE), :].astype(F32)).T
            probs, raws, masked_grads, masked_queries, dqs = [], [], [], [], []
            for head in (0, 1):
                qx = one_head(query, side, head, 0.125)
                dox = grad * head_lanes(head)
                scores = mm(kx_ref[head, pl.ds(start, width), :], qx, NT)
                prob = jnp.exp(scores - lse_ref[0, head : head + 1, pl.ds(at, TILE)])
                gprob = mm(v_ref[pl.ds(start, width), :], dox, NT)
                delta = jnp.sum(dots[head * HEAD_DIM : (head + 1) * HEAD_DIM, :], axis=0, keepdims=True)
                raw = (prob * (gprob - delta)).astype(BF16)
                keys_t = kt_ref[head * HEAD_DIM : (head + 1) * HEAD_DIM, pl.ds(start, width)]
                dqs.append(mm(keys_t, raw))
                probs.append(prob.astype(BF16))
                raws.append(raw)
                masked_grads.append(dox)
                masked_queries.append(query * head_lanes(head, 0.125))
            dv_acc[pl.ds(start, width), :] += mm(
                jnp.concatenate(probs, axis=1), jnp.concatenate(masked_grads, axis=0)
            )
            dk_acc[pl.ds(start, width), :] += mm(
                jnp.concatenate(raws, axis=1), jnp.concatenate(masked_queries, axis=0)
            )
            dq_ref[pl.ds(at, TILE), :] = (jnp.concatenate(dqs, axis=0).T * 0.125).astype(BF16)

        by_width(steps, group, body)
        return carry

    lax.fori_loop(0, group // TILE, tile, 0)
    dk_ref[...] = dk_acc[...].astype(BF16)
    dv_ref[...] = dv_acc[...].astype(BF16)
    grads = jnp.concatenate([dq_ref[...], dk_ref[...], dv_ref[...]], axis=1)
    total = jnp.sum(grads.astype(F32), axis=0, keepdims=True)
    product = mm(unit[...], grads)
    column = lambda row: jnp.broadcast_to(row, (PAIR, row.shape[1])).T[:, :1]
    gain, shift = column(gains[0:1, :]), column(biases[0:1, :])
    block[...] = product * gain + total * shift
    weight = jnp.concatenate([wq[...], wk[...], wv[...]], axis=1).astype(F32)
    lane = lax.broadcasted_iota(jnp.int32, sum_ref.shape, 1)
    sum_ref[...] = (
        sum((ref[...] for ref in sums), jnp.zeros(sum_ref.shape, F32))
        + jnp.where(lane == 0, jnp.sum(weight * product, axis=1, keepdims=True), 0.0)
        + jnp.where(lane == 2, jnp.sum(weight * total, axis=1, keepdims=True), 0.0)
    )
    here = pl.ds(pl.multiple_of(meta[HALF] * LANES + pair * PAIR, PAIR), PAIR)
    lane = lax.broadcasted_iota(jnp.int32, (PAIR, PAIR), 1)
    for column, part in ((4, total[:, :PAIR]), (5, total[:, 2 * PAIR :])):
        sum_ref[here, :] += jnp.where(lane == column, jnp.broadcast_to(part, (PAIR, PAIR)).T, 0.0)
    put_parts(block, meta[ME], masks, offsets, targets, 0)
    if pair == 2:
        put_sums(sum_ref, meta[ME], masks, offsets, targets, 2 * PART)


SMALL = 128


def pair_parts(pair):
    masks = PAIR_ORDERS[pair]
    if pair == 2:
        return masks[2:], (0, masks[0], masks[1], masks[0] ^ masks[1])
    return masks[1:], (0, masks[0])


def put_sums(source, me, masks, offsets, refs, low):
    for offset, ref in zip(offsets, refs):
        for place, value in enumerate(places(masks)):
            chip = (me & ~CORE) ^ (value ^ offset)
            both = [
                jnp.concatenate([source[pl.ds(pl.multiple_of((chip + c) * PART + 8 * i, 8), 8), :] for i in range(3)], axis=1)
                for c in (0, CORE)
            ]
            ref[place, low : low + 16, :] = jnp.concatenate(both, axis=0).astype(BF16)


def attend_back_call(meta, q, k, v, grad, o, lse, side, unit, w_qkv, gains, biases, sums, pair, after=()):
    group, half = q.shape
    width = unit.shape[0]
    pairs = half // PAIR
    whole = pl.BlockSpec((group, PAIR), lambda i, m: (0, pair))

    def weight(which):
        return pl.BlockSpec((width, PAIR), lambda i, m: (0, 2 * pairs * which + pairs * m[HALF] + pair))

    rows = 2 * PART + 16 * (pair == 2)
    out_shape = [jax.ShapeDtypeStruct((group, PAIR), BF16)] * 3
    masks, offsets = pair_parts(pair)
    out_shape += [jax.ShapeDtypeStruct((width, SMALL), F32)]
    out_shape += [jax.ShapeDtypeStruct((2 ** len(masks), rows, LANES), BF16)] * len(offsets)
    return pl.pallas_call(
        without(partial(attend_back_kernel, pair=pair), 14 + len(sums), len(after)),
        grid_spec=pltpu.PrefetchScalarGridSpec(
            num_scalar_prefetch=1,
            grid=(1,),
            in_specs=[whole] * 5
            + [pl.BlockSpec((1, 2, group), lambda i, m: (pair, 0, 0)), full(side.shape), full(unit.shape), weight(0), weight(1), weight(2)]
            + [full(a.shape) for a in (gains, biases, *sums)] + unread(len(after)),
            out_specs=[full(a.shape) for a in out_shape],
            scratch_shapes=[
                pltpu.VMEM((2, group, PAIR), BF16),
                pltpu.VMEM((PAIR, group), BF16),
                pltpu.VMEM((group, PAIR), F32),
                pltpu.VMEM((group, PAIR), F32),
                pltpu.VMEM((width, LANES), F32),
            ],
        ),
        out_shape=out_shape,
        compiler_params=params(),
        name="attend_back",
    )(meta, q, k, v, grad, o, lse, side, unit, w_qkv, w_qkv, w_qkv, gains, biases, *sums, *after)


UNITS = 192
STEPS = 2
ROWS = 256
MLP_ROWS = 512

ERF_TOP = (0.00022905065861350646, 0.0034082910107109506, 0.050955695062380861, 0.18520832239976145, 1.128379143519084)
ERF_LOW = (
    -1.1791602954361697e-7, 0.000023547966471313185, 0.0010179625278914885, 0.014070470171167667,
    0.11098505178285362, 0.49746925110067538, 1.0,
)


def erf(x):
    x = jnp.clip(x, -3.832506856900711, 3.832506856900711)
    square = x * x
    top = jnp.full_like(x, ERF_TOP[0])
    for c in ERF_TOP[1:]:
        top = top * square + c
    low = jnp.full_like(x, ERF_LOW[0])
    for c in ERF_LOW[1:]:
        low = low * square + c
    return x * top / low


def mid_kernel(
    meta, tok_mine, tok_other, cot_mine, cot_other, a_own, a_got, w_out, w_up, w_down, gains, biases, up_bias,
    res_ref, block_ref, block_send, dn_ref, gub_ref, k0, s0, k1, s1, k2, s2,
    n2, n2t, gl, act, gh, wu, up_acc, down_acc, out_acc, dn_acc,
):
    step = pl.program_id(0)
    rows, width = tok_mine.shape
    half = a_own.shape[1]
    chunk = wu.shape[1]
    me = meta[ME]
    own = pl.multiple_of(meta[HALF] * half, half)
    far = pl.multiple_of((1 - meta[HALF]) * half, half)
    mine = pl.multiple_of(meta[HALF] * rows, rows)
    other = pl.multiple_of((1 - meta[HALF]) * rows, rows)

    @pl.when(step == 0)
    def _():
        for place, tok, cot in ((mine, tok_mine, cot_mine), (other, tok_other, cot_other)):
            for low in range(0, rows, ROWS):
                at = pl.ds(pl.multiple_of(place + low, ROWS), ROWS)
                residual = (
                    tok[low : low + ROWS, :].astype(F32)
                    + mm(a_own[at, :], w_out[pl.ds(own, half), :])
                    + mm(a_got[at, :], w_out[pl.ds(far, half), :])
                    + biases[4:5, :]
                )
                res_ref[at, :] = residual
                unit, _ = norm_parts(residual)
                n2[at, :] = (unit * gains[1:2, :] + biases[1:2, :]).astype(BF16)
                live = place + low + lax.broadcasted_iota(jnp.int32, (ROWS, 1), 0) < meta[LIVE]
                cots = cot[low : low + ROWS, :]
                gl[at, :] = jnp.where(live, cots, jnp.zeros_like(cots))
        n2t[...] = n2[...].T

    for core in (0, 1):

        @pl.when(meta[HALF] == core)
        def _(core=core):
            for block in range(chunk // UNITS):
                at = (2 * block + core) * UNITS
                wu[:, block * UNITS : (block + 1) * UNITS] = w_up[:, at : at + UNITS]

    wd = w_down[...].reshape(chunk, width)
    gub = jnp.zeros((1, chunk), F32)
    def tile(index, gub):
        at = pl.ds(pl.multiple_of(index * MLP_ROWS, MLP_ROWS), MLP_ROWS)
        hidden = mm(n2[at, :], wu[...]) + up_bias[...]
        gact = mm(gl[at, :], wd, NT)
        cdf = 0.5 * (1.0 + erf(hidden * 0.7071067811865476))
        pdf = jnp.exp(-0.5 * hidden * hidden) * 0.3989422804014327
        active = (hidden * cdf).astype(BF16)
        grad_hidden = gact * (cdf + hidden * pdf)
        gub = gub + jnp.sum(grad_hidden, axis=0, keepdims=True)
        grad_hidden = grad_hidden.astype(BF16)
        act[at, :] = active
        gh[at, :] = grad_hidden
        out_acc[at, :] = jnp.where(step == 0, 0.0, out_acc[at, :]) + mm(active, wd)
        dn_acc[at, :] = jnp.where(step == 0, 0.0, dn_acc[at, :]) + mm(grad_hidden, wu[...], NT)
        return gub

    gub = lax.fori_loop(0, 2 * rows // MLP_ROWS, tile, gub)
    gub_ref[...] = gub
    down_acc[pl.ds(pl.multiple_of(step * chunk, chunk), chunk), :] = mm(act[...], gl[...], TN).astype(BF16)
    up_acc[step] = mm(n2t[...], gh[...])

    @pl.when(step == STEPS - 1)
    def _():
        pos = lax.broadcasted_iota(jnp.int32, (rows, 1), 0)
        at = pl.ds(mine, rows)
        block_ref[...] = jnp.where(
            mine + pos < meta[LIVE], res_ref[at, :] + out_acc[at, :] + biases[5:6, :], 0.0
        ).astype(BF16)
        block_send[...] = jnp.where(other + pos < meta[LIVE], out_acc[pl.ds(other, rows), :], 0.0).astype(BF16)
        dn_ref[...] = dn_acc[...].astype(BF16)
        for block, (keep, send, masks, low) in enumerate(
            ((k0, s0, ORDERS[0], 0), (k0, s0, ORDERS[0], 48), (k0, s0, ORDERS[0], 96), (k1, s1, ORDERS[1], 0))
        ):
            put_rows(up_acc, me, masks, keep, send, low, (block % 2) * LANES, block // 2)
        for col, (keep, send, masks, low) in enumerate(((k1, s1, ORDERS[1], 48), (k2, s2, ORDERS[2], 0))):
            for bit, ref in ((0, keep), (1, send)):
                for place, value in enumerate(places(masks[1:])):
                    chip = me ^ (value ^ (masks[0] * bit))
                    first = pl.multiple_of((chip // 4) * UNITS + (chip & 1) * (UNITS // 2), UNITS // 2)
                    ref[place, low : low + UNITS // 2, :] = down_acc[
                        pl.ds(first, UNITS // 2), col * LANES : (col + 1) * LANES
                    ]


def full(shape):
    return pl.BlockSpec(shape, lambda *a: (0,) * len(shape))


def once(shape):
    return pl.BlockSpec(shape, lambda *a: (0,) * len(shape), pipeline_mode=pl.Buffered(1))


def mid_call(meta, tok_mine, tok_other, cot_mine, cot_other, a_own, a_got, w_out, w_up, w_down, gains, biases, up_bias):
    rows, width = tok_mine.shape
    ff = w_up.shape[1]
    chunk = ff // 2 // STEPS
    blocks = chunk // UNITS
    group = 2 * rows
    stream = [144, 144, 144, 144, 96, 96]
    out_shape = [
        jax.ShapeDtypeStruct((group, width), F32), jax.ShapeDtypeStruct((rows, width), BF16),
        jax.ShapeDtypeStruct((rows, width), BF16), jax.ShapeDtypeStruct((group, width), BF16),
        jax.ShapeDtypeStruct((1, ff // 2), F32),
    ] + [jax.ShapeDtypeStruct((8, n, LANES), BF16) for n in stream]
    out_specs = [once(s.shape) for s in out_shape]
    out_specs[4] = pl.BlockSpec((1, chunk), lambda i, m: (0, i))
    out = pl.pallas_call(
        mid_kernel,
        grid_spec=pltpu.PrefetchScalarGridSpec(
            num_scalar_prefetch=1,
            grid=(STEPS,),
            in_specs=[
                once((rows, width)), once((rows, width)), once((rows, width)), once((rows, width)),
                once(a_own.shape), once(a_got.shape), once(w_out.shape),
                pl.BlockSpec((width, 2 * chunk), lambda i, m: (0, i)),
                pl.BlockSpec((blocks, 1, UNITS, width), lambda i, m: (i, m[HALF], 0, 0)),
                full(gains.shape), full(biases.shape),
                pl.BlockSpec((1, chunk), lambda i, m: (0, i)),
            ],
            out_specs=out_specs,
            scratch_shapes=[
                pltpu.VMEM((group, width), BF16), pltpu.VMEM((width, group), BF16), pltpu.VMEM((group, width), BF16),
                pltpu.VMEM((group, chunk), BF16), pltpu.VMEM((group, chunk), BF16), pltpu.VMEM((width, chunk), BF16),
                pltpu.VMEM((STEPS, width, chunk), F32), pltpu.VMEM((ff // 2, width), BF16),
                pltpu.VMEM((group, width), F32), pltpu.VMEM((group, width), F32),
            ],
        ),
        out_shape=out_shape,
        compiler_params=params(),
        name="mid",
    )(
        meta, tok_mine, tok_other, cot_mine, cot_other, a_own, a_got, w_out, w_up,
        w_down.reshape(ff // UNITS // 2, 2, UNITS, width), gains, biases, up_bias,
    )
    return out[:5], out[5::2], out[6::2]


def branch_kernel(
    meta, res, cot_mine, cot_other, dn_own, dn_got, a_own, a_got, w_out, gains,
    gres_ref, ga_ref, small_ref, keep, send, gb, whole,
):
    rows, width = cot_mine.shape
    half = a_own.shape[1]
    own = pl.multiple_of(meta[HALF] * half, half)
    far = pl.multiple_of((1 - meta[HALF]) * half, half)
    mine = pl.multiple_of(meta[HALF] * rows, rows)
    other = pl.multiple_of((1 - meta[HALF]) * rows, rows)
    small = jnp.zeros((4, width), F32)
    for place, cot in ((mine, cot_mine), (other, cot_other)):
        for low in range(0, rows, ROWS):
            at = pl.ds(pl.multiple_of(place + low, ROWS), ROWS)
            unit, rstd = norm_parts(res[at, :])
            grad = dn_own[at, :].astype(F32) + dn_got[at, :].astype(F32)
            live = place + low + lax.broadcasted_iota(jnp.int32, (ROWS, 1), 0) < meta[LIVE]
            gl = jnp.where(live, cot[low : low + ROWS, :].astype(F32), 0.0)
            gres = gl + norm_back(grad, unit, rstd, gains[1:2, :])
            branch = gres.astype(BF16)
            gb[at, :] = branch
            if cot is cot_mine:
                gres_ref[low : low + ROWS, :] = branch
                small += jnp.concatenate(
                    [jnp.sum(a, axis=0, keepdims=True) for a in (grad * unit, grad, branch.astype(F32), gl)], axis=0
                )
    small_ref[0:4, :] = small
    small_ref[4:8, :] = jnp.zeros((4, width), F32)
    ga_ref[...] = mm(gb[...], w_out[pl.ds(own, half), :], NT).astype(BF16)
    part = gb[:, pl.ds(own, half)]
    whole[pl.ds(own, half), :] = mm(a_own[...], part, TN)
    whole[pl.ds(far, half), :] = mm(a_got[...], part, TN)
    put_rows(whole, meta[ME], ORDERS[2], keep, send, 0)


def branch_call(meta, res, cot_mine, cot_other, dn_own, dn_got, a_own, a_got, w_out, gains):
    rows, width = cot_mine.shape
    group, half = a_own.shape
    args = (res, cot_mine, cot_other, dn_own, dn_got, a_own, a_got, w_out, gains)
    out_shape = [
        jax.ShapeDtypeStruct((rows, width), BF16), jax.ShapeDtypeStruct((group, half), BF16),
        jax.ShapeDtypeStruct((8, width), F32),
    ] + [jax.ShapeDtypeStruct((8, 2 * PART, LANES), BF16)] * 2
    return pl.pallas_call(
        branch_kernel,
        grid_spec=pltpu.PrefetchScalarGridSpec(
            num_scalar_prefetch=1,
            grid=(1,),
            in_specs=[full(a.shape) for a in args],
            out_specs=[full(a.shape) for a in out_shape],
            scratch_shapes=[pltpu.VMEM((group, width), BF16), pltpu.VMEM((width, half), F32)],
        ),
        out_shape=out_shape,
        compiler_params=params(),
        name="branch",
    )(meta, *args)


def qkv_back_kernel(meta, d0, d1, d2, d3, d4, d5, d6, d7, d8, wq, wk, wv, dn_own, dn_send):
    rows = dn_own.shape[0]
    for ref, half in ((dn_send, 1 - meta[HALF]), (dn_own, meta[HALF])):
        at = pl.ds(pl.multiple_of(half * rows, rows), rows)
        total = 0.0
        for parts, weight in (((d0, d3, d6), wq), ((d1, d4, d7), wk), ((d2, d5, d8), wv)):
            total += mm(jnp.concatenate([a[at, :] for a in parts], axis=1), weight[...], NT)
        ref[...] = total.astype(ref.dtype)


def qkv_back_call(meta, grads, w_qkv, after=()):
    group = grads[0].shape[0]
    width = w_qkv.shape[0]
    half = width // 2

    def weight(which):
        return pl.BlockSpec((width, half), lambda i, m: (0, 2 * which + m[HALF]))

    out_shape = [jax.ShapeDtypeStruct((group // 2, width), BF16)] * 2
    return pl.pallas_call(
        without(qkv_back_kernel, 13, len(after)),
        grid_spec=pltpu.PrefetchScalarGridSpec(
            num_scalar_prefetch=1,
            grid=(1,),
            in_specs=[full(a.shape) for a in grads] + [weight(0), weight(1), weight(2)] + unread(len(after)),
            out_specs=[full(a.shape) for a in out_shape],
        ),
        out_shape=out_shape,
        compiler_params=params(),
        name="qkv_back",
    )(meta, *grads, w_qkv, w_qkv, w_qkv, *after)


def tail_kernel(tok, gres, dn_own, dn_got, gains, out):
    unit, rstd = norm_parts(tok[...].astype(F32))
    grad = dn_own[...].astype(F32) + dn_got[...].astype(F32)
    out[...] = (gres[...].astype(F32) + norm_back(grad, unit, rstd, gains[0:1, :])).astype(BF16)


def tail_call(tok, gres, dn_own, dn_got, gains, after=()):
    rows, width = tok.shape
    block = pl.BlockSpec((rows // 2, width), lambda i: (i, 0))
    return pl.pallas_call(
        without(tail_kernel, 5, len(after)),
        grid=(2,),
        in_specs=[block, block, block, block, pl.BlockSpec(gains.shape, lambda i: (0, 0))] + unread(len(after)),
        out_specs=block,
        out_shape=jax.ShapeDtypeStruct((rows, width), BF16),
        compiler_params=params(),
        name="tail",
    )(tok, gres, dn_own, dn_got, gains, *after)


A_SECTIONS = (
    [(0, 48, True), (48, 48, True), (96, 48, True)], [(0, 48, True), (48, 96, False)], [(0, 96, False), (96, 48, True)],
)


def join_a_kernel(meta, keep, from_core, from_chip, from_both, block, up, out, down, block_out, own, far):
    block_out[...] = block[...]
    split = from_core.shape[0]
    own[...] = keep[...] + from_chip[...].astype(F32)
    far[...] = from_core[...].astype(F32) + from_both[...].astype(F32)
    down[:, :LANES] = own[split : split + 4 * PART, :]
    down[:, LANES:] = own[split + 4 * PART :, :]
    for core in (0, 1):

        @pl.when(meta[HALF] == core)
        def _(core=core):
            for side, ref in ((core, own), (1 - core, far)):
                for block in range(8):
                    at = (2 * block + side) * UNITS
                    low = (block % 2) * UNITS
                    row = (block // 2) * PART
                    up[:, at : at + UNITS] = ref[row : row + PART, low : low + UNITS]
                out[:, side * LANES : (side + 1) * LANES] = ref[4 * PART : 5 * PART, :]


def join_b_kernel(meta, keep, from_core, from_chip, from_both, qkv, gain, bias, up_bias):
    own = keep[...] + from_chip[...].astype(F32)
    far = from_core[...].astype(F32) + from_both[...].astype(F32)
    for core in (0, 1):

        @pl.when(meta[HALF] == core)
        def _(core=core):
            for side, value in ((core, own), (1 - core, far)):
                for pair in range(3):
                    part = value[pair * PART : (pair + 1) * PART]
                    for i in range(3):
                        at = (2 * i + side) * LANES + pair * PAIR
                        qkv[:, at : at + PAIR] = part[:, i * PAIR : (i + 1) * PAIR]

    small = own[3 * PART :] + far[3 * PART :]
    turned = jnp.concatenate([small[:, i * SMALL : (i + 1) * SMALL] for i in range(3)], axis=0).T
    gain[...] = turned[0:2]
    bias[...] = turned[2:8]
    up_bias[...] = jnp.concatenate([turned[8 + i : 9 + i] for i in range(4)], axis=1)


def whole_call(kernel, name, meta, args, shapes, scratch=(), after=()):
    shapes = [jax.ShapeDtypeStruct(s, F32) if isinstance(s, tuple) else jax.ShapeDtypeStruct(s.shape, s.dtype) for s in shapes]
    return pl.pallas_call(
        without(kernel, 1 + len(args), len(after)),
        grid_spec=pltpu.PrefetchScalarGridSpec(
            num_scalar_prefetch=1,
            grid=(1,),
            in_specs=[full(a.shape) for a in args] + unread(len(after)),
            out_specs=[full(s.shape) for s in shapes],
            scratch_shapes=[pltpu.VMEM(s, F32) for s in scratch],
        ),
        out_shape=shapes,
        compiler_params=params(),
        name=name,
    )(meta, *args, *after)


def paired(
    tokens, w_qkv, w_out, w_up, w_down, gains, biases, up_bias, image_cut, group_live, cotangent
):
    width = tokens.shape[1]
    half = width // 2
    width_ff = w_up.shape[1]
    core = lax.axis_index("dp") % 2
    me = (lax.axis_index("dp") * 2 + lax.axis_index("seq")).astype(jnp.int32)
    swap = [(i, (i & ~3) | ((i & 1) << 1) | ((i >> 1) & 1)) for i in range(COUNT)]

    def trade(value):
        return lax.ppermute(value, BOTH, swap)

    def across(value):
        return hop(value, CORE)

    tok = trade(tokens)
    own_bounds = jnp.concatenate([image_cut, group_live])
    bounds = jnp.where(core == lax.axis_index("seq"), own_bounds, across(own_bounds))
    tok_far = across(tok)
    meta = jnp.concatenate([jnp.stack([me, core.astype(jnp.int32)]), bounds])
    cot_here, tok_far, meta = lax.optimization_barrier((cotangent, tok_far, meta))
    cot = trade(cot_here)
    blocks = up_bias.reshape(-1, 2, UNITS)
    own_bias = jnp.where(core == 0, blocks[:, 0], blocks[:, 1]).reshape(1, -1)

    unit, q, k, v, side = qkv_call(meta, tok, tok_far, w_qkv, gains, biases)
    o, lse = attend_call(meta, q, k, v, side)
    o_got = across(o)
    cot_far = across(lax.optimization_barrier((cot, o))[0])
    (res, block, block_send, dn, gub), keeps, sends = mid_call(
        meta, tok, tok_far, cot, cot_far, o, o_got, w_out, w_up, w_down, gains, biases, own_bias
    )
    dn_got = across(dn)
    a_got = hops(0, sends)
    block_got = across(block_send)
    block_out = trade((block.astype(F32) + block_got.astype(F32)).astype(BF16))
    gres, ga, small, out_keep, out_send = branch_call(meta, res, cot, cot_far, dn, dn_got, o, o_got, w_out, gains)
    out_got = hop(out_send, ORDERS[2][0])

    zero = jnp.zeros((width,), F32)
    rows = jnp.stack([zero, small[0], zero, small[1], zero, zero, small[2], small[3]])
    units = gub.reshape(-1, 1, UNITS)
    units = jnp.where(jnp.arange(2)[None, :, None] == core, units, 0.0)
    units = units.reshape(COUNT, 4, PART).transpose(0, 2, 1).reshape(width, 4)
    early = jnp.concatenate([rows.T, units, jnp.zeros((width, SMALL - 12), F32)], axis=1)

    def pair_hop(pair, step, send):
        return hop(send, PAIR_ORDERS[pair][step])

    def tied(value, to):
        return lax.optimization_barrier((value, to))[0]

    *grads, sums, b0, b0_send = attend_back_call(meta, q, k, v, ga, o, lse, side, unit, w_qkv, gains, biases, [], 0)
    a0, a1, a2 = fold_call(
        meta,
        [
            ([(keeps[0], a_got[0])], None), ([(keeps[1], a_got[1])], None),
            ([(keeps[2], a_got[2]), (out_keep, out_got)], None),
        ],
        [b0_send],
    )
    a_got = hops(1, [a0[1], a1[1], a2[1]])
    b0_got = pair_hop(0, 0, tied(b0_send, a0[1]))
    *more, sums, b1, b1_send = attend_back_call(meta, q, k, v, ga, o, lse, side, unit, w_qkv, gains, biases, [sums], 1, [a0[1]])
    grads = grads + more
    a0, a1, a2, p0 = fold_call(
        meta,
        [([(a[0], g)], None) for a, g in zip((a0, a1, a2), a_got)] + [([(b0, b0_got)], None)],
        [b1_send],
    )
    a_got = hops(2, [a0[1], a1[1], a2[1]])
    p0_got = pair_hop(0, 1, p0[1])
    b1_got = pair_hop(1, 0, tied(b1_send, p0[1]))
    more = attend_back_call(meta, q, k, v, ga, o, lse, side, unit, w_qkv, gains, biases, [sums, early], 2, [a0[1]])
    grads, b2, b2_sends = grads + list(more[:3]), more[4], more[5:]
    p0, p1, a_end = fold_call(
        meta,
        [([(p0[0], p0_got)], None), ([(b1, b1_got)], None)]
        + [([(a[0], g)], sections) for a, g, sections in zip((a0, a1, a2), a_got, A_SECTIONS)],
        [b2_sends[0], block_out],
    )
    p0_got, p1_got = pair_hop(0, 2, p0[1]), pair_hop(1, 1, p1[1])
    b2_sends = lax.optimization_barrier((*b2_sends, p1[1]))[:-1]
    b2_got = [hop(send, mask) for send, mask in zip(b2_sends, pair_parts(2)[1][1:])]
    a_end = last_hop(a_end)
    dn_own, dn_send = qkv_back_call(meta, grads, w_qkv, [p1[1]])
    p1, p2 = fold_call(meta, [([(p1[0], p1_got)], None), ([(b2, *b2_got)], None)], [dn_own, *a_end[1:]])
    p1_got, p2_got = pair_hop(1, 2, p1[1]), pair_hop(2, 2, p2[1])
    dn_got = across(tied(dn_send, p2[1]))
    mine = tail_call(tok, gres, dn_own, dn_got, gains, [p2[1]])
    cut = [(0, 48, True)]
    (b_end,) = fold_call(
        meta,
        [([(p0[0], p0_got)], cut), ([(p1[0], p1_got)], cut), ([(p2[0], p2_got)], cut + [(48, 16, True)])],
        [mine],
    )
    grad_tokens = trade(tied(mine, b_end[1]))
    grad_wup, grad_wout, grad_wdown, block_out = whole_call(
        join_a_kernel, "join_a", meta, [*a_end, block_out],
        [(PART, width_ff), (PART, width), (4 * PART, width), block_out],
        [a_end[0].shape, a_end[1].shape], [b_end[1]],
    )
    b_end = last_hop(b_end)
    grad_qkv, grad_gains, grad_biases, grad_upbias = whole_call(
        join_b_kernel, "join_b", meta, b_end, [(PART, 3 * width), (2, PART), (6, PART), (1, 4 * PART)],
        after=[grad_wdown],
    )
    return (
        block_out, grad_tokens, grad_qkv, grad_wout, grad_wup, grad_wdown, grad_gains, grad_biases,
        grad_upbias.reshape(-1),
    )


def norm_rows(values, gain, shift):
    center = values - jnp.mean(values, axis=-1, keepdims=True)
    spread = jnp.mean(center * center, axis=-1, keepdims=True)
    return center * lax.rsqrt(spread + EPSILON) * gain + shift


def split_heads(values):
    return values.reshape(values.shape[0], HEADS, -1).transpose(1, 0, 2)


def join_heads(values):
    return values.transpose(1, 0, 2).reshape(values.shape[1], -1)


def head_probs(query_head, key_head, mask):
    raw = jnp.einsum("qd,kd->qk", query_head, key_head, preferred_element_type=jnp.float32)
    return jax.nn.softmax(raw * 0.125 + mask, axis=-1)


def shards(
    tokens, w_qkv, w_out, w_up, w_down, gains, biases, up_bias, image_cut, group_live, cotangent
):
    rows_here = tokens.shape[0]
    width = tokens.shape[1]
    group = rows_here * lax.axis_size("seq")
    first_row = lax.axis_index("seq") * rows_here
    cut_row = image_cut[0]
    live_rows = group_live[0]
    key_pos = jnp.arange(group, dtype=jnp.int32)
    query_pos = first_row + jnp.arange(rows_here, dtype=jnp.int32)
    query_live = (query_pos < live_rows)[:, None]
    allowed = ((query_pos >= cut_row)[:, None] == (key_pos >= cut_row)[None, :]) & (
        key_pos < live_rows
    )[None, :]
    mask = jnp.where(allowed, 0.0, -1000000000.0).astype(jnp.float32)
    inputs = tokens.astype(jnp.float32)
    normed_one, norm_back_one = jax.vjp(norm_rows, inputs, gains[0], biases[0])
    normed_one = normed_one.astype(jnp.bfloat16)
    projected = jnp.dot(normed_one, w_qkv, preferred_element_type=jnp.float32)
    queries = (projected[:, :width] + biases[2]).astype(jnp.bfloat16)
    key_rows = projected[:, width : 2 * width].astype(jnp.bfloat16)
    value_rows = (projected[:, 2 * width :] + biases[3]).astype(jnp.bfloat16)
    kv_local = jnp.concatenate([key_rows, value_rows], axis=1)
    kv_whole = lax.all_gather(kv_local, "seq", axis=0, tiled=True)
    query_heads = split_heads(queries)

    def attend(operands):
        query_head, key_head, value_head = operands
        probs = head_probs(query_head, key_head, mask)
        return jnp.dot(probs.astype(jnp.bfloat16), value_head, preferred_element_type=jnp.float32)

    heads_out = lax.map(
        attend, (query_heads, split_heads(kv_whole[:, :width]), split_heads(kv_whole[:, width:]))
    )
    attended = join_heads(heads_out).astype(jnp.bfloat16)
    residual = inputs + jnp.dot(attended, w_out, preferred_element_type=jnp.float32) + biases[4]
    normed_two, norm_back_two = jax.vjp(norm_rows, residual, gains[1], biases[1])
    normed_two = normed_two.astype(jnp.bfloat16)
    hidden_pre = jnp.dot(normed_two, w_up, preferred_element_type=jnp.float32) + up_bias
    activated, gelu_back = jax.vjp(partial(jax.nn.gelu, approximate=False), hidden_pre)
    activated = activated.astype(jnp.bfloat16)
    mlp_out = jnp.dot(activated, w_down, preferred_element_type=jnp.float32) + biases[5]
    block_out = jnp.where(query_live, residual + mlp_out, 0.0).astype(jnp.bfloat16)
    grad_live = jnp.where(query_live, cotangent, jnp.zeros_like(cotangent))
    grad_wdown = jnp.einsum("rf,rd->fd", activated, grad_live, preferred_element_type=jnp.float32)
    grad_activated = jnp.einsum("rd,fd->rf", grad_live, w_down, preferred_element_type=jnp.float32)
    grad_hidden = gelu_back(grad_activated)[0].astype(jnp.bfloat16)
    grad_wup = jnp.einsum("rd,rf->df", normed_two, grad_hidden, preferred_element_type=jnp.float32)
    grad_normed_two = jnp.einsum("rf,df->rd", grad_hidden, w_up, preferred_element_type=jnp.float32)
    grad_res_norm, gain_two, shift_two = norm_back_two(grad_normed_two)
    grad_residual = grad_live.astype(jnp.float32) + grad_res_norm
    grad_branch = grad_residual.astype(jnp.bfloat16)
    grad_wout = jnp.einsum("rd,re->de", attended, grad_branch, preferred_element_type=jnp.float32)
    grad_attended = jnp.einsum(
        "re,de->rd", grad_branch, w_out, preferred_element_type=jnp.float32
    ).astype(jnp.bfloat16)

    def attend_back(operands):
        query_head, key_head, value_head, grad_head = operands
        probs = head_probs(query_head, key_head, mask)
        grad_probs = jnp.einsum(
            "qd,kd->qk", grad_head, value_head, preferred_element_type=jnp.float32
        )
        grad_scores = probs * (grad_probs - jnp.sum(probs * grad_probs, axis=-1, keepdims=True))
        grad_raw = (grad_scores * 0.125).astype(jnp.bfloat16)
        grad_query = jnp.dot(grad_raw, key_head, preferred_element_type=jnp.float32)
        grad_key = jnp.einsum("qk,qd->kd", grad_raw, query_head, preferred_element_type=jnp.float32)
        grad_value = jnp.einsum(
            "qk,qd->kd", probs.astype(jnp.bfloat16), grad_head, preferred_element_type=jnp.float32
        )
        return (grad_query, grad_key, grad_value)

    grad_q_heads, grad_k_heads, grad_v_heads = lax.map(
        attend_back,
        (
            query_heads,
            split_heads(kv_whole[:, :width]),
            split_heads(kv_whole[:, width:]),
            split_heads(grad_attended),
        ),
    )
    grad_queries = join_heads(grad_q_heads).astype(jnp.bfloat16)
    grad_kv_terms = jnp.concatenate([join_heads(grad_k_heads), join_heads(grad_v_heads)], axis=1)
    grad_kv = lax.psum_scatter(
        grad_kv_terms.astype(jnp.bfloat16), "seq", scatter_dimension=0, tiled=True
    )
    grad_projected = jnp.concatenate([grad_queries, grad_kv], axis=1)
    grad_wqkv = jnp.einsum(
        "rd,re->de", normed_one, grad_projected, preferred_element_type=jnp.float32
    )
    grad_normed_one = jnp.einsum(
        "re,de->rd", grad_projected, w_qkv, preferred_element_type=jnp.float32
    )
    grad_in_norm, gain_one, shift_one = norm_back_one(grad_normed_one)
    grad_tokens = (grad_residual + grad_in_norm).astype(jnp.bfloat16)
    grad_gains = jnp.stack([gain_one, gain_two])
    grad_biases = jnp.stack(
        [
            shift_one,
            shift_two,
            jnp.sum(grad_queries.astype(jnp.float32), axis=0),
            jnp.sum(grad_kv[:, width:].astype(jnp.float32), axis=0),
            jnp.sum(grad_branch.astype(jnp.float32), axis=0),
            jnp.sum(grad_live.astype(jnp.float32), axis=0),
        ]
    )
    grad_upbias = jnp.sum(grad_hidden.astype(jnp.float32), axis=0)
    summed = (
        lax.psum_scatter(grad_wqkv, ("dp", "seq"), scatter_dimension=0, tiled=True),
        lax.psum_scatter(grad_wout, ("dp", "seq"), scatter_dimension=0, tiled=True),
        lax.psum_scatter(grad_wup, ("dp", "seq"), scatter_dimension=0, tiled=True),
        lax.psum_scatter(grad_wdown, ("dp", "seq"), scatter_dimension=0, tiled=True),
        lax.psum_scatter(grad_gains, ("dp", "seq"), scatter_dimension=1, tiled=True),
        lax.psum_scatter(grad_biases, ("dp", "seq"), scatter_dimension=1, tiled=True),
        lax.psum_scatter(grad_upbias, ("dp", "seq"), scatter_dimension=0, tiled=True),
    )
    return (
        block_out,
        grad_tokens,
        summed[0],
        summed[1],
        summed[2],
        summed[3],
        summed[4],
        summed[5],
        summed[6],
    )


def solution(mesh):
    in_specs = (
        P(("dp", "seq"), None),
        P(),
        P(),
        P(),
        P(),
        P(),
        P(),
        P(),
        P("dp"),
        P("dp"),
        P(("dp", "seq"), None),
    )
    out_specs = (
        P(("dp", "seq"), None),
        P(("dp", "seq"), None),
        P(("dp", "seq"), None),
        P(("dp", "seq"), None),
        P(("dp", "seq"), None),
        P(("dp", "seq"), None),
        P(None, ("dp", "seq")),
        P(None, ("dp", "seq")),
        P(("dp", "seq")),
    )
    fits = mesh.shape["seq"] == 2 and mesh.shape["dp"] * 2 == COUNT
    return jax.shard_map(paired if fits else shards, mesh=mesh, in_specs=in_specs, out_specs=out_specs, check_vma=False)
```

```python
from functools import partial

import jax
import jax.numpy as jnp
from jax import lax
from jax.experimental import pallas as pl
from jax.experimental.pallas import tpu as pltpu
from jax.sharding import PartitionSpec as P

HEADS = 12
HEAD_DIM = 64
PAIR = 2 * HEAD_DIM
EPSILON = 1e-06
BOTH = ("dp", "seq")
FAR = -1000000000.0
F32 = jnp.float32
BF16 = jnp.bfloat16

ME, HALF, CUT, LIVE = 0, 1, 2, 3

NN = (((1,), (0,)), ((), ()))
NT = (((1,), (1,)), ((), ()))
TN = (((0,), (0,)), ((), ()))


def mm(a, b, dims=NN):
    return lax.dot_general(a, b, dims, preferred_element_type=F32)


def params(**more):
    return pltpu.CompilerParams(vmem_limit_bytes=61 * 1024 * 1024, **more)


def norm_parts(values):
    center = values - jnp.mean(values, axis=-1, keepdims=True)
    spread = jnp.mean(center * center, axis=-1, keepdims=True)
    rstd = lax.rsqrt(spread + EPSILON)
    return center * rstd, rstd


def norm_back(grad, unit, rstd, gain):
    scaled = grad * gain
    first = jnp.mean(scaled, axis=-1, keepdims=True)
    second = jnp.mean(scaled * unit, axis=-1, keepdims=True)
    return rstd * (scaled - first - unit * second)


SIDE_X, CORE, SIDE_Y, Z_NEAR, Z_FAR = 1, 2, 4, 8, 24
ORDERS = (
    (SIDE_X, SIDE_Y, Z_NEAR, Z_FAR), (SIDE_Y, Z_NEAR, SIDE_X, Z_FAR), (Z_NEAR, SIDE_X, SIDE_Y, Z_FAR),
)
PAIR_ORDERS = (
    (SIDE_Y, Z_NEAR, SIDE_X, Z_FAR), (SIDE_Y, SIDE_X, Z_NEAR, Z_FAR), (SIDE_Y, SIDE_X, Z_NEAR, Z_FAR),
)
COUNT = 32
LANES = 384
PART = 24


def hop(value, mask):
    return lax.ppermute(value, BOTH, [(i, i ^ mask) for i in range(COUNT)])


def places(masks):
    out = [0]
    for mask in masks:
        out = [value ^ (mask * bit) for value in out for bit in (0, 1)]
    return out


def without(kernel, first, count):
    def run(*refs):
        return kernel(*refs[:first], *refs[first + count :])

    return run


def unread(count):
    return [pl.BlockSpec(memory_space=pl.ANY)] * count


def fold_kernel(*refs, jobs):
    total = sum(terms for pieces, _ in jobs for _, terms in pieces)
    meta, parts, outs = refs[0], refs[1 : total + 1], refs[total + 1 :]
    at = 0
    used = 0
    lasts = []
    for pieces, sections in jobs:
        low = 0
        for rows, terms in pieces:
            for bit in (0, 1):
                both = sum(ref[bit].astype(F32) for ref in parts[at : at + terms])
                if sections is None:
                    outs[used + bit][:, low : low + rows, :] = both.astype(BF16)
                elif bit == 0:
                    stay = both[0]
                else:
                    lasts += [(stay[a : a + n], both[0, a : a + n], split) for a, n, split in sections]
            low += rows
            at += terms
        used += 2 * (sections is None)
    if lasts:
        keep, to_core, to_chip, to_both = outs[used:]
        first = meta[HALF] == 0
        place = 0
        for stay, leave, split in sorted(lasts, key=lambda entry: not entry[2]):
            rows = stay.shape[0]
            if split:
                rows //= 2
                for value, own, far in ((stay, keep, to_core), (leave, to_chip, to_both)):
                    low, high = value[:rows], value[rows:]
                    own[place : place + rows, :] = jnp.where(first, low, high).astype(own.dtype)
                    far[place : place + rows, :] = jnp.where(first, high, low).astype(BF16)
            else:
                keep[place : place + rows, :] = stay
                to_chip[place : place + rows, :] = leave.astype(BF16)
            place += rows


def fold_call(meta, jobs, after=()):
    parts = [a for pieces, _ in jobs for piece in pieces for a in piece]
    steps = min(a.shape[0] // 2 for a in parts)
    view = lambda a: a.reshape(2, a.shape[0] // 2, *a.shape[1:])
    spec = lambda a: pl.BlockSpec((2, a.shape[0] // 2 // steps, *a.shape[1:]), lambda i, m: (0, i, 0, 0))
    sizes = [([(piece[0].shape[1], len(piece)) for piece in pieces], sections) for pieces, sections in jobs]
    out_shape, out_specs, ends = [], [], []
    for pieces, sections in jobs:
        if sections is None:
            count = pieces[0][0].shape[0] // 2
            rows = sum(piece[0].shape[1] for piece in pieces)
            out_shape += [jax.ShapeDtypeStruct((count, rows, LANES), BF16)] * 2
            out_specs += [pl.BlockSpec((count // steps, rows, LANES), lambda i, m: (i, 0, 0))] * 2
        else:
            ends += sections
    if ends:
        split = sum(n // 2 for _, n, s in ends if s)
        plain = split + sum(n for _, n, s in ends if not s)
        for rows, kind in ((plain, F32), (split, BF16), (plain, BF16), (split, BF16)):
            out_shape.append(jax.ShapeDtypeStruct((rows, LANES), kind))
            out_specs.append(pl.BlockSpec((rows, LANES), lambda i, m: (0, 0)))
    out = pl.pallas_call(
        without(partial(fold_kernel, jobs=sizes), 1 + len(parts), len(after)),
        grid_spec=pltpu.PrefetchScalarGridSpec(
            num_scalar_prefetch=1,
            grid=(steps,),
            in_specs=[spec(a) for a in parts] + unread(len(after)),
            out_specs=out_specs,
        ),
        out_shape=out_shape,
        compiler_params=params(),
        name="fold",
    )(meta, *[view(a) for a in parts], *after)
    moving = sum(sections is None for _, sections in jobs)
    result = [(out[2 * i], out[2 * i + 1]) for i in range(moving)]
    return result + ([tuple(out[2 * moving :])] if ends else [])


def hops(step, sends):
    return [hop(send, masks[step]) for send, masks in zip(sends, ORDERS)]


def last_hop(ends):
    keep, to_core, to_chip, to_both = ends
    return keep, hop(to_core, CORE), hop(to_chip, Z_FAR), hop(to_both, Z_FAR ^ CORE)


def put_rows(source, me, masks, keep, send, low, col=0, at=None):
    put_parts(source, me, masks[1:], (0, masks[0]), (keep, send), low, col, at)


def put_parts(source, me, masks, offsets, refs, low, col=0, at=None):
    cols = pl.ds(col, LANES)
    for offset, ref in zip(offsets, refs):
        for place, value in enumerate(places(masks)):
            chip = (me & ~CORE) ^ (value ^ offset)
            first = pl.multiple_of(chip * PART, 8)
            second = pl.multiple_of((chip + CORE) * PART, 8)
            where = (lambda r: source[pl.ds(r, PART), cols]) if at is None else (lambda r: source[at, pl.ds(r, PART), cols])
            both = jnp.concatenate([where(first), where(second)], axis=0)
            ref[place, low : low + 2 * PART, :] = both.astype(BF16)


def qkv_kernel(meta, mine, other, wq, wk, wv, gains, biases, unit_ref, q_ref, k_ref, v_ref, side_ref, here):
    step = pl.program_id(0)
    rows = side_ref.shape[1]
    key_lanes, query_lanes = mask_lanes((step ^ meta[HALF]) * rows, rows, meta)
    side_ref[0] = key_lanes
    side_ref[1] = query_lanes

    @pl.when(step == 0)
    def _():
        here[...] = mine[...]

    @pl.when(step == 1)
    def _():
        here[...] = other[...]

    unit, _ = norm_parts(here[...].astype(F32))
    normed = (unit * gains[0:1, :] + biases[0:1, :]).astype(BF16)
    unit_ref[...] = unit.astype(BF16).T
    half = q_ref.shape[1]
    first = pl.multiple_of(meta[HALF] * half, half)
    q_ref[...] = (mm(normed, wq[...]) + biases_at(biases, 2, first, half)).astype(BF16)
    k_ref[...] = mm(normed, wk[...]).astype(BF16)
    v_ref[...] = (mm(normed, wv[...]) + biases_at(biases, 3, first, half)).astype(BF16)


def biases_at(biases, row, first, size):
    return biases[row : row + 1, pl.ds(first, size)]


def qkv_call(meta, mine, other, w_qkv, gains, biases):
    rows, width = mine.shape
    half = width // 2
    full = lambda shape: pl.BlockSpec(shape, lambda i, m: (0, 0))
    weight = lambda part: pl.BlockSpec((width, half), lambda i, m: (0, 2 * part + m[HALF]))
    out = lambda cols: pl.BlockSpec((rows, cols), lambda i, m: (i ^ m[HALF], 0))
    shape = lambda cols: jax.ShapeDtypeStruct((2 * rows, cols), BF16)
    return pl.pallas_call(
        qkv_kernel,
        grid_spec=pltpu.PrefetchScalarGridSpec(
            num_scalar_prefetch=1,
            grid=(2,),
            in_specs=[
                full((rows, width)), full((rows, width)), weight(0), weight(1), weight(2),
                full(gains.shape), full(biases.shape),
            ],
            out_specs=[
                pl.BlockSpec((width, rows), lambda i, m: (0, i ^ m[HALF])), out(half), out(half), out(half),
                pl.BlockSpec((2, rows, PAIR), lambda i, m: (0, i ^ m[HALF], 0)),
            ],
            scratch_shapes=[pltpu.VMEM((rows, width), BF16)],
        ),
        out_shape=[
            jax.ShapeDtypeStruct((width, 2 * rows), BF16), shape(half), shape(half), shape(half),
            jax.ShapeDtypeStruct((2, 2 * rows, PAIR), BF16),
        ],
        compiler_params=params(),
        name="qkv",
    )(meta, mine, other, w_qkv, w_qkv, w_qkv, gains, biases)


TILE = 256
FORWARD_UNIT = 512
BACK_UNIT = 512


def mask_lanes(first_row, rows, meta):
    at = lax.broadcasted_iota(jnp.int32, (rows, PAIR), 1) % HEAD_DIM
    pos = first_row + lax.broadcasted_iota(jnp.int32, (rows, PAIR), 0)
    alive = pos < meta[LIVE]
    second = pos >= meta[CUT]
    first = jnp.logical_not(second)
    hidden = ((at == 0) & jnp.logical_not(alive & first)) | ((at == 1) & jnp.logical_not(alive & second))
    named = ((at == 0) & first) | ((at == 1) & second)
    keys = jnp.where(hidden, FAR, 0.0)
    queries = jnp.where(named, 1.0, 0.0)
    return keys.astype(BF16), queries.astype(BF16)


def head_lanes(head, value=1.0):
    lane = lax.broadcasted_iota(jnp.int32, (1, PAIR), 1)
    return jnp.where((lane // HEAD_DIM) == head, value, 0.0).astype(BF16)


def one_head(pair, side, head, scale=1.0):
    return pair * head_lanes(head, scale) + side * head_lanes(1 - head)


def key_range(first_row, group, meta, unit):
    cut = meta[CUT]
    low = jnp.where(first_row >= cut, cut, 0)
    high = jnp.where(first_row + TILE <= cut, cut, meta[LIVE])
    low = (low // 128) * 128
    steps = (high - low + (unit - 1)) // unit
    return pl.multiple_of(jnp.minimum(low, group - steps * unit), 128), steps


def by_width(steps, group, unit, body):
    for count in range(1, group // unit + 1):

        @pl.when(steps == count)
        def _(count=count):
            body(count * unit)


def attend_kernel(meta, q_ref, k_ref, v_ref, side_ref, o_ref, lse_ref, kx_ref, vt_ref):
    group = k_ref.shape[0]
    for head in (0, 1):
        kx_ref[head] = one_head(k_ref[...], side_ref[0], head)
    vt_ref[...] = v_ref[...].T

    def tile(index, carry):
        at = pl.multiple_of(index * TILE, TILE)
        start, steps = key_range(at, group, meta, FORWARD_UNIT)

        def body(width):
            query, side = q_ref[pl.ds(at, TILE), :], side_ref[1, pl.ds(at, TILE), :]
            parts = []
            for head in (0, 1):
                qx = one_head(query, side, head, 0.125)
                scores = mm(kx_ref[head, pl.ds(start, width), :], qx, NT)
                top = jnp.max(scores, axis=0, keepdims=True)
                weight = jnp.exp(scores - top).astype(BF16)
                value = vt_ref[head * HEAD_DIM : (head + 1) * HEAD_DIM, pl.ds(start, width)]
                left = jnp.concatenate([value, jnp.ones((16, width), BF16)], axis=0)
                both = mm(left, weight)
                total = both[HEAD_DIM : HEAD_DIM + 1, :]
                parts.append(both[:HEAD_DIM, :] / total)
                lse_ref[0, head : head + 1, pl.ds(at, TILE)] = top + jnp.log(total)
            o_ref[pl.ds(at, TILE), :] = jnp.concatenate(parts, axis=0).T.astype(BF16)

        by_width(steps, group, FORWARD_UNIT, body)
        return carry

    lax.fori_loop(0, group // TILE, tile, 0)


def attend_call(meta, q, k, v, side):
    group, half = q.shape
    pairs = half // PAIR
    whole = pl.BlockSpec((group, PAIR), lambda p, m: (0, p))
    return pl.pallas_call(
        attend_kernel,
        grid_spec=pltpu.PrefetchScalarGridSpec(
            num_scalar_prefetch=1,
            grid=(pairs,),
            in_specs=[whole, whole, whole, full(side.shape)],
            out_specs=[whole, pl.BlockSpec((1, 2, group), lambda p, m: (p, 0, 0))],
            scratch_shapes=[pltpu.VMEM((2, group, PAIR), BF16), pltpu.VMEM((PAIR, group), BF16)],
        ),
        out_shape=[
            jax.ShapeDtypeStruct((group, half), BF16),
            jax.ShapeDtypeStruct((pairs, 2, group), F32),
        ],
        compiler_params=params(),
        name="attend",
    )(meta, q, k, v, side)


def attend_back_kernel(
    meta, q_ref, k_ref, v_ref, do_ref, o_ref, lse_ref, side_ref, unit, wq, wk, wv, gains, biases, *refs, pair,
):
    masks, offsets = pair_parts(pair)
    *refs, kx_ref, kt_ref, dk_acc, dv_acc, block = refs
    ends = len(refs) - 4 - len(offsets)
    sums, (dq_ref, dk_ref, dv_ref, sum_ref, *targets) = refs[:ends], refs[ends:]
    group = k_ref.shape[0]
    for head in (0, 1):
        kx_ref[head] = one_head(k_ref[...], side_ref[0], head)
    kt_ref[...] = k_ref[...].T
    dk_acc[...] = jnp.zeros_like(dk_acc)
    dv_acc[...] = jnp.zeros_like(dv_acc)

    def tile(index, carry):
        at = pl.multiple_of(index * TILE, TILE)
        start, steps = key_range(at, group, meta, BACK_UNIT)

        def body(width):
            query, side = q_ref[pl.ds(at, TILE), :], side_ref[1, pl.ds(at, TILE), :]
            grad = do_ref[pl.ds(at, TILE), :]
            dots = (grad.astype(F32) * o_ref[pl.ds(at, TILE), :].astype(F32)).T
            probs, raws, masked_grads, masked_queries, dqs = [], [], [], [], []
            for head in (0, 1):
                qx = one_head(query, side, head, 0.125)
                dox = grad * head_lanes(head)
                scores = mm(kx_ref[head, pl.ds(start, width), :], qx, NT)
                prob = jnp.exp(scores - lse_ref[0, head : head + 1, pl.ds(at, TILE)])
                gprob = mm(v_ref[pl.ds(start, width), :], dox, NT)
                delta = jnp.sum(dots[head * HEAD_DIM : (head + 1) * HEAD_DIM, :], axis=0, keepdims=True)
                raw = (prob * (gprob - delta)).astype(BF16)
                keys_t = kt_ref[head * HEAD_DIM : (head + 1) * HEAD_DIM, pl.ds(start, width)]
                dqs.append(mm(keys_t, raw))
                probs.append(prob.astype(BF16))
                raws.append(raw)
                masked_grads.append(dox)
                masked_queries.append(query * head_lanes(head, 0.125))
            dv_acc[pl.ds(start, width), :] += mm(
                jnp.concatenate(probs, axis=1), jnp.concatenate(masked_grads, axis=0)
            )
            dk_acc[pl.ds(start, width), :] += mm(
                jnp.concatenate(raws, axis=1), jnp.concatenate(masked_queries, axis=0)
            )
            dq_ref[pl.ds(at, TILE), :] = (jnp.concatenate(dqs, axis=0).T * 0.125).astype(BF16)

        by_width(steps, group, BACK_UNIT, body)
        return carry

    lax.fori_loop(0, group // TILE, tile, 0)
    dk_ref[...] = dk_acc[...].astype(BF16)
    dv_ref[...] = dv_acc[...].astype(BF16)
    grads = jnp.concatenate([dq_ref[...], dk_ref[...], dv_ref[...]], axis=1)
    total = jnp.sum(grads.astype(F32), axis=0, keepdims=True)
    product = mm(unit[...], grads)
    column = lambda row: jnp.broadcast_to(row, (PAIR, row.shape[1])).T[:, :1]
    gain, shift = column(gains[0:1, :]), column(biases[0:1, :])
    block[...] = product * gain + total * shift
    weight = jnp.concatenate([wq[...], wk[...], wv[...]], axis=1).astype(F32)
    lane = lax.broadcasted_iota(jnp.int32, sum_ref.shape, 1)
    sum_ref[...] = (
        sum((ref[...] for ref in sums), jnp.zeros(sum_ref.shape, F32))
        + jnp.where(lane == 0, jnp.sum(weight * product, axis=1, keepdims=True), 0.0)
        + jnp.where(lane == 2, jnp.sum(weight * total, axis=1, keepdims=True), 0.0)
    )
    here = pl.ds(pl.multiple_of(meta[HALF] * LANES + pair * PAIR, PAIR), PAIR)
    lane = lax.broadcasted_iota(jnp.int32, (PAIR, PAIR), 1)
    for column, part in ((4, total[:, :PAIR]), (5, total[:, 2 * PAIR :])):
        sum_ref[here, :] += jnp.where(lane == column, jnp.broadcast_to(part, (PAIR, PAIR)).T, 0.0)
    put_parts(block, meta[ME], masks, offsets, targets, 0)
    if pair == 2:
        put_sums(sum_ref, meta[ME], masks, offsets, targets, 2 * PART)


SMALL = 128


def pair_parts(pair):
    masks = PAIR_ORDERS[pair]
    if pair == 2:
        return masks[2:], (0, masks[0], masks[1], masks[0] ^ masks[1])
    return masks[1:], (0, masks[0])


def put_sums(source, me, masks, offsets, refs, low):
    for offset, ref in zip(offsets, refs):
        for place, value in enumerate(places(masks)):
            chip = (me & ~CORE) ^ (value ^ offset)
            both = [
                jnp.concatenate([source[pl.ds(pl.multiple_of((chip + c) * PART + 8 * i, 8), 8), :] for i in range(3)], axis=1)
                for c in (0, CORE)
            ]
            ref[place, low : low + 16, :] = jnp.concatenate(both, axis=0).astype(BF16)


def attend_back_call(meta, q, k, v, grad, o, lse, side, unit, w_qkv, gains, biases, sums, pair, after=()):
    group, half = q.shape
    width = unit.shape[0]
    pairs = half // PAIR
    whole = pl.BlockSpec((group, PAIR), lambda i, m: (0, pair))

    def weight(which):
        return pl.BlockSpec((width, PAIR), lambda i, m: (0, 2 * pairs * which + pairs * m[HALF] + pair))

    rows = 2 * PART + 16 * (pair == 2)
    out_shape = [jax.ShapeDtypeStruct((group, PAIR), BF16)] * 3
    masks, offsets = pair_parts(pair)
    out_shape += [jax.ShapeDtypeStruct((width, SMALL), F32)]
    out_shape += [jax.ShapeDtypeStruct((2 ** len(masks), rows, LANES), BF16)] * len(offsets)
    return pl.pallas_call(
        without(partial(attend_back_kernel, pair=pair), 14 + len(sums), len(after)),
        grid_spec=pltpu.PrefetchScalarGridSpec(
            num_scalar_prefetch=1,
            grid=(1,),
            in_specs=[whole] * 5
            + [pl.BlockSpec((1, 2, group), lambda i, m: (pair, 0, 0)), full(side.shape), full(unit.shape), weight(0), weight(1), weight(2)]
            + [full(a.shape) for a in (gains, biases, *sums)] + unread(len(after)),
            out_specs=[full(a.shape) for a in out_shape],
            scratch_shapes=[
                pltpu.VMEM((2, group, PAIR), BF16),
                pltpu.VMEM((PAIR, group), BF16),
                pltpu.VMEM((group, PAIR), F32),
                pltpu.VMEM((group, PAIR), F32),
                pltpu.VMEM((width, LANES), F32),
            ],
        ),
        out_shape=out_shape,
        compiler_params=params(),
        name="attend_back",
    )(meta, q, k, v, grad, o, lse, side, unit, w_qkv, w_qkv, w_qkv, gains, biases, *sums, *after)


UNITS = 192
STEPS = 2
ROWS = 256
MLP_ROWS = 512

ERF_TOP = (0.00022905065861350646, 0.0034082910107109506, 0.050955695062380861, 0.18520832239976145, 1.128379143519084)
ERF_LOW = (
    -1.1791602954361697e-7, 0.000023547966471313185, 0.0010179625278914885, 0.014070470171167667,
    0.11098505178285362, 0.49746925110067538, 1.0,
)


def erf(x):
    x = jnp.clip(x, -3.832506856900711, 3.832506856900711)
    square = x * x
    top = jnp.full_like(x, ERF_TOP[0])
    for c in ERF_TOP[1:]:
        top = top * square + c
    low = jnp.full_like(x, ERF_LOW[0])
    for c in ERF_LOW[1:]:
        low = low * square + c
    return x * top / low


def mid_kernel(
    meta, tok_mine, tok_other, cot_mine, cot_other, a_own, a_got, w_out, w_up, w_down, gains, biases, up_bias,
    res_ref, block_ref, block_send, dn_ref, gub_ref, k0, s0, k1, s1, k2, s2,
    n2, n2t, gl, act, gh, wu, up_acc, down_acc, out_acc, dn_acc,
):
    step = pl.program_id(0)
    rows, width = tok_mine.shape
    half = a_own.shape[1]
    chunk = wu.shape[1]
    me = meta[ME]
    own = pl.multiple_of(meta[HALF] * half, half)
    far = pl.multiple_of((1 - meta[HALF]) * half, half)
    mine = pl.multiple_of(meta[HALF] * rows, rows)
    other = pl.multiple_of((1 - meta[HALF]) * rows, rows)

    @pl.when(step == 0)
    def _():
        for place, tok, cot in ((mine, tok_mine, cot_mine), (other, tok_other, cot_other)):
            def part(index, carry, place=place, tok=tok, cot=cot):
                low = pl.multiple_of(index * ROWS, ROWS)
                at = pl.ds(pl.multiple_of(place + low, ROWS), ROWS)
                residual = (
                    tok[pl.ds(low, ROWS), :].astype(F32)
                    + mm(a_own[at, :], w_out[pl.ds(own, half), :])
                    + mm(a_got[at, :], w_out[pl.ds(far, half), :])
                    + biases[4:5, :]
                )
                res_ref[at, :] = residual
                unit, _ = norm_parts(residual)
                n2[at, :] = (unit * gains[1:2, :] + biases[1:2, :]).astype(BF16)
                live = place + low + lax.broadcasted_iota(jnp.int32, (ROWS, 1), 0) < meta[LIVE]
                cots = cot[pl.ds(low, ROWS), :]
                gl[at, :] = jnp.where(live, cots, jnp.zeros_like(cots))
                return carry

            lax.fori_loop(0, rows // ROWS, part, 0)
        n2t[...] = n2[...].T

    for core in (0, 1):

        @pl.when(meta[HALF] == core)
        def _(core=core):
            for block in range(chunk // UNITS):
                at = (2 * block + core) * UNITS
                wu[:, block * UNITS : (block + 1) * UNITS] = w_up[:, at : at + UNITS]

    wd = w_down[...].reshape(chunk, width)
    gub = jnp.zeros((1, chunk), F32)
    def tile(index, gub):
        at = pl.ds(pl.multiple_of(index * MLP_ROWS, MLP_ROWS), MLP_ROWS)
        hidden = mm(n2[at, :], wu[...]) + up_bias[...]
        gact = mm(gl[at, :], wd, NT)
        cdf = 0.5 * (1.0 + erf(hidden * 0.7071067811865476))
        pdf = jnp.exp(-0.5 * hidden * hidden) * 0.3989422804014327
        active = (hidden * cdf).astype(BF16)
        grad_hidden = gact * (cdf + hidden * pdf)
        gub = gub + jnp.sum(grad_hidden, axis=0, keepdims=True)
        grad_hidden = grad_hidden.astype(BF16)
        act[at, :] = active
        gh[at, :] = grad_hidden
        out_acc[at, :] = jnp.where(step == 0, 0.0, out_acc[at, :]) + mm(active, wd)
        dn_acc[at, :] = jnp.where(step == 0, 0.0, dn_acc[at, :]) + mm(grad_hidden, wu[...], NT)
        return gub

    gub = lax.fori_loop(0, 2 * rows // MLP_ROWS, tile, gub)
    gub_ref[...] = gub
    down_acc[pl.ds(pl.multiple_of(step * chunk, chunk), chunk), :] = mm(act[...], gl[...], TN).astype(BF16)
    up_acc[step] = mm(n2t[...], gh[...])

    @pl.when(step == STEPS - 1)
    def _():
        pos = lax.broadcasted_iota(jnp.int32, (rows, 1), 0)
        at = pl.ds(mine, rows)
        block_ref[...] = jnp.where(
            mine + pos < meta[LIVE], res_ref[at, :] + out_acc[at, :] + biases[5:6, :], 0.0
        ).astype(BF16)
        block_send[...] = jnp.where(other + pos < meta[LIVE], out_acc[pl.ds(other, rows), :], 0.0).astype(BF16)
        dn_ref[...] = dn_acc[...].astype(BF16)
        for block, (keep, send, masks, low) in enumerate(
            ((k0, s0, ORDERS[0], 0), (k0, s0, ORDERS[0], 48), (k0, s0, ORDERS[0], 96), (k1, s1, ORDERS[1], 0))
        ):
            put_rows(up_acc, me, masks, keep, send, low, (block % 2) * LANES, block // 2)
        for col, (keep, send, masks, low) in enumerate(((k1, s1, ORDERS[1], 48), (k2, s2, ORDERS[2], 0))):
            for bit, ref in ((0, keep), (1, send)):
                for place, value in enumerate(places(masks[1:])):
                    chip = me ^ (value ^ (masks[0] * bit))
                    first = pl.multiple_of((chip // 4) * UNITS + (chip & 1) * (UNITS // 2), UNITS // 2)
                    ref[place, low : low + UNITS // 2, :] = down_acc[
                        pl.ds(first, UNITS // 2), col * LANES : (col + 1) * LANES
                    ]


def full(shape):
    return pl.BlockSpec(shape, lambda *a: (0,) * len(shape))


def once(shape):
    return pl.BlockSpec(shape, lambda *a: (0,) * len(shape), pipeline_mode=pl.Buffered(1))


def mid_call(meta, tok_mine, tok_other, cot_mine, cot_other, a_own, a_got, w_out, w_up, w_down, gains, biases, up_bias):
    rows, width = tok_mine.shape
    ff = w_up.shape[1]
    chunk = ff // 2 // STEPS
    blocks = chunk // UNITS
    group = 2 * rows
    stream = [144, 144, 144, 144, 96, 96]
    out_shape = [
        jax.ShapeDtypeStruct((group, width), F32), jax.ShapeDtypeStruct((rows, width), BF16),
        jax.ShapeDtypeStruct((rows, width), BF16), jax.ShapeDtypeStruct((group, width), BF16),
        jax.ShapeDtypeStruct((1, ff // 2), F32),
    ] + [jax.ShapeDtypeStruct((8, n, LANES), BF16) for n in stream]
    out_specs = [once(s.shape) for s in out_shape]
    out_specs[4] = pl.BlockSpec((1, chunk), lambda i, m: (0, i))
    out = pl.pallas_call(
        mid_kernel,
        grid_spec=pltpu.PrefetchScalarGridSpec(
            num_scalar_prefetch=1,
            grid=(STEPS,),
            in_specs=[
                once((rows, width)), once((rows, width)), once((rows, width)), once((rows, width)),
                once(a_own.shape), once(a_got.shape), once(w_out.shape),
                pl.BlockSpec((width, 2 * chunk), lambda i, m: (0, i)),
                pl.BlockSpec((blocks, 1, UNITS, width), lambda i, m: (i, m[HALF], 0, 0)),
                full(gains.shape), full(biases.shape),
                pl.BlockSpec((1, chunk), lambda i, m: (0, i)),
            ],
            out_specs=out_specs,
            scratch_shapes=[
                pltpu.VMEM((group, width), BF16), pltpu.VMEM((width, group), BF16), pltpu.VMEM((group, width), BF16),
                pltpu.VMEM((group, chunk), BF16), pltpu.VMEM((group, chunk), BF16), pltpu.VMEM((width, chunk), BF16),
                pltpu.VMEM((STEPS, width, chunk), F32), pltpu.VMEM((ff // 2, width), BF16),
                pltpu.VMEM((group, width), F32), pltpu.VMEM((group, width), F32),
            ],
        ),
        out_shape=out_shape,
        compiler_params=params(),
        name="mid",
    )(
        meta, tok_mine, tok_other, cot_mine, cot_other, a_own, a_got, w_out, w_up,
        w_down.reshape(ff // UNITS // 2, 2, UNITS, width), gains, biases, up_bias,
    )
    return out[:5], out[5::2], out[6::2]


def branch_kernel(
    meta, res, cot_mine, cot_other, dn_own, dn_got, a_own, a_got, w_out, gains,
    gres_ref, ga_ref, small_ref, keep, send, gb, whole,
):
    rows, width = cot_mine.shape
    half = a_own.shape[1]
    own = pl.multiple_of(meta[HALF] * half, half)
    far = pl.multiple_of((1 - meta[HALF]) * half, half)
    mine = pl.multiple_of(meta[HALF] * rows, rows)
    other = pl.multiple_of((1 - meta[HALF]) * rows, rows)
    for place, cot in ((other, cot_other), (mine, cot_mine)):

        def tile(index, small, place=place, cot=cot):
            low = pl.multiple_of(index * ROWS, ROWS)
            at = pl.ds(pl.multiple_of(place + low, ROWS), ROWS)
            unit, rstd = norm_parts(res[at, :])
            grad = dn_own[at, :].astype(F32) + dn_got[at, :].astype(F32)
            live = place + low + lax.broadcasted_iota(jnp.int32, (ROWS, 1), 0) < meta[LIVE]
            gl = jnp.where(live, cot[pl.ds(low, ROWS), :].astype(F32), 0.0)
            gres = gl + norm_back(grad, unit, rstd, gains[1:2, :])
            branch = gres.astype(BF16)
            gb[at, :] = branch
            if cot is cot_mine:
                gres_ref[pl.ds(low, ROWS), :] = branch
                small += jnp.concatenate(
                    [jnp.sum(a, axis=0, keepdims=True) for a in (grad * unit, grad, branch.astype(F32), gl)], axis=0
                )
            return small

        small = lax.fori_loop(0, rows // ROWS, tile, jnp.zeros((4, width), F32))
    small_ref[0:4, :] = small
    small_ref[4:8, :] = jnp.zeros((4, width), F32)
    ga_ref[...] = mm(gb[...], w_out[pl.ds(own, half), :], NT).astype(BF16)
    part = gb[:, pl.ds(own, half)]
    whole[pl.ds(own, half), :] = mm(a_own[...], part, TN)
    whole[pl.ds(far, half), :] = mm(a_got[...], part, TN)
    put_rows(whole, meta[ME], ORDERS[2], keep, send, 0)


def branch_call(meta, res, cot_mine, cot_other, dn_own, dn_got, a_own, a_got, w_out, gains):
    rows, width = cot_mine.shape
    group, half = a_own.shape
    args = (res, cot_mine, cot_other, dn_own, dn_got, a_own, a_got, w_out, gains)
    out_shape = [
        jax.ShapeDtypeStruct((rows, width), BF16), jax.ShapeDtypeStruct((group, half), BF16),
        jax.ShapeDtypeStruct((8, width), F32),
    ] + [jax.ShapeDtypeStruct((8, 2 * PART, LANES), BF16)] * 2
    return pl.pallas_call(
        branch_kernel,
        grid_spec=pltpu.PrefetchScalarGridSpec(
            num_scalar_prefetch=1,
            grid=(1,),
            in_specs=[full(a.shape) for a in args],
            out_specs=[full(a.shape) for a in out_shape],
            scratch_shapes=[pltpu.VMEM((group, width), BF16), pltpu.VMEM((width, half), F32)],
        ),
        out_shape=out_shape,
        compiler_params=params(),
        name="branch",
    )(meta, *args)


def qkv_back_kernel(meta, d0, d1, d2, d3, d4, d5, d6, d7, d8, wq, wk, wv, dn_own, dn_send):
    rows = dn_own.shape[0]

    def part(place, carry):
        at = pl.ds(pl.multiple_of(place * rows, rows), rows)
        total = 0.0
        for parts, weight in (((d0, d3, d6), wq), ((d1, d4, d7), wk), ((d2, d5, d8), wv)):
            total += mm(jnp.concatenate([a[at, :] for a in parts], axis=1), weight[...], NT)
        total = total.astype(BF16)

        @pl.when(place == meta[HALF])
        def _():
            dn_own[...] = total

        @pl.when(place != meta[HALF])
        def _():
            dn_send[...] = total

        return carry

    lax.fori_loop(0, 2, part, 0)


def qkv_back_call(meta, grads, w_qkv, after=()):
    group = grads[0].shape[0]
    width = w_qkv.shape[0]
    half = width // 2

    def weight(which):
        return pl.BlockSpec((width, half), lambda i, m: (0, 2 * which + m[HALF]))

    out_shape = [jax.ShapeDtypeStruct((group // 2, width), BF16)] * 2
    return pl.pallas_call(
        without(qkv_back_kernel, 13, len(after)),
        grid_spec=pltpu.PrefetchScalarGridSpec(
            num_scalar_prefetch=1,
            grid=(1,),
            in_specs=[full(a.shape) for a in grads] + [weight(0), weight(1), weight(2)] + unread(len(after)),
            out_specs=[full(a.shape) for a in out_shape],
        ),
        out_shape=out_shape,
        compiler_params=params(),
        name="qkv_back",
    )(meta, *grads, w_qkv, w_qkv, w_qkv, *after)


def tail_kernel(tok, gres, dn_own, dn_got, gains, out):
    unit, rstd = norm_parts(tok[...].astype(F32))
    grad = dn_own[...].astype(F32) + dn_got[...].astype(F32)
    out[...] = (gres[...].astype(F32) + norm_back(grad, unit, rstd, gains[0:1, :])).astype(BF16)


def tail_call(tok, gres, dn_own, dn_got, gains, after=()):
    rows, width = tok.shape
    block = pl.BlockSpec((rows // 2, width), lambda i: (i, 0))
    return pl.pallas_call(
        without(tail_kernel, 5, len(after)),
        grid=(2,),
        in_specs=[block, block, block, block, pl.BlockSpec(gains.shape, lambda i: (0, 0))] + unread(len(after)),
        out_specs=block,
        out_shape=jax.ShapeDtypeStruct((rows, width), BF16),
        compiler_params=params(),
        name="tail",
    )(tok, gres, dn_own, dn_got, gains, *after)


A_SECTIONS = (
    [(0, 48, True), (48, 48, True), (96, 48, True)], [(0, 48, True), (48, 96, False)], [(0, 96, False), (96, 48, True)],
)


def join_a_kernel(meta, keep, from_core, from_chip, from_both, block, up, out, down, block_out, own, far):
    block_out[...] = block[...]
    split = from_core.shape[0]
    own[...] = keep[...] + from_chip[...].astype(F32)
    far[...] = from_core[...].astype(F32) + from_both[...].astype(F32)
    down[:, :LANES] = own[split : split + 4 * PART, :]
    down[:, LANES:] = own[split + 4 * PART :, :]
    for core in (0, 1):

        @pl.when(meta[HALF] == core)
        def _(core=core):
            for side, ref in ((core, own), (1 - core, far)):
                for block in range(8):
                    at = (2 * block + side) * UNITS
                    low = (block % 2) * UNITS
                    row = (block // 2) * PART
                    up[:, at : at + UNITS] = ref[row : row + PART, low : low + UNITS]
                out[:, side * LANES : (side + 1) * LANES] = ref[4 * PART : 5 * PART, :]


def join_b_kernel(meta, keep, from_core, from_chip, from_both, qkv, gain, bias, up_bias):
    own = keep[...] + from_chip[...].astype(F32)
    far = from_core[...].astype(F32) + from_both[...].astype(F32)
    for core in (0, 1):

        @pl.when(meta[HALF] == core)
        def _(core=core):
            for side, value in ((core, own), (1 - core, far)):
                for pair in range(3):
                    part = value[pair * PART : (pair + 1) * PART]
                    for i in range(3):
                        at = (2 * i + side) * LANES + pair * PAIR
                        qkv[:, at : at + PAIR] = part[:, i * PAIR : (i + 1) * PAIR]

    small = own[3 * PART :] + far[3 * PART :]
    turned = jnp.concatenate([small[:, i * SMALL : (i + 1) * SMALL] for i in range(3)], axis=0).T
    gain[...] = turned[0:2]
    bias[...] = turned[2:8]
    up_bias[...] = jnp.concatenate([turned[8 + i : 9 + i] for i in range(4)], axis=1)


def whole_call(kernel, name, meta, args, shapes, scratch=(), after=()):
    shapes = [jax.ShapeDtypeStruct(s, F32) if isinstance(s, tuple) else jax.ShapeDtypeStruct(s.shape, s.dtype) for s in shapes]
    return pl.pallas_call(
        without(kernel, 1 + len(args), len(after)),
        grid_spec=pltpu.PrefetchScalarGridSpec(
            num_scalar_prefetch=1,
            grid=(1,),
            in_specs=[full(a.shape) for a in args] + unread(len(after)),
            out_specs=[full(s.shape) for s in shapes],
            scratch_shapes=[pltpu.VMEM(s, F32) for s in scratch],
        ),
        out_shape=shapes,
        compiler_params=params(),
        name=name,
    )(meta, *args, *after)


def paired(
    tokens, w_qkv, w_out, w_up, w_down, gains, biases, up_bias, image_cut, group_live, cotangent
):
    width = tokens.shape[1]
    half = width // 2
    width_ff = w_up.shape[1]
    core = lax.axis_index("dp") % 2
    me = (lax.axis_index("dp") * 2 + lax.axis_index("seq")).astype(jnp.int32)
    swap = [(i, (i & ~3) | ((i & 1) << 1) | ((i >> 1) & 1)) for i in range(COUNT)]

    def trade(value):
        return lax.ppermute(value, BOTH, swap)

    def across(value):
        return hop(value, CORE)

    tok = trade(tokens)
    own_bounds = jnp.concatenate([image_cut, group_live])
    bounds = jnp.where(core == lax.axis_index("seq"), own_bounds, across(own_bounds))
    tok_far = across(tok)
    meta = jnp.concatenate([jnp.stack([me, core.astype(jnp.int32)]), bounds])
    cot_here, tok_far, meta = lax.optimization_barrier((cotangent, tok_far, meta))
    cot = trade(cot_here)
    blocks = up_bias.reshape(-1, 2, UNITS)
    own_bias = jnp.where(core == 0, blocks[:, 0], blocks[:, 1]).reshape(1, -1)

    unit, q, k, v, side = qkv_call(meta, tok, tok_far, w_qkv, gains, biases)
    o, lse = attend_call(meta, q, k, v, side)
    o_got = across(o)
    cot_far = across(lax.optimization_barrier((cot, o))[0])
    (res, block, block_send, dn, gub), keeps, sends = mid_call(
        meta, tok, tok_far, cot, cot_far, o, o_got, w_out, w_up, w_down, gains, biases, own_bias
    )
    dn_got = across(dn)
    a_got = hops(0, sends)
    block_got = across(block_send)
    block_out = trade((block.astype(F32) + block_got.astype(F32)).astype(BF16))
    gres, ga, small, out_keep, out_send = branch_call(meta, res, cot, cot_far, dn, dn_got, o, o_got, w_out, gains)
    out_got = hop(out_send, ORDERS[2][0])

    zero = jnp.zeros((width,), F32)
    rows = jnp.stack([zero, small[0], zero, small[1], zero, zero, small[2], small[3]])
    units = gub.reshape(-1, 1, UNITS)
    units = jnp.where(jnp.arange(2)[None, :, None] == core, units, 0.0)
    units = units.reshape(COUNT, 4, PART).transpose(0, 2, 1).reshape(width, 4)
    early = jnp.concatenate([rows.T, units, jnp.zeros((width, SMALL - 12), F32)], axis=1)

    def pair_hop(pair, step, send):
        return hop(send, PAIR_ORDERS[pair][step])

    def tied(value, to):
        return lax.optimization_barrier((value, to))[0]

    *grads, sums, b0, b0_send = attend_back_call(meta, q, k, v, ga, o, lse, side, unit, w_qkv, gains, biases, [], 0)
    a0, a1, a2 = fold_call(
        meta,
        [
            ([(keeps[0], a_got[0])], None), ([(keeps[1], a_got[1])], None),
            ([(keeps[2], a_got[2]), (out_keep, out_got)], None),
        ],
        [b0_send],
    )
    a_got = hops(1, [a0[1], a1[1], a2[1]])
    b0_got = pair_hop(0, 0, tied(b0_send, a0[1]))
    *more, sums, b1, b1_send = attend_back_call(meta, q, k, v, ga, o, lse, side, unit, w_qkv, gains, biases, [sums], 1, [a0[1]])
    grads = grads + more
    a0, a1, a2, p0 = fold_call(
        meta,
        [([(a[0], g)], None) for a, g in zip((a0, a1, a2), a_got)] + [([(b0, b0_got)], None)],
        [b1_send],
    )
    a_got = hops(2, [a0[1], a1[1], a2[1]])
    p0_got = pair_hop(0, 1, p0[1])
    b1_got = pair_hop(1, 0, tied(b1_send, p0[1]))
    more = attend_back_call(meta, q, k, v, ga, o, lse, side, unit, w_qkv, gains, biases, [sums, early], 2, [a0[1]])
    grads, b2, b2_sends = grads + list(more[:3]), more[4], more[5:]
    p0, p1, a_end = fold_call(
        meta,
        [([(p0[0], p0_got)], None), ([(b1, b1_got)], None)]
        + [([(a[0], g)], sections) for a, g, sections in zip((a0, a1, a2), a_got, A_SECTIONS)],
        [b2_sends[0], block_out],
    )
    p0_got, p1_got = pair_hop(0, 2, p0[1]), pair_hop(1, 1, p1[1])
    b2_sends = lax.optimization_barrier((*b2_sends, p1[1]))[:-1]
    b2_got = [hop(send, mask) for send, mask in zip(b2_sends, pair_parts(2)[1][1:])]
    a_end = last_hop(a_end)
    dn_own, dn_send = qkv_back_call(meta, grads, w_qkv, [p1[1]])
    p1, p2 = fold_call(meta, [([(p1[0], p1_got)], None), ([(b2, *b2_got)], None)], [dn_own, *a_end[1:]])
    p1_got, p2_got = pair_hop(1, 2, p1[1]), pair_hop(2, 2, p2[1])
    dn_got = across(tied(dn_send, p2[1]))
    mine = tail_call(tok, gres, dn_own, dn_got, gains, [p2[1]])
    cut = [(0, 48, True)]
    (b_end,) = fold_call(
        meta,
        [([(p0[0], p0_got)], cut), ([(p1[0], p1_got)], cut), ([(p2[0], p2_got)], cut + [(48, 16, True)])],
        [mine],
    )
    grad_tokens = trade(tied(mine, b_end[1]))
    grad_wup, grad_wout, grad_wdown, block_out = whole_call(
        join_a_kernel, "join_a", meta, [*a_end, block_out],
        [(PART, width_ff), (PART, width), (4 * PART, width), block_out],
        [a_end[0].shape, a_end[1].shape], [b_end[1]],
    )
    b_end = last_hop(b_end)
    grad_qkv, grad_gains, grad_biases, grad_upbias = whole_call(
        join_b_kernel, "join_b", meta, b_end, [(PART, 3 * width), (2, PART), (6, PART), (1, 4 * PART)],
        after=[grad_wdown],
    )
    return (
        block_out, grad_tokens, grad_qkv, grad_wout, grad_wup, grad_wdown, grad_gains, grad_biases,
        grad_upbias.reshape(-1),
    )


def norm_rows(values, gain, shift):
    center = values - jnp.mean(values, axis=-1, keepdims=True)
    spread = jnp.mean(center * center, axis=-1, keepdims=True)
    return center * lax.rsqrt(spread + EPSILON) * gain + shift


def split_heads(values):
    return values.reshape(values.shape[0], HEADS, -1).transpose(1, 0, 2)


def join_heads(values):
    return values.transpose(1, 0, 2).reshape(values.shape[1], -1)


def head_probs(query_head, key_head, mask):
    raw = jnp.einsum("qd,kd->qk", query_head, key_head, preferred_element_type=jnp.float32)
    return jax.nn.softmax(raw * 0.125 + mask, axis=-1)


def shards(
    tokens, w_qkv, w_out, w_up, w_down, gains, biases, up_bias, image_cut, group_live, cotangent
):
    rows_here = tokens.shape[0]
    width = tokens.shape[1]
    group = rows_here * lax.axis_size("seq")
    first_row = lax.axis_index("seq") * rows_here
    cut_row = image_cut[0]
    live_rows = group_live[0]
    key_pos = jnp.arange(group, dtype=jnp.int32)
    query_pos = first_row + jnp.arange(rows_here, dtype=jnp.int32)
    query_live = (query_pos < live_rows)[:, None]
    allowed = ((query_pos >= cut_row)[:, None] == (key_pos >= cut_row)[None, :]) & (
        key_pos < live_rows
    )[None, :]
    mask = jnp.where(allowed, 0.0, -1000000000.0).astype(jnp.float32)
    inputs = tokens.astype(jnp.float32)
    normed_one, norm_back_one = jax.vjp(norm_rows, inputs, gains[0], biases[0])
    normed_one = normed_one.astype(jnp.bfloat16)
    projected = jnp.dot(normed_one, w_qkv, preferred_element_type=jnp.float32)
    queries = (projected[:, :width] + biases[2]).astype(jnp.bfloat16)
    key_rows = projected[:, width : 2 * width].astype(jnp.bfloat16)
    value_rows = (projected[:, 2 * width :] + biases[3]).astype(jnp.bfloat16)
    kv_local = jnp.concatenate([key_rows, value_rows], axis=1)
    kv_whole = lax.all_gather(kv_local, "seq", axis=0, tiled=True)
    query_heads = split_heads(queries)

    def attend(operands):
        query_head, key_head, value_head = operands
        probs = head_probs(query_head, key_head, mask)
        return jnp.dot(probs.astype(jnp.bfloat16), value_head, preferred_element_type=jnp.float32)

    heads_out = lax.map(
        attend, (query_heads, split_heads(kv_whole[:, :width]), split_heads(kv_whole[:, width:]))
    )
    attended = join_heads(heads_out).astype(jnp.bfloat16)
    residual = inputs + jnp.dot(attended, w_out, preferred_element_type=jnp.float32) + biases[4]
    normed_two, norm_back_two = jax.vjp(norm_rows, residual, gains[1], biases[1])
    normed_two = normed_two.astype(jnp.bfloat16)
    hidden_pre = jnp.dot(normed_two, w_up, preferred_element_type=jnp.float32) + up_bias
    activated, gelu_back = jax.vjp(partial(jax.nn.gelu, approximate=False), hidden_pre)
    activated = activated.astype(jnp.bfloat16)
    mlp_out = jnp.dot(activated, w_down, preferred_element_type=jnp.float32) + biases[5]
    block_out = jnp.where(query_live, residual + mlp_out, 0.0).astype(jnp.bfloat16)
    grad_live = jnp.where(query_live, cotangent, jnp.zeros_like(cotangent))
    grad_wdown = jnp.einsum("rf,rd->fd", activated, grad_live, preferred_element_type=jnp.float32)
    grad_activated = jnp.einsum("rd,fd->rf", grad_live, w_down, preferred_element_type=jnp.float32)
    grad_hidden = gelu_back(grad_activated)[0].astype(jnp.bfloat16)
    grad_wup = jnp.einsum("rd,rf->df", normed_two, grad_hidden, preferred_element_type=jnp.float32)
    grad_normed_two = jnp.einsum("rf,df->rd", grad_hidden, w_up, preferred_element_type=jnp.float32)
    grad_res_norm, gain_two, shift_two = norm_back_two(grad_normed_two)
    grad_residual = grad_live.astype(jnp.float32) + grad_res_norm
    grad_branch = grad_residual.astype(jnp.bfloat16)
    grad_wout = jnp.einsum("rd,re->de", attended, grad_branch, preferred_element_type=jnp.float32)
    grad_attended = jnp.einsum(
        "re,de->rd", grad_branch, w_out, preferred_element_type=jnp.float32
    ).astype(jnp.bfloat16)

    def attend_back(operands):
        query_head, key_head, value_head, grad_head = operands
        probs = head_probs(query_head, key_head, mask)
        grad_probs = jnp.einsum(
            "qd,kd->qk", grad_head, value_head, preferred_element_type=jnp.float32
        )
        grad_scores = probs * (grad_probs - jnp.sum(probs * grad_probs, axis=-1, keepdims=True))
        grad_raw = (grad_scores * 0.125).astype(jnp.bfloat16)
        grad_query = jnp.dot(grad_raw, key_head, preferred_element_type=jnp.float32)
        grad_key = jnp.einsum("qk,qd->kd", grad_raw, query_head, preferred_element_type=jnp.float32)
        grad_value = jnp.einsum(
            "qk,qd->kd", probs.astype(jnp.bfloat16), grad_head, preferred_element_type=jnp.float32
        )
        return (grad_query, grad_key, grad_value)

    grad_q_heads, grad_k_heads, grad_v_heads = lax.map(
        attend_back,
        (
            query_heads,
            split_heads(kv_whole[:, :width]),
            split_heads(kv_whole[:, width:]),
            split_heads(grad_attended),
        ),
    )
    grad_queries = join_heads(grad_q_heads).astype(jnp.bfloat16)
    grad_kv_terms = jnp.concatenate([join_heads(grad_k_heads), join_heads(grad_v_heads)], axis=1)
    grad_kv = lax.psum_scatter(
        grad_kv_terms.astype(jnp.bfloat16), "seq", scatter_dimension=0, tiled=True
    )
    grad_projected = jnp.concatenate([grad_queries, grad_kv], axis=1)
    grad_wqkv = jnp.einsum(
        "rd,re->de", normed_one, grad_projected, preferred_element_type=jnp.float32
    )
    grad_normed_one = jnp.einsum(
        "re,de->rd", grad_projected, w_qkv, preferred_element_type=jnp.float32
    )
    grad_in_norm, gain_one, shift_one = norm_back_one(grad_normed_one)
    grad_tokens = (grad_residual + grad_in_norm).astype(jnp.bfloat16)
    grad_gains = jnp.stack([gain_one, gain_two])
    grad_biases = jnp.stack(
        [
            shift_one,
            shift_two,
            jnp.sum(grad_queries.astype(jnp.float32), axis=0),
            jnp.sum(grad_kv[:, width:].astype(jnp.float32), axis=0),
            jnp.sum(grad_branch.astype(jnp.float32), axis=0),
            jnp.sum(grad_live.astype(jnp.float32), axis=0),
        ]
    )
    grad_upbias = jnp.sum(grad_hidden.astype(jnp.float32), axis=0)
    summed = (
        lax.psum_scatter(grad_wqkv, ("dp", "seq"), scatter_dimension=0, tiled=True),
        lax.psum_scatter(grad_wout, ("dp", "seq"), scatter_dimension=0, tiled=True),
        lax.psum_scatter(grad_wup, ("dp", "seq"), scatter_dimension=0, tiled=True),
        lax.psum_scatter(grad_wdown, ("dp", "seq"), scatter_dimension=0, tiled=True),
        lax.psum_scatter(grad_gains, ("dp", "seq"), scatter_dimension=1, tiled=True),
        lax.psum_scatter(grad_biases, ("dp", "seq"), scatter_dimension=1, tiled=True),
        lax.psum_scatter(grad_upbias, ("dp", "seq"), scatter_dimension=0, tiled=True),
    )
    return (
        block_out,
        grad_tokens,
        summed[0],
        summed[1],
        summed[2],
        summed[3],
        summed[4],
        summed[5],
        summed[6],
    )


def solution(mesh):
    in_specs = (
        P(("dp", "seq"), None),
        P(),
        P(),
        P(),
        P(),
        P(),
        P(),
        P(),
        P("dp"),
        P("dp"),
        P(("dp", "seq"), None),
    )
    out_specs = (
        P(("dp", "seq"), None),
        P(("dp", "seq"), None),
        P(("dp", "seq"), None),
        P(("dp", "seq"), None),
        P(("dp", "seq"), None),
        P(("dp", "seq"), None),
        P(None, ("dp", "seq")),
        P(None, ("dp", "seq")),
        P(("dp", "seq")),
    )
    fits = mesh.shape["seq"] == 2 and mesh.shape["dp"] * 2 == COUNT
    return jax.shard_map(paired if fits else shards, mesh=mesh, in_specs=in_specs, out_specs=out_specs, check_vma=False)
```
